32 devices in a mesh: dp: 8 (over y, x, core), tensor: 4 (over z).
Axes of the slice: x: 2, y: 2, z: 4, core: 2. Of those that a mesh axis runs over, the one named last changes fastest.
Arguments:
- tokens: bfloat16 [8192, 768], P(('dp', 'tensor')), may hold values from -6 to 6
- cotangent: bfloat16 [8192, 768], P(('dp', 'tensor')), may hold values from -6 to 6
- segments: int32 [8, 1024], P('dp'), may hold values from 0 to 7, never falling along the last dimension, each value on 1 to 256 neighbouring positions
- gates_local: float32 [4, 771], P('tensor'), may hold values from 0.3 to 1
- gates_shared: float32 [770], replicated, may hold values from 0.3 to 1
- gate_logits: float32 [4, 771], P('tensor')
- shared_logits: float32 [770], replicated, may hold values from -6 to 6
- masters: float32 [4, 48, 36864], P('tensor', 'dp')
- moment_one: float32 [4, 48, 36864], P('tensor', 'dp')
- moment_two: float32 [4, 48, 36864], P('tensor', 'dp'), as said below
- block_bases: float32 [4, 48, 2, 36864], P('tensor', 'dp'), as said below
- block_stats: float32 [4, 48, 2, 36864], P('tensor', 'dp'), as said below
- unit_params: float32 [4, 1152], P('tensor', 'dp'), may hold values from -4 to 4
- unit_first: float32 [4, 1152], P('tensor', 'dp'), may hold values from -5 to 5
- unit_second: float32 [4, 1152], P('tensor', 'dp'), may hold values from 68.94387 to 275.77548
- norm_params: float32 [6, 768], replicated
- norm_first: float32 [6, 768], replicated, may hold values from -16 to 16
- norm_second: float32 [6, 768], replicated, may hold values from 155.12372 to 620.4949
- slot_ids: int32 [48], replicated, may hold values from 0 to 47, as said below
- step_count: int32 [1], replicated, may hold values from 2 to 20
Outputs:
- layer_out: bfloat16 [8192, 768], P(('dp', 'tensor'))
- token_grad: float32 [8192, 768], P(('dp', 'tensor'))
- block_grads: float32 [4, 48, 36864], P('tensor', 'dp')
- masters_new: float32 [4, 48, 36864], P('tensor', 'dp')
- moment_one_new: float32 [4, 48, 36864], P('tensor', 'dp')
- moment_two_new: float32 [4, 48, 36864], P('tensor', 'dp')
- bases_new: float32 [4, 48, 2, 36864], P('tensor', 'dp')
- stats_new: float32 [4, 48, 2, 36864], P('tensor', 'dp')
- unit_params_new: float32 [4, 1152], P('tensor', 'dp')
- unit_first_new: float32 [4, 1152], P('tensor', 'dp')
- unit_second_new: float32 [4, 1152], P('tensor', 'dp')
- norm_grads: float32 [6, 768], replicated
- norm_params_new: float32 [6, 768], replicated
- norm_first_new: float32 [6, 768], replicated
- norm_second_new: float32 [6, 768], replicated
- param_count: float32 [1], replicated
The draws below stay inside these ranges and needn't reach their ends.
Inputs may be any that keep to these rules, and one draw needn't show every extreme that they name: `slot_ids`: the 48 entries are different; slot s is kept by index s // 6 of dp. `block_stats`: each block of each pair, read as a 192 x 192 matrix, is symmetric positive definite. `block_bases`: each block of each pair, read as a 192 x 192 matrix, is invertible. `moment_two`: all entries are positive.
All inputs are finite; a program needn't handle non-finite values.
Results may differ from the reference program's by a relative error of at most 0.02.
Values may be sent and summed in bfloat16 or wider, within the bound.
No kernel may reach another device: no remote copies, remote signals or barrier semaphores. Data moves between devices by JAX's collectives and lax.ppermute only.
A program may use at most 192 MiB of HBM per device.

```python
import math
import jax
import jax.numpy as jnp
import numpy as np
from jax import lax

D = 768
FF = 3072
HD = 64
BLK = 192
LEN = 1024
ITEMS = 8
SHARDS = 4
HEADS_T = 3
HEAD_COLS = 192
UNITS_T = 768
GATE_LEN = 771
UNIT_LEN = 1152
SEQS = 8
TOKENS = 8192
ITEM_MAX = 256
QKV_BLOCKS = 12
OUT_BLOCKS = 4
UP_BLOCKS = 16
NBLK = 48
SLOTS = 48


def slot_table(key):
    order = jax.random.permutation(jax.random.fold_in(key, 11), SLOTS).astype(jnp.int32)
    chosen = order[:NBLK]
    chosen = jnp.where(chosen == jnp.min(chosen), 0, chosen)
    chosen = jnp.where(chosen == jnp.max(chosen), SLOTS - 1, chosen)
    return chosen.astype(jnp.int32)


def slot_kinds(key):
    chosen = slot_table(key)
    blocks = jnp.arange(NBLK, dtype=jnp.int32)
    kinds = (blocks >= QKV_BLOCKS).astype(jnp.int32) + (blocks >= QKV_BLOCKS + OUT_BLOCKS).astype(jnp.int32) + (blocks >= QKV_BLOCKS + OUT_BLOCKS + UP_BLOCKS).astype(jnp.int32)
    return jnp.zeros((SLOTS,), jnp.int32).at[chosen].set(kinds)


def grad_sizes(key):
    table = jnp.array([0.5, 0.06, 0.15, 0.25], jnp.float32) * math.sqrt(TOKENS)
    return table[slot_kinds(key)]


def rough_noise(key, shape):
    return jnp.clip(jax.random.normal(key, shape, jnp.float32), -5.0, 5.0)


def draw_slot_ids(key, part):
    return slot_table(key)


def draw_masters(key, part):
    spreads = jnp.array([D ** (-0.5), 8.0 * D ** (-0.5), D ** (-0.5), FF ** (-0.5)], jnp.float32)[slot_kinds(key)]
    drawn = rough_noise(jax.random.fold_in(key, 1), (SHARDS, SLOTS, BLK, BLK)) * spreads[None, :, None, None]
    return drawn.reshape(SHARDS, SLOTS, BLK * BLK)


def draw_moment_one(key, part):
    spreads = 0.0526 * grad_sizes(key)
    drawn = rough_noise(jax.random.fold_in(key, 2), (SHARDS, SLOTS, BLK, BLK)) * spreads[None, :, None, None]
    return drawn.reshape(SHARDS, SLOTS, BLK * BLK)


def draw_moment_two(key, part):
    spreads = 0.0526 * grad_sizes(key) ** 2
    factor = jnp.exp(jax.random.uniform(jax.random.fold_in(key, 3), (SHARDS, SLOTS, BLK, BLK), jnp.float32) * math.log(4.0))
    return (factor * spreads[None, :, None, None]).reshape(SHARDS, SLOTS, BLK * BLK)


def draw_block_bases(key, part):
    identity = jnp.eye(BLK, dtype=jnp.float32)
    drawn = identity + 0.3 * rough_noise(jax.random.fold_in(key, 4), (SHARDS, SLOTS, 2, BLK, BLK)) / math.sqrt(BLK)
    return drawn.reshape(SHARDS, SLOTS, 2, BLK * BLK)


def draw_block_stats(key, part):
    shape = (SHARDS, SLOTS, 2, BLK, BLK)
    random_part = rough_noise(jax.random.fold_in(key, 5), shape)
    symmetric = (random_part + jnp.swapaxes(random_part, -1, -2)) * (0.35 / math.sqrt(2.0 * BLK))
    identity = jnp.eye(BLK, dtype=jnp.float32)
    diagonal = jnp.exp(jax.random.uniform(jax.random.fold_in(key, 6), shape[:-1], jnp.float32) * math.log(2.0))
    magnitude = 0.0526 * BLK * grad_sizes(key) ** 2
    drawn = (identity * diagonal[..., None] + symmetric * (1.0 - identity)) * magnitude[None, :, None, None, None]
    return drawn.reshape(SHARDS, SLOTS, 2, BLK * BLK)


def draw_norm_params(key, part):
    random_part = rough_noise(jax.random.fold_in(key, 7), (6, D))
    row_index = jnp.arange(6)[:, None]
    is_gain = (row_index == 0) | (row_index == 3)
    return jnp.where(is_gain, 1.0 + 0.2 * random_part, 0.3 * random_part)


def draw_gate_logits(key, part):
    position = jnp.arange(SHARDS, dtype=jnp.float32)[:, None] / max(SHARDS - 1, 1)
    offset = -2.9 + 2.4 * position
    return offset + 0.5 * jax.random.normal(jax.random.fold_in(key, 8), (SHARDS, GATE_LEN), jnp.float32)


def shard_levels(own_key, dims, cuts, least, high):
    def one(dim, parts):
        steps = jax.random.uniform(jax.random.fold_in(jax.random.fold_in(own_key, 6), dim), (parts,), jnp.float32, least / len(cuts), high / len(cuts))
        return jnp.repeat(jnp.exp(steps), dims[dim] // parts).reshape((-1,) + (1,) * (len(dims) - dim - 1))

    level = one(*cuts[0])
    for cut in cuts[1:]:
        level = level * one(*cut)
    return level


def split_up(count, total, limit, slope):
    portions = [(1 << 20) // math.isqrt(standing ** slope) + 1 for standing in range(2, count + 1)]
    surplus, given = total - limit - (count - 1), [1] * (count - 1)
    while surplus > 0:
        movable = [i for i in range(count - 1) if given[i] < limit]
        whole, remaining = sum([portions[i] for i in movable]), surplus
        for i in movable:
            more = min(limit - given[i], max(1, remaining * portions[i] // whole), surplus)
            given[i] = given[i] + more
            surplus = surplus - more
    return np.array([limit] + given)


def uneven(own_key, amount, total, reach, skew):
    if amount == 2:
        one = jax.random.randint(own_key, (), max(1, total - reach), min(reach, total - 1) + 1)
        return jnp.stack([one, total - one])
    tallies = jnp.asarray(split_up(amount, total, reach, skew), jnp.int32)
    pairs = (amount - 1) // 2
    source_of, sink = tallies[1:1 + 2 * pairs:2], tallies[2:2 + 2 * pairs:2]
    room = jnp.minimum(source_of - 1, reach - sink)
    moved = jax.random.randint(jax.random.fold_in(own_key, 1), (pairs,), 0, 1 << 20) % (room + 1)
    tallies = tallies.at[1:1 + 2 * pairs:2].set(source_of - moved).at[2:2 + 2 * pairs:2].set(sink + moved)
    return tallies[jax.random.permutation(jax.random.fold_in(own_key, 2), amount)]


def normal_values(stream_key, shape, scale, limit, cuts=(), kind=jnp.bfloat16):
    values = jax.random.normal(stream_key, shape, jnp.float32) * scale
    if len(cuts) > 0:
        values = shard_levels(stream_key, shape, cuts, -0.22, 0.18) * values
    return jnp.clip(values, min=-limit, max=limit).astype(kind)


def setup_inputs(seed: int = 0) -> dict:
    key_list = jax.random.split(jax.random.key(seed), 21)
    tokens = normal_values(key_list[0], (TOKENS, D), 1.0, 6.0, ((0, 32),))
    cotangent = normal_values(key_list[1], (TOKENS, D), 1.0, 6.0, ((0, 32),))
    segments = jax.vmap(lambda own: jnp.searchsorted(jnp.cumsum(uneven(own, ITEMS, LEN, ITEM_MAX, 2)), jnp.arange(LEN), side="right"))(jax.random.split(key_list[2], SEQS)).reshape((SEQS, LEN)).astype(jnp.int32)
    gates_local = jnp.clip(0.3 + 0.7 * jax.random.uniform(key_list[3], (SHARDS, GATE_LEN), jnp.float32) ** shard_levels(key_list[3], (SHARDS, GATE_LEN), ((0, 4),), -0.2, 0.2), 0.3, 1.0)
    gates_shared = jnp.clip(jax.random.uniform(key_list[4], (D + 2,), jnp.float32, 0.3, 1.0), 0.3, 1.0)
    gate_logits = draw_gate_logits(jax.random.fold_in(key_list[20], 71), 0)
    shared_logits = normal_values(key_list[6], (D + 2,), 1.5, 6.0, (), jnp.float32)
    masters = draw_masters(jax.random.fold_in(key_list[20], 71), 0)
    moment_one = draw_moment_one(jax.random.fold_in(key_list[20], 71), 0)
    moment_two = draw_moment_two(jax.random.fold_in(key_list[20], 71), 0)
    block_bases = draw_block_bases(jax.random.fold_in(key_list[20], 71), 0)
    block_stats = draw_block_stats(jax.random.fold_in(key_list[20], 71), 0)
    unit_params = normal_values(key_list[12], (SHARDS, UNIT_LEN), 0.3, 4.0, ((0, 4), (1, 8)), jnp.float32)
    unit_first = normal_values(key_list[13], (SHARDS, UNIT_LEN), (0.0526 * 0.4 * TOKENS ** 0.5), 5.0, ((0, 4), (1, 8)), jnp.float32)
    unit_second = jnp.clip(jnp.exp(math.log(275.77548) - 1.3862944 * jax.random.uniform(key_list[14], (SHARDS, UNIT_LEN), jnp.float32) ** shard_levels(key_list[14], (SHARDS, UNIT_LEN), ((0, 4), (1, 8)), -0.2, 0.2)), 68.94387, 275.77548)
    norm_params = draw_norm_params(jax.random.fold_in(key_list[20], 71), 0)
    norm_first = normal_values(key_list[16], (6, D), (0.0526 * 0.6 * TOKENS ** 0.5), 16.0, (), jnp.float32)
    norm_second = jnp.clip(jnp.exp(jax.random.uniform(key_list[17], (6, D), jnp.float32, math.log(155.12372), math.log(620.4949))), 155.12372, 620.4949)
    slot_ids = draw_slot_ids(jax.random.fold_in(key_list[20], 71), 0)
    step_count = jax.random.randint(key_list[19], (1,), 2, 21).astype(jnp.int32)
    return {"tokens": tokens, "cotangent": cotangent, "segments": segments, "gates_local": gates_local, "gates_shared": gates_shared, "gate_logits": gate_logits, "shared_logits": shared_logits, "masters": masters, "moment_one": moment_one, "moment_two": moment_two, "block_bases": block_bases, "block_stats": block_stats, "unit_params": unit_params, "unit_first": unit_first, "unit_second": unit_second, "norm_params": norm_params, "norm_first": norm_first, "norm_second": norm_second, "slot_ids": slot_ids, "step_count": step_count}


@jax.custom_vjp
def low(v):
    return lax.optimization_barrier(v.astype(jnp.bfloat16)).astype(jnp.float32)

@jax.custom_vjp
def low_back(v):
    return v

def low_keep(v):
    return (low(v), None)

def low_pass(kept, grad):
    return (grad,)

def back_keep(v):
    return (v, None)

def back_low(kept, grad):
    return (low(grad),)
low.defvjp(low_keep, low_pass)
low_back.defvjp(back_keep, back_low)
exact_mode = lax.Precision.HIGHEST
norm_eps = 1e-12
beta_one = 0.95
beta_two = 0.95
beta_stat = 0.95
adam_eps = 1e-08
rate_matrix = 0.1
rate_vector = 0.25
query_scale = 0.125
stretch_shift = 2.0 / 3.0 * math.log(0.1 / 1.1)

def keep_prob(logits):
    return jax.nn.sigmoid(logits - stretch_shift)

def assemble_all(blocks, row_size, col_size):
    shards = blocks.shape[0]
    tiling = blocks.reshape(shards, row_size // BLK, col_size // BLK, BLK, BLK)
    return tiling.transpose(0, 1, 3, 2, 4).reshape(shards, row_size, col_size)

def split_all(matrices):
    shards = matrices.shape[0]
    row_size = matrices.shape[1]
    col_size = matrices.shape[2]
    tiling = matrices.reshape(shards, row_size // BLK, BLK, col_size // BLK, BLK)
    return tiling.transpose(0, 1, 3, 2, 4).reshape(shards, row_size // BLK * (col_size // BLK), BLK, BLK)

def norm_apply(hidden, gain_row, shift_row, keeper):
    row_mean = lax.optimization_barrier(jnp.mean(hidden, axis=-1, keepdims=True))
    centred = hidden - row_mean
    variance = lax.optimization_barrier(jnp.mean(centred * centred, axis=-1, keepdims=True))
    return keeper * (centred * lax.rsqrt(variance + norm_eps) * gain_row + shift_row)

def attend_ref(packed):
    queries, key_rows, value_rows, labels = packed
    scores = low_back(jnp.einsum('qhd,khd->hqk', queries, key_rows, precision=exact_mode))
    same_item = labels[:, None] == labels[None, :]
    scores = jnp.where(same_item[None], scores, -1e+30)
    top_score = lax.optimization_barrier(jnp.max(scores, axis=-1, keepdims=True))
    weights = jnp.exp(scores - top_score)
    probability = weights / lax.optimization_barrier(jnp.sum(weights, axis=-1, keepdims=True))
    return low_back(jnp.einsum('hqk,khd->qhd', low(probability), value_rows, precision=exact_mode))

def layer_forward(params, token_rows, labels, gate_pack):
    qkv_weight, out_weight, up_weight, down_weight, unit_bias, norm_rows = params
    head_gate, unit_gate, keeper, mha_gate, ffn_gate = gate_pack
    row_total = token_rows.shape[0]
    shards = qkv_weight.shape[0]
    projected = jnp.einsum('rd,sdc->rsc', token_rows, qkv_weight, precision=exact_mode)
    queries = low_back(low((projected[:, :, :HEAD_COLS] + unit_bias[None, :, :HEAD_COLS]) * query_scale))
    key_rows = low_back(low(projected[:, :, HEAD_COLS:2 * HEAD_COLS]))
    value_rows = low_back(low(projected[:, :, 2 * HEAD_COLS:] + unit_bias[None, :, HEAD_COLS:2 * HEAD_COLS]))
    shaped = (row_total // LEN, LEN, shards * HEADS_T, HD)
    context = lax.map(jax.checkpoint(attend_ref), (queries.reshape(shaped), key_rows.reshape(shaped), value_rows.reshape(shaped), labels))
    gated_ctx = context.reshape(row_total, shards, HEADS_T, HD) * head_gate[None, :, :, None]
    gated_ctx = low(gated_ctx.reshape(row_total, shards, HEAD_COLS))
    pieces_one = low(low_back(jnp.einsum('rsc,scd->rsd', gated_ctx, out_weight, precision=exact_mode)))
    hidden_one = token_rows + mha_gate * (lax.optimization_barrier(jnp.sum(pieces_one, axis=1)) + norm_rows[2])
    middle = norm_apply(hidden_one, norm_rows[0], norm_rows[1], keeper)
    middle_low = low(middle)
    raised = low_back(jnp.einsum('rd,sdf->rsf', middle_low, up_weight, precision=exact_mode) + unit_bias[None, :, 2 * HEAD_COLS:])
    active = low(jax.nn.gelu(raised, approximate=False) * unit_gate[None])
    pieces_two = low(low_back(jnp.einsum('rsf,sfd->rsd', active, down_weight, precision=exact_mode)))
    hidden_two = middle + ffn_gate * (lax.optimization_barrier(jnp.sum(pieces_two, axis=1)) + norm_rows[5])
    return norm_apply(hidden_two, norm_rows[3], norm_rows[4], keeper)

def adam_moments(gradient, first_moment, second_moment, count_now):
    first_moment = beta_one * first_moment + (1.0 - beta_one) * gradient
    second_moment = beta_two * second_moment + (1.0 - beta_two) * gradient * gradient
    scaled = first_moment / (1.0 - beta_one ** count_now) / (jnp.sqrt(second_moment / (1.0 - beta_two ** count_now)) + adam_eps)
    return (first_moment, second_moment, scaled)

def orthonormal(panels):
    gram_matrix = jnp.einsum('...ij,...ik->...jk', panels, panels, precision=exact_mode)
    factor = jnp.linalg.cholesky(gram_matrix)
    return lax.linalg.triangular_solve(factor, panels, left_side=False, lower=True, transpose_a=True)

def soap_update(gradient, weights, first_moment, second_moment, basis_pair, stat_pair, count_now):
    left_basis = basis_pair[..., 0, :, :]
    right_basis = basis_pair[..., 1, :, :]
    turned = jnp.einsum('...ji,...jk->...ik', left_basis, gradient, precision=exact_mode)
    turned = jnp.einsum('...ik,...kl->...il', turned, right_basis, precision=exact_mode)
    first_moment, second_moment, scaled = adam_moments(turned, first_moment, second_moment, count_now)
    restored = jnp.einsum('...ij,...jk->...ik', left_basis, scaled, precision=exact_mode)
    restored = jnp.einsum('...ik,...lk->...il', restored, right_basis, precision=exact_mode)
    weights = weights - rate_matrix * restored
    left_stat = beta_stat * stat_pair[..., 0, :, :] + (1.0 - beta_stat) * jnp.einsum('...ik,...jk->...ij', gradient, gradient, precision=exact_mode)
    right_stat = beta_stat * stat_pair[..., 1, :, :] + (1.0 - beta_stat) * jnp.einsum('...ki,...kj->...ij', gradient, gradient, precision=exact_mode)
    new_left = orthonormal(jnp.einsum('...ij,...jk->...ik', left_stat, left_basis, precision=exact_mode))
    new_right = orthonormal(jnp.einsum('...ij,...jk->...ik', right_stat, right_basis, precision=exact_mode))
    return (weights, first_moment, second_moment, jnp.stack([new_left, new_right], axis=-3), jnp.stack([left_stat, right_stat], axis=-3))

def reference(tokens, cotangent, segments, gates_local, gates_shared, gate_logits, shared_logits, masters, moment_one, moment_two, block_bases, block_stats, unit_params, unit_first, unit_second, norm_params, norm_first, norm_second, slot_ids, step_count):
    square_shape = (SHARDS, SLOTS, BLK, BLK)
    pair_shape = (SHARDS, SLOTS, 2, BLK, BLK)
    master_sq = masters.reshape(square_shape)
    picked = master_sq.astype(jnp.bfloat16).astype(jnp.float32)[:, slot_ids]
    qkv_end = QKV_BLOCKS
    out_end = qkv_end + OUT_BLOCKS
    up_end = out_end + UP_BLOCKS
    params = (assemble_all(picked[:, :qkv_end], D, 3 * HEAD_COLS), assemble_all(picked[:, qkv_end:out_end], HEAD_COLS, D), assemble_all(picked[:, out_end:up_end], D, UNITS_T), assemble_all(picked[:, up_end:], UNITS_T, D), unit_params.astype(jnp.bfloat16).astype(jnp.float32), norm_params)
    gate_pack = (gates_local[:, :HEADS_T], gates_local[:, HEADS_T:], gates_shared[:D], gates_shared[D], gates_shared[D + 1])
    upper = max(1, min(SEQS, 4096 // LEN))
    per_group = max((divisor for divisor in range(1, upper + 1) if SEQS % divisor == 0))
    group_count = SEQS // per_group
    group_rows = per_group * LEN
    rows_all = tokens.astype(jnp.float32).reshape(group_count, group_rows, D)
    backs_all = cotangent.astype(jnp.float32).reshape(group_count, group_rows, D)
    labels_all = segments.reshape(group_count, per_group, LEN)

    def one_group(totals, packed):
        group_tokens, group_labels, group_back = packed

        def forward_rows(param_set, row_values):
            return layer_forward(param_set, row_values, group_labels, gate_pack)
        outputs, pullback = jax.vjp(forward_rows, params, group_tokens)
        d_params, d_rows = pullback(group_back)
        totals = jax.tree.map(jnp.add, totals, d_params)
        return (totals, (outputs.astype(jnp.bfloat16), d_rows))
    zeros_init = jax.tree.map(jnp.zeros_like, params)
    totals, (outputs, d_rows) = lax.scan(one_group, zeros_init, (rows_all, labels_all, backs_all))
    d_qkv, d_out, d_up, d_down, d_units, d_norm = totals
    grad_blocks = jnp.concatenate([split_all(d_qkv), split_all(d_out), split_all(d_up), split_all(d_down)], axis=1)
    block_grads = jnp.zeros(square_shape, jnp.float32).at[:, slot_ids].set(grad_blocks)
    count_now = step_count[0].astype(jnp.float32)
    masters_new, moment_one_new, moment_two_new, bases_new, stats_new = soap_update(block_grads, master_sq, moment_one.reshape(square_shape), moment_two.reshape(square_shape), block_bases.reshape(pair_shape), block_stats.reshape(pair_shape), count_now)
    unit_first_new, unit_second_new, unit_scaled = adam_moments(d_units, unit_first, unit_second, count_now)
    norm_first_new, norm_second_new, norm_scaled = adam_moments(d_norm, norm_first, norm_second, count_now)
    head_keep = keep_prob(gate_logits[:, :HEADS_T])
    unit_keep = keep_prob(gate_logits[:, HEADS_T:])
    shared_keep = keep_prob(shared_logits)
    hidden_sum = jnp.sum(shared_keep[:D])
    param_count = 1e-06 * (shared_keep[D] * jnp.sum(head_keep) * (4 * HD) * hidden_sum + shared_keep[D + 1] * jnp.sum(unit_keep) * 2 * hidden_sum)
    flat_shape = (SHARDS, SLOTS, BLK * BLK)
    pair_flat = (SHARDS, SLOTS, 2, BLK * BLK)
    return (outputs.reshape(TOKENS, D), d_rows.reshape(TOKENS, D), block_grads.reshape(flat_shape), masters_new.reshape(flat_shape), moment_one_new.reshape(flat_shape), moment_two_new.reshape(flat_shape), bases_new.reshape(pair_flat), stats_new.reshape(pair_flat), unit_params - rate_vector * unit_scaled, unit_first_new, unit_second_new, d_norm, norm_params - rate_vector * norm_scaled, norm_first_new, norm_second_new, param_count.reshape(1))
```

```python
import math
import functools
import jax
import jax.numpy as jnp
from jax import lax
from jax.sharding import PartitionSpec as P
from jax.experimental import pallas as pl
from jax.experimental.pallas import tpu as pltpu

BLK = 192
HALF = 96
QUART = 48
FLAT = 288
PAN = 32
beta_one = 0.95
beta_two = 0.95
beta_stat = 0.95
adam_eps = 1e-08
rate_matrix = 0.1
HIGH = lax.Precision.HIGH
EXACT = lax.Precision.HIGHEST


def mm(a, b, da, db, precision):
    return lax.dot_general(
        a, b, (((da,), (db,)), ((), ())), precision=precision, preferred_element_type=jnp.float32
    )


def read_square(src, lead, scratch, stride, first):
    def rows(q):
        return src[lead + (pl.ds(first + q * (stride // 3), HALF, stride=stride), slice(None))]

    a, b, c = rows(0), rows(1), rows(2)
    scratch[0, pl.ds(0, HALF, stride=2), :] = a
    scratch[1, pl.ds(0, HALF, stride=2), :] = b
    scratch[0, pl.ds(1, HALF, stride=2), :] = jnp.concatenate([b[:, 64:], c[:, :64]], axis=1)
    scratch[1, pl.ds(1, HALF, stride=2), :] = jnp.concatenate([c[:, 64:], c[:, 64:]], axis=1)
    return jnp.concatenate([scratch[0], scratch[1, :, :64]], axis=1)


def write_square(value, dst, lead, scratch, stride, first):
    scratch[0] = value[:, :128]
    scratch[1, :, :64] = value[:, 128:]
    e0 = scratch[0, pl.ds(0, HALF, stride=2), :]
    e1 = scratch[1, pl.ds(0, HALF, stride=2), :]
    o0 = scratch[0, pl.ds(1, HALF, stride=2), :]
    o1 = scratch[1, pl.ds(1, HALF, stride=2), :]
    step = stride // 3
    dst[lead + (pl.ds(first, HALF, stride=stride), slice(None))] = e0
    dst[lead + (pl.ds(first + step, HALF, stride=stride), slice(None))] = jnp.concatenate(
        [e1[:, :64], o0[:, :64]], axis=1
    )
    dst[lead + (pl.ds(first + 2 * step, HALF, stride=stride), slice(None))] = jnp.concatenate(
        [o0[:, 64:], o1[:, :64]], axis=1
    )


def soap_body(
    scale_ref, ka, ra, kb, rb, w_ref, m1_ref, m2_ref, b_ref, s_ref,
    g_out, w_out, m1_out, m2_out, s_out, mt_out, *scr,
):
    scratch = list(scr)
    ga = ka[0].astype(jnp.float32) + ra[0].astype(jnp.float32)
    gb = kb[0].astype(jnp.float32) + rb[0].astype(jnp.float32)
    g = jnp.concatenate([ga[:, :BLK], gb[:, :BLK], ga[:, BLK:], gb[:, BLK:]], axis=0)
    write_square(g, g_out, (0,), scratch[0], 3, 0)
    ql = read_square(b_ref, (0,), scratch[1], 6, 0)
    qr = read_square(b_ref, (0,), scratch[2], 6, 1)
    t3 = mm(g, qr, 1, 0, HIGH)
    r = mm(ql, t3, 0, 0, HIGH)
    rs, as_ = scratch[3], scratch[4]
    write_square(r, m1_out, (0,), rs, 3, 0)
    flat = m1_out[0]
    m1 = beta_one * m1_ref[0] + (1.0 - beta_one) * flat
    m2 = beta_two * m2_ref[0] + (1.0 - beta_two) * flat * flat
    m1_out[0] = m1
    m2_out[0] = m2
    corr = scale_ref[0, 0]
    w_out[0] = (m1 * corr) / (jnp.sqrt(m2 * corr) + adam_eps)
    a = read_square(w_out, (0,), as_, 3, 0)
    restored = mm(mm(ql, a, 1, 0, HIGH), qr, 1, 1, HIGH)
    write_square(restored, w_out, (0,), rs, 3, 0)
    w_out[0] = w_ref[0] - rate_matrix * w_out[0]
    sl = read_square(s_ref, (0,), scratch[5], 6, 0)
    sl = beta_stat * sl + (1.0 - beta_stat) * mm(g, g, 1, 1, HIGH)
    write_square(sl, s_out, (0,), scratch[6], 6, 0)
    mt_out[0, 0] = mm(ql, sl, 0, 0, HIGH)
    sr = read_square(s_ref, (0,), scratch[7], 6, 1)
    sr = beta_stat * sr + (1.0 - beta_stat) * mm(g, g, 0, 0, HIGH)
    write_square(sr, s_out, (0,), scratch[6], 6, 1)
    mt_out[0, 1] = mm(qr, sr, 0, 0, HIGH)


def soap_call(scale, ka, ra, kb, rb, w, m1, m2, b, s):
    n = w.shape[0]
    f32 = jnp.float32

    def spec(shape):
        zeros = (0,) * (len(shape) - 1)
        return pl.BlockSpec((1,) + shape[1:], lambda i: (i,) + zeros)

    ins = [ka, ra, kb, rb, w, m1, m2, b, s]
    outs = [
        jax.ShapeDtypeStruct((n, FLAT, 128), f32),
        jax.ShapeDtypeStruct((n, FLAT, 128), f32),
        jax.ShapeDtypeStruct((n, FLAT, 128), f32),
        jax.ShapeDtypeStruct((n, FLAT, 128), f32),
        jax.ShapeDtypeStruct((n, 2 * FLAT, 128), f32),
        jax.ShapeDtypeStruct((n, 2, BLK, BLK), f32),
    ]
    return pl.pallas_call(
        soap_body,
        grid=(n,),
        in_specs=[pl.BlockSpec(memory_space=pltpu.SMEM)] + [spec(x.shape) for x in ins],
        out_specs=[spec(o.shape) for o in outs],
        out_shape=outs,
        scratch_shapes=[pltpu.VMEM((2, BLK, 128), f32)] * 8,
        name="soap",
    )(scale, *ins)


def orth_body(mt_ref, q_out, ga, qt, xs, sq):
    n = mt_ref.shape[0] * 2
    for i in range(n):
        m = mt_ref[i // 2, i % 2]
        qt[i] = m
        ga[i] = mm(m, m, 1, 1, EXACT)
    lane = lax.broadcasted_iota(jnp.int32, (1, 1, 2 * PAN), 2)
    row_id = lax.broadcasted_iota(jnp.int32, (1, PAN, 1), 1)
    eye = (
        lax.broadcasted_iota(jnp.int32, (n, PAN, PAN), 1)
        == lax.broadcasted_iota(jnp.int32, (n, PAN, PAN), 2)
    ).astype(jnp.float32)
    for k in range(BLK // PAN):
        lo, hi = k * PAN, (k + 1) * PAN
        xs[...] = jnp.concatenate([ga[:, lo:hi, lo:hi], eye], axis=2)

        def step(j, carry):
            x = xs[...]
            row = xs[:, pl.ds(j, 1), :]
            col = jnp.sum(jnp.where(lane == j, x, 0.0), axis=2, keepdims=True)
            pivot = jnp.sum(jnp.where(lane == j, row, 0.0), axis=2, keepdims=True)
            factor = jnp.where(row_id > j, col / pivot, 0.0)
            xs[...] = x - factor * row
            return carry

        lax.fori_loop(0, PAN, step, 0)
        x = xs[...]
        diag = jnp.sum(jnp.where(lane == row_id, x, 0.0), axis=2, keepdims=True)
        t = x[:, :, PAN:] * lax.rsqrt(diag)
        for i in range(n):
            ti = t[i]
            wq = mm(ti, qt[i, lo:hi, :], 1, 0, EXACT)
            qt[i, lo:hi, :] = wq
            if hi < BLK:
                wa = mm(ti, ga[i, lo:hi, :], 1, 0, EXACT)
                rest = wa[:, hi:]
                ga[i, hi:, :] = ga[i, hi:, :] - mm(rest, wa, 0, 0, EXACT)
                qt[i, hi:, :] = qt[i, hi:, :] - mm(rest, wq, 0, 0, EXACT)
    for i in range(n):
        write_square(qt[i].T, q_out, (i // 2,), sq, 6, i % 2)


def orth_call(mt):
    n = mt.shape[0]
    f32 = jnp.float32
    return pl.pallas_call(
        orth_body,
        out_shape=jax.ShapeDtypeStruct((n, 2 * FLAT, 128), f32),
        scratch_shapes=[
            pltpu.VMEM((2 * n, BLK, BLK), f32),
            pltpu.VMEM((2 * n, BLK, BLK), f32),
            pltpu.VMEM((2 * n, PAN, 2 * PAN), f32),
            pltpu.VMEM((2, BLK, 128), f32),
        ],
        name="orth",
    )(mt)


D = 768
H = 12
FF = 3072
HD = 64
LEN = 1024
norm_eps = 1e-12
rate_vector = 0.25
query_scale = 0.125
stretch_shift = 2.0 / 3.0 * math.log(0.1 / 1.1)
root_half = 1.0 / math.sqrt(2.0)
normal_peak = 1.0 / math.sqrt(2.0 * math.pi)


def keep_prob(logits):
    return jax.nn.sigmoid(logits - stretch_shift)


def norm_forward(hidden, gain_row, shift_row, keeper):
    row_mean = jnp.mean(hidden, axis=-1, keepdims=True)
    centred = hidden - row_mean
    variance = jnp.mean(centred * centred, axis=-1, keepdims=True)
    inverse = lax.rsqrt(variance + norm_eps)
    normed = centred * inverse
    return (keeper * (normed * gain_row + shift_row), normed, inverse)


def norm_backward(incoming, normed, inverse, gain_row, keeper):
    scaled = incoming * keeper
    d_gain = jnp.sum(scaled * normed, axis=0)
    d_shift = jnp.sum(scaled, axis=0)
    d_normed = scaled * gain_row
    d_input = inverse * (
        d_normed
        - jnp.mean(d_normed, axis=-1, keepdims=True)
        - normed * jnp.mean(d_normed * normed, axis=-1, keepdims=True)
    )
    return (d_input, d_gain, d_shift)


def gelu_slope(values):
    return (
        0.5 * (1.0 + lax.erf(values * root_half))
        + values * jnp.exp(-0.5 * values * values) * normal_peak
    )


def attend_forward(packed):
    queries, key_rows, value_rows, labels = packed
    scores = jnp.einsum("qhd,khd->hqk", queries, key_rows, preferred_element_type=jnp.float32)
    same_item = labels[:, None] == labels[None, :]
    scores = jnp.where(same_item[None], scores, -1e30)
    top_score = jnp.max(scores, axis=-1, keepdims=True)
    weights = jnp.exp(scores - top_score)
    weight_sum = jnp.sum(weights, axis=-1, keepdims=True)
    probability = weights / weight_sum
    context = jnp.einsum(
        "hqk,khd->qhd",
        probability.astype(jnp.bfloat16),
        value_rows,
        preferred_element_type=jnp.float32,
    )
    return (context, (top_score + jnp.log(weight_sum))[..., 0])


def attend_backward(packed):
    queries, key_rows, value_rows, labels, log_total, d_context = packed
    scores = jnp.einsum("qhd,khd->hqk", queries, key_rows, preferred_element_type=jnp.float32)
    same_item = labels[:, None] == labels[None, :]
    scores = jnp.where(same_item[None], scores, -1e30)
    probability = jnp.exp(scores - log_total[..., None])
    d_value = jnp.einsum(
        "hqk,qhd->khd",
        probability.astype(jnp.bfloat16),
        d_context,
        preferred_element_type=jnp.float32,
    )
    d_probability = jnp.einsum(
        "qhd,khd->hqk", d_context, value_rows, preferred_element_type=jnp.float32
    )
    inner_sum = jnp.sum(probability * d_probability, axis=-1, keepdims=True)
    d_scores = (probability * (d_probability - inner_sum)).astype(jnp.bfloat16)
    d_query = jnp.einsum("hqk,khd->qhd", d_scores, key_rows, preferred_element_type=jnp.float32)
    d_keys = jnp.einsum("hqk,qhd->khd", d_scores, queries, preferred_element_type=jnp.float32)
    return (d_query.astype(jnp.bfloat16), d_keys.astype(jnp.bfloat16), d_value.astype(jnp.bfloat16))


def adam_moments(gradient, first_moment, second_moment, count_now):
    first_moment = beta_one * first_moment + (1.0 - beta_one) * gradient
    second_moment = beta_two * second_moment + (1.0 - beta_two) * gradient * gradient
    scaled = (
        first_moment
        / (1.0 - beta_one**count_now)
        / (jnp.sqrt(second_moment / (1.0 - beta_two**count_now)) + adam_eps)
    )
    return (first_moment, second_moment, scaled)


def bit_pairs(bit, size):
    return [(i, i ^ (1 << bit)) for i in range(size)]


def bit_count(size):
    return size.bit_length() - 1


def second_order(bits):
    return ([bits[1], bits[0]] + bits[2:]) if len(bits) > 1 else bits


def cast_body(w_ref, a_out, b_out, scratch):
    m = read_square(w_ref, (0,), scratch, 3, 0)
    packed = jnp.concatenate([m[:HALF], m[HALF:]], axis=1).astype(jnp.bfloat16)
    a_out[0] = packed[:QUART]
    b_out[0] = packed[QUART:]


def cast_call(flat):
    n = flat.shape[0]
    piece = jax.ShapeDtypeStruct((n, QUART, 2 * BLK), jnp.bfloat16)
    spec = pl.BlockSpec((1, QUART, 2 * BLK), lambda i: (i, 0, 0))
    return pl.pallas_call(
        cast_body,
        grid=(n,),
        in_specs=[pl.BlockSpec((1, FLAT, 128), lambda i: (i, 0, 0))],
        out_specs=[spec, spec],
        out_shape=[piece, piece],
        scratch_shapes=[pltpu.VMEM((2, BLK, 128), jnp.float32)],
        name="cast",
    )(flat)


def spread(block, order, size):
    pieces = [block[None]]
    rel = [[0]]
    for bit in order:
        moved = [lax.ppermute(p, "dp", bit_pairs(bit, size)) for p in pieces]
        rel = rel + [[r ^ (1 << bit) for r in group] for group in rel]
        pieces = pieces + moved
        if size > 8:
            pieces = [jnp.concatenate(pieces)]
            rel = [sum(rel, [])]
    return pieces, sum(rel, [])


def build_body(pos_a, pos_b, *refs, count, total, qkv_cols, heads_rows):
    ins_a, ins_b = refs[:count], refs[count : 2 * count]
    outs = refs[2 * count : 2 * count + 4]
    buf_a, buf_b, sems = refs[2 * count + 4 :]
    copies = []
    for side, (ins, buf) in enumerate(((ins_a, buf_a), (ins_b, buf_b))):
        at = 0
        for i, src in enumerate(ins):
            m = src.shape[0]
            copy = pltpu.make_async_copy(src, buf.at[pl.ds(at, m)], sems.at[side, i])
            copy.start()
            copies.append(copy)
            at += m
    for copy in copies:
        copy.wait()
    base = 0
    for out in outs:
        rows, cols = out.shape[0] // BLK, out.shape[1] // BLK
        for i in range(rows):
            for side, (buf, pos) in enumerate(((buf_a, pos_a), (buf_b, pos_b))):
                got = [buf[pos[base + i * cols + j]] for j in range(cols)]
                at = i * BLK + side * QUART
                out[at : at + QUART, :] = jnp.concatenate([g[:, :BLK] for g in got], axis=1)
                at += HALF
                out[at : at + QUART, :] = jnp.concatenate([g[:, BLK:] for g in got], axis=1)
        base += rows * cols


def build_call(pos_a, pos_b, pieces_a, pieces_b, shapes):
    slots = pieces_a[0].shape[1]
    flat_a = [p.reshape(-1, QUART, 2 * BLK) for p in pieces_a]
    flat_b = [p.reshape(-1, QUART, 2 * BLK) for p in pieces_b]
    count = len(flat_a)
    total = sum(p.shape[0] for p in flat_a)
    bf16 = jnp.bfloat16
    kernel = functools.partial(build_body, count=count, total=total, qkv_cols=0, heads_rows=0)
    return pl.pallas_call(
        kernel,
        in_specs=[pl.BlockSpec(memory_space=pltpu.SMEM)] * 2
        + [pl.BlockSpec(memory_space=pl.ANY)] * (2 * count),
        out_shape=[jax.ShapeDtypeStruct(s, bf16) for s in shapes],
        scratch_shapes=[
            pltpu.VMEM((total, QUART, 2 * BLK), bf16),
            pltpu.VMEM((total, QUART, 2 * BLK), bf16),
            pltpu.SemaphoreType.DMA((2, count)),
        ],
        name="build",
    )(pos_a, pos_b, *flat_a, *flat_b)


def pack_body(pos_a, pos_b, *refs, clear):
    ins, (out_a, out_b) = refs[:-2], refs[-2:]
    if clear:
        out_a[...] = jnp.zeros_like(out_a)
        out_b[...] = jnp.zeros_like(out_b)
    base = 0
    for src in ins:
        rows, cols = src.shape[0] // BLK, src.shape[1] // BLK
        for i in range(rows):
            for side, (out, pos) in enumerate(((out_a, pos_a), (out_b, pos_b))):
                at = i * BLK + side * QUART
                top = src[at : at + QUART, :].astype(jnp.bfloat16)
                low = src[at + HALF : at + HALF + QUART, :].astype(jnp.bfloat16)
                for j in range(cols):
                    cut = slice(j * BLK, (j + 1) * BLK)
                    out[pos[base + i * cols + j]] = jnp.concatenate(
                        [top[:, cut], low[:, cut]], axis=1
                    )
        base += rows * cols


def pack_call(pos_a, pos_b, grads, total):
    blocks = sum(g.shape[0] * g.shape[1] for g in grads) // (BLK * BLK)
    piece = jax.ShapeDtypeStruct((total, QUART, 2 * BLK), jnp.bfloat16)
    return pl.pallas_call(
        functools.partial(pack_body, clear=total > blocks),
        in_specs=[pl.BlockSpec(memory_space=pltpu.SMEM)] * 2
        + [pl.BlockSpec(memory_space=pltpu.VMEM)] * len(grads),
        out_shape=[piece, piece],
        name="pack",
    )(pos_a, pos_b, *grads)


def fold(payload, order, size):
    cur = payload
    for step, bit in enumerate(order):
        half = cur.shape[0] // 2
        keep, send = cur[:half], cur[half:]
        got = lax.ppermute(send, "dp", bit_pairs(bit, size))
        if step == len(order) - 1:
            return keep, got
        cur = (keep.astype(jnp.float32) + got.astype(jnp.float32)).astype(jnp.bfloat16)


def fold_position(owner, slot, order, slots, me):
    rel = owner ^ me
    index = jnp.zeros_like(rel)
    for bit in order:
        index = index * 2 + ((rel >> bit) & 1)
    return index * slots + slot


def butterfly(value, axis, size):
    for bit in range(bit_count(size)):
        value = value + lax.ppermute(value, axis, bit_pairs(bit, size))
    return value


def gather_rows(rows, shards):
    moved = [
        lax.ppermute(rows, "tensor", [(i, (i - s) % shards) for i in range(shards)])
        for s in range(1, shards)
    ]
    return jnp.concatenate([rows] + moved, axis=0)


def scatter_rows(rows, shards):
    cut = rows.shape[0] // shards
    total = rows[:cut].astype(jnp.float32)
    for s in range(1, shards):
        got = lax.ppermute(
            rows[s * cut : (s + 1) * cut],
            "tensor",
            [(i, (i + s) % shards) for i in range(shards)],
        )
        total = total + got.astype(jnp.float32)
    return total


def body(
    tokens,
    cotangent,
    segments,
    gates_local,
    gates_shared,
    gate_logits,
    shared_logits,
    masters,
    moment_one,
    moment_two,
    block_bases,
    block_stats,
    unit_params,
    unit_first,
    unit_second,
    norm_params,
    norm_first,
    norm_second,
    slot_ids,
    step_count,
):
    shards = lax.axis_size("tensor")
    owners = lax.axis_size("dp")
    head_count = H // shards
    head_cols = head_count * HD
    unit_count = FF // shards
    seq_count = segments.shape[0]
    row_total = seq_count * LEN
    slot_count = masters.shape[1]
    me = lax.axis_index("dp")
    place = lax.axis_index("tensor")
    bits = list(range(bit_count(owners)))
    head_keep = keep_prob(gate_logits[0, :head_count])
    unit_keep = keep_prob(gate_logits[0, head_count:])
    shared_keep = keep_prob(shared_logits)
    keep_row = jnp.zeros((1, D), jnp.float32)
    keep_row = keep_row.at[0, 0].set(jnp.sum(head_keep)).at[0, 1].set(jnp.sum(unit_keep))
    flat_view = (slot_count, FLAT, 128)
    cast_a, cast_b = cast_call(masters.reshape(flat_view))
    order_a = bits[1:] + bits[:1]
    order_b = second_order(bits[1:]) + bits[:1]
    pieces_a, rel_a = spread(cast_a, order_a, owners)
    pieces_b, rel_b = spread(cast_b, order_b, owners)
    owner_of = slot_ids // slot_count
    slot_of = slot_ids % slot_count
    rel_of = owner_of ^ me

    def piece_spot(rel_list):
        table = [0] * owners
        for spot, rel in enumerate(rel_list):
            table[rel] = spot
        return jnp.asarray(table, jnp.int32)[rel_of] * slot_count + slot_of

    qkv_weight, out_weight, up_weight, down_weight = build_call(
        piece_spot(rel_a),
        piece_spot(rel_b),
        pieces_a,
        pieces_b,
        ((D, 3 * head_cols), (head_cols, D), (D, unit_count), (unit_count, D)),
    )
    unit_low = unit_params.astype(jnp.bfloat16)
    unit_pieces, unit_rel = spread(unit_low[0], bits, owners)
    unit_all = jnp.concatenate(unit_pieces, axis=0)
    unit_bias = unit_all[jnp.arange(owners) ^ me].reshape(-1).astype(jnp.float32)
    head_gate = gates_local[0, :head_count]
    unit_gate = gates_local[0, head_count:]
    keeper = gates_shared[:D]
    mha_gate = gates_shared[D]
    ffn_gate = gates_shared[D + 1]
    gain_one = norm_params[0]
    shift_one = norm_params[1]
    bias_attn = norm_params[2]
    gain_two = norm_params[3]
    shift_two = norm_params[4]
    bias_ffn = norm_params[5]
    token_rows = gather_rows(tokens, shards)
    labels = lax.dynamic_slice(
        jnp.concatenate([segments, segments], axis=1), (0, place * (LEN // shards)), (1, LEN)
    )[0]
    projected = jnp.dot(token_rows, qkv_weight, preferred_element_type=jnp.float32)
    queries = ((projected[:, :head_cols] + unit_bias[:head_cols]) * query_scale).astype(
        jnp.bfloat16
    )
    key_rows = projected[:, head_cols : 2 * head_cols].astype(jnp.bfloat16)
    value_rows = (projected[:, 2 * head_cols :] + unit_bias[head_cols : 2 * head_cols]).astype(
        jnp.bfloat16
    )
    shaped = (LEN, head_count, HD)
    query_seq = queries.reshape(shaped)
    key_seq = key_rows.reshape(shaped)
    value_seq = value_rows.reshape(shaped)
    context, log_total = attend_forward((query_seq, key_seq, value_seq, labels))
    gated_ctx = (
        (context.reshape(row_total, head_count, HD) * head_gate[:, None])
        .reshape(row_total, head_cols)
        .astype(jnp.bfloat16)
    )
    attn_sum = scatter_rows(jnp.dot(gated_ctx, out_weight, preferred_element_type=jnp.float32).astype(jnp.bfloat16), shards)
    residual = tokens.astype(jnp.float32)
    hidden_one = residual + mha_gate * (attn_sum + bias_attn)
    middle, normed_one, inverse_one = norm_forward(hidden_one, gain_one, shift_one, keeper)
    middle_rows = gather_rows(middle.astype(jnp.bfloat16), shards)
    raised = (
        jnp.dot(middle_rows, up_weight, preferred_element_type=jnp.float32)
        + unit_bias[2 * head_cols :]
    )
    hidden_low = (jax.nn.gelu(raised, approximate=False) * unit_gate).astype(jnp.bfloat16)
    ffn_sum = scatter_rows(jnp.dot(hidden_low, down_weight, preferred_element_type=jnp.float32).astype(jnp.bfloat16), shards)
    hidden_two = middle + ffn_gate * (ffn_sum + bias_ffn)
    layer_out, normed_two, inverse_two = norm_forward(hidden_two, gain_two, shift_two, keeper)
    upstream = cotangent.astype(jnp.float32)
    grad_two, d_gain_two, d_shift_two = norm_backward(
        upstream, normed_two, inverse_two, gain_two, keeper
    )
    d_bias_ffn = ffn_gate * jnp.sum(grad_two, axis=0)
    branch_low = (ffn_gate * grad_two).astype(jnp.bfloat16)
    gathered = gather_rows(branch_low, shards)
    d_hidden = jnp.einsum("rd,fd->rf", gathered, down_weight, preferred_element_type=jnp.float32)
    d_down = jnp.einsum("rf,rd->fd", hidden_low, gathered, preferred_element_type=jnp.float32)
    d_hidden, d_down = (d_hidden, d_down)
    d_raised = (d_hidden * unit_gate * gelu_slope(raised)).astype(jnp.bfloat16)
    d_up_bias = jnp.sum(d_raised.astype(jnp.float32), axis=0)
    d_up = jnp.einsum("rd,rf->df", middle_rows, d_raised, preferred_element_type=jnp.float32)
    grad_middle = grad_two + scatter_rows(jnp.einsum("rf,df->rd", d_raised, up_weight, preferred_element_type=jnp.float32).astype(
            jnp.bfloat16
        ), shards)
    grad_one, d_gain_one, d_shift_one = norm_backward(
        grad_middle, normed_one, inverse_one, gain_one, keeper
    )
    d_bias_attn = mha_gate * jnp.sum(grad_one, axis=0)
    attn_low = (mha_gate * grad_one).astype(jnp.bfloat16)
    gathered = gather_rows(attn_low, shards)
    d_gated = jnp.einsum("rd,cd->rc", gathered, out_weight, preferred_element_type=jnp.float32)
    d_out = jnp.einsum("rc,rd->cd", gated_ctx, gathered, preferred_element_type=jnp.float32)
    d_gated, d_out = (d_gated, d_out)
    d_context = (
        (d_gated.reshape(row_total, head_count, HD) * head_gate[:, None])
        .astype(jnp.bfloat16)
        .reshape(shaped)
    )
    d_query, d_keys, d_value = attend_backward(
        (query_seq, key_seq, value_seq, labels, log_total, d_context)
    )
    d_query = d_query.reshape(row_total, head_cols) * query_scale
    d_keys = d_keys.reshape(row_total, head_cols)
    d_value = d_value.reshape(row_total, head_cols)
    d_qkv = jnp.concatenate([d_query, d_keys, d_value], axis=1)
    d_units = jnp.concatenate(
        [
            jnp.sum(d_query.astype(jnp.float32), axis=0),
            jnp.sum(d_value.astype(jnp.float32), axis=0),
            d_up_bias,
        ]
    )
    d_weight_qkv = jnp.einsum("rd,rc->dc", token_rows, d_qkv, preferred_element_type=jnp.float32)
    token_grad = grad_one + scatter_rows(jnp.einsum("rc,dc->rd", d_qkv, qkv_weight, preferred_element_type=jnp.float32).astype(
            jnp.bfloat16
        ), shards)
    fold_a = bits
    fold_b = bits[:1] + second_order(bits[1:])
    load_a, load_b = pack_call(
        fold_position(owner_of, slot_of, fold_a, slot_count, me),
        fold_position(owner_of, slot_of, fold_b, slot_count, me),
        (d_weight_qkv, d_out, d_up, d_down),
        owners * slot_count,
    )
    keep_a, got_a = fold(load_a, fold_a, owners)
    keep_b, got_b = fold(load_b, fold_b, owners)
    share = unit_params.shape[1]
    unit_grad = lax.dynamic_slice(butterfly(d_units, "dp", owners), (me * share,), (share,))
    norm_local = jnp.concatenate(
        [
            jnp.stack([d_gain_one, d_shift_one, d_bias_attn, d_gain_two, d_shift_two, d_bias_ffn]),
            keep_row,
        ]
    )
    summed = butterfly(butterfly(norm_local, "tensor", shards), "dp", owners)
    norm_grads = summed[:6]
    keep_sums = summed[6, :2] * (1.0 / owners)
    count_now = step_count[0].astype(jnp.float32)

    def pair_view(x):
        x = x.reshape(slot_count, 2, FLAT, 128)
        return x.transpose(0, 2, 1, 3).reshape(slot_count, 2 * FLAT, 128)

    def pair_back(x):
        x = x.reshape(slot_count, FLAT, 2, 128).transpose(0, 2, 1, 3)
        return x.reshape(1, slot_count, 2, BLK * BLK)

    correction = (1.0 / (1.0 - beta_one**count_now)).reshape(1, 1)
    owned, masters_new, moment_one_new, moment_two_new, stats_new, turned = soap_call(
        correction,
        keep_a,
        got_a,
        keep_b,
        got_b,
        masters.reshape(flat_view),
        moment_one.reshape(flat_view),
        moment_two.reshape(flat_view),
        pair_view(block_bases),
        pair_view(block_stats),
    )
    bases_new = orth_call(turned)
    flat_shape = (1, slot_count, BLK * BLK)
    unit_first_new, unit_second_new, unit_scaled = adam_moments(
        unit_grad, unit_first[0], unit_second[0], count_now
    )
    norm_first_new, norm_second_new, norm_scaled = adam_moments(
        norm_grads, norm_first, norm_second, count_now
    )
    hidden_sum = jnp.sum(shared_keep[:D])
    param_count = 1e-06 * (
        shared_keep[D] * keep_sums[0] * (4 * HD) * hidden_sum
        + shared_keep[D + 1] * keep_sums[1] * 2 * hidden_sum
    )
    return (
        layer_out.astype(jnp.bfloat16),
        token_grad,
        owned.reshape(flat_shape),
        masters_new.reshape(flat_shape),
        moment_one_new.reshape(flat_shape),
        moment_two_new.reshape(flat_shape),
        pair_back(bases_new),
        pair_back(stats_new),
        (unit_params[0] - rate_vector * unit_scaled)[None],
        unit_first_new[None],
        unit_second_new[None],
        norm_grads,
        norm_params - rate_vector * norm_scaled,
        norm_first_new,
        norm_second_new,
        param_count.reshape(1),
    )


def solution(mesh):
    placed = (
        P(("dp", "tensor"), None),
        P(("dp", "tensor"), None),
        P("dp", None),
        P("tensor", None),
        P(),
        P("tensor", None),
        P(),
        P("tensor", "dp", None),
        P("tensor", "dp", None),
        P("tensor", "dp", None),
        P("tensor", "dp", None, None),
        P("tensor", "dp", None, None),
        P("tensor", "dp"),
        P("tensor", "dp"),
        P("tensor", "dp"),
        P(),
        P(),
        P(),
        P(),
        P(),
    )
    return jax.shard_map(
        body,
        mesh=mesh,
        in_specs=placed,
        out_specs=(
            P(("dp", "tensor"), None),
            P(("dp", "tensor"), None),
            P("tensor", "dp", None),
            P("tensor", "dp", None),
            P("tensor", "dp", None),
            P("tensor", "dp", None),
            P("tensor", "dp", None, None),
            P("tensor", "dp", None, None),
            P("tensor", "dp"),
            P("tensor", "dp"),
            P("tensor", "dp"),
            P(),
            P(),
            P(),
            P(),
            P(),
        ),
        check_vma=False,
    )
```

```python
import math
import functools
import jax
import jax.numpy as jnp
from jax import lax
from jax.sharding import PartitionSpec as P
from jax.experimental import pallas as pl
from jax.experimental.pallas import tpu as pltpu

BLK = 192
HALF = 96
QUART = 48
FLAT = 288
PAN = 64
beta_one = 0.95
beta_two = 0.95
beta_stat = 0.95
adam_eps = 1e-08
rate_matrix = 0.1
HIGH = lax.Precision.HIGH
EXACT = lax.Precision.HIGHEST


def mm(a, b, da, db, precision):
    return lax.dot_general(
        a, b, (((da,), (db,)), ((), ())), precision=precision, preferred_element_type=jnp.float32
    )


def read_square(src, lead, scratch, stride, first):
    def rows(q):
        return src[lead + (pl.ds(first + q * (stride // 3), HALF, stride=stride), slice(None))]

    a, b, c = rows(0), rows(1), rows(2)
    scratch[0, pl.ds(0, HALF, stride=2), :] = a
    scratch[1, pl.ds(0, HALF, stride=2), :] = b
    scratch[0, pl.ds(1, HALF, stride=2), :] = jnp.concatenate([b[:, 64:], c[:, :64]], axis=1)
    scratch[1, pl.ds(1, HALF, stride=2), :] = jnp.concatenate([c[:, 64:], c[:, 64:]], axis=1)
    return jnp.concatenate([scratch[0], scratch[1, :, :64]], axis=1)


def write_square(value, dst, lead, scratch, stride, first):
    scratch[0] = value[:, :128]
    scratch[1, :, :64] = value[:, 128:]
    e0 = scratch[0, pl.ds(0, HALF, stride=2), :]
    e1 = scratch[1, pl.ds(0, HALF, stride=2), :]
    o0 = scratch[0, pl.ds(1, HALF, stride=2), :]
    o1 = scratch[1, pl.ds(1, HALF, stride=2), :]
    step = stride // 3
    dst[lead + (pl.ds(first, HALF, stride=stride), slice(None))] = e0
    dst[lead + (pl.ds(first + step, HALF, stride=stride), slice(None))] = jnp.concatenate(
        [e1[:, :64], o0[:, :64]], axis=1
    )
    dst[lead + (pl.ds(first + 2 * step, HALF, stride=stride), slice(None))] = jnp.concatenate(
        [o0[:, 64:], o1[:, :64]], axis=1
    )


def soap_body(
    scale_ref, ka, ra, kb, rb, w_ref, m1_ref, m2_ref, b_ref, s_ref,
    g_out, w_out, m1_out, m2_out, s_out, mt_out, *scr,
):
    scratch = list(scr)
    ga = ka[0].astype(jnp.float32) + ra[0].astype(jnp.float32)
    gb = kb[0].astype(jnp.float32) + rb[0].astype(jnp.float32)
    g = jnp.concatenate([ga[:, :BLK], gb[:, :BLK], ga[:, BLK:], gb[:, BLK:]], axis=0)
    write_square(g, g_out, (0,), scratch[0], 3, 0)
    ql = read_square(b_ref, (0,), scratch[1], 6, 0)
    qr = read_square(b_ref, (0,), scratch[2], 6, 1)
    t3 = mm(g, qr, 1, 0, HIGH)
    r = mm(ql, t3, 0, 0, HIGH)
    rs, as_ = scratch[3], scratch[4]
    write_square(r, m1_out, (0,), rs, 3, 0)
    flat = m1_out[0]
    m1 = beta_one * m1_ref[0] + (1.0 - beta_one) * flat
    m2 = beta_two * m2_ref[0] + (1.0 - beta_two) * flat * flat
    m1_out[0] = m1
    m2_out[0] = m2
    corr = scale_ref[0, 0]
    w_out[0] = (m1 * corr) / (jnp.sqrt(m2 * corr) + adam_eps)
    a = read_square(w_out, (0,), as_, 3, 0)
    restored = mm(mm(ql, a, 1, 0, HIGH), qr, 1, 1, HIGH)
    write_square(restored, w_out, (0,), rs, 3, 0)
    w_out[0] = w_ref[0] - rate_matrix * w_out[0]
    sl = read_square(s_ref, (0,), scratch[5], 6, 0)
    sl = beta_stat * sl + (1.0 - beta_stat) * mm(g, g, 1, 1, HIGH)
    write_square(sl, s_out, (0,), scratch[6], 6, 0)
    mt_out[0, 0] = mm(ql, sl, 0, 0, EXACT)
    sr = read_square(s_ref, (0,), scratch[7], 6, 1)
    sr = beta_stat * sr + (1.0 - beta_stat) * mm(g, g, 0, 0, HIGH)
    write_square(sr, s_out, (0,), scratch[6], 6, 1)
    mt_out[0, 1] = mm(qr, sr, 0, 0, EXACT)


def soap_call(scale, ka, ra, kb, rb, w, m1, m2, b, s):
    n = w.shape[0]
    f32 = jnp.float32

    def spec(shape):
        zeros = (0,) * (len(shape) - 1)
        return pl.BlockSpec((1,) + shape[1:], lambda i: (i,) + zeros)

    ins = [ka, ra, kb, rb, w, m1, m2, b, s]
    outs = [
        jax.ShapeDtypeStruct((n, FLAT, 128), f32),
        jax.ShapeDtypeStruct((n, FLAT, 128), f32),
        jax.ShapeDtypeStruct((n, FLAT, 128), f32),
        jax.ShapeDtypeStruct((n, FLAT, 128), f32),
        jax.ShapeDtypeStruct((n, 2 * FLAT, 128), f32),
        jax.ShapeDtypeStruct((n, 2, BLK, BLK), f32),
    ]
    return pl.pallas_call(
        soap_body,
        grid=(n,),
        in_specs=[pl.BlockSpec(memory_space=pltpu.SMEM)] + [spec(x.shape) for x in ins],
        out_specs=[spec(o.shape) for o in outs],
        out_shape=outs,
        scratch_shapes=[pltpu.VMEM((2, BLK, 128), f32)] * 8,
        name="soap",
    )(scale, *ins)


def orth_body(mt_ref, q_out, xa, xs, sq):
    n = mt_ref.shape[0] * 2
    for i in range(n):
        m = mt_ref[i // 2, i % 2]
        xa[i, :, 256 : 256 + BLK] = m
        xa[i, :, 0:BLK] = mm(m, m, 1, 1, EXACT)
    lane = lax.broadcasted_iota(jnp.int32, (1, 1, 2 * PAN), 2)
    eye = (
        lax.broadcasted_iota(jnp.int32, (n, PAN, PAN), 1)
        == lax.broadcasted_iota(jnp.int32, (n, PAN, PAN), 2)
    ).astype(jnp.float32)

    def pick(v, j):
        return jnp.sum(jnp.where(lane == j, v, 0.0), axis=2, keepdims=True)

    for k in range(BLK // PAN):
        lo, hi = k * PAN, (k + 1) * PAN
        xs[...] = jnp.concatenate([xa[:, lo:hi, lo:hi], eye], axis=2)
        for first in range(0, PAN, 8):
            row_id = lax.broadcasted_iota(jnp.int32, (1, PAN - first, 1), 1) + first

            def step(s, carry):
                x = xs[:, first:, :]
                j = first + 2 * s
                r0 = xs[:, pl.ds(j, 1), :]
                r1 = xs[:, pl.ds(j + 1, 1), :]
                c0, c1 = pick(x, j), pick(x, j + 1)
                p, q, d = pick(r0, j), pick(r0, j + 1), pick(r1, j + 1)
                ip = 1.0 / p
                e = q * ip
                r1 = r1 - e * r0
                ip1 = 1.0 / (d - e * q)
                f0 = c0 * ip
                f1 = (c1 - f0 * q) * ip1
                f0 = jnp.where(row_id > j, f0, 0.0)
                f1 = jnp.where(row_id > j + 1, f1, 0.0)
                xs[:, first:, :] = x - (f0 * r0 + f1 * r1)
                return carry

            lax.fori_loop(0, 4, step, 0)
        x = xs[...]
        row_id = lax.broadcasted_iota(jnp.int32, (1, PAN, 1), 1)
        diag = jnp.sum(jnp.where(lane == row_id, x, 0.0), axis=2, keepdims=True)
        t = x[:, :, PAN:] * lax.rsqrt(diag)
        for i in range(n):
            w = mm(t[i], xa[i, lo:hi, :], 1, 0, EXACT)
            xa[i, lo:hi, :] = w
            if hi < BLK:
                wt = w[:, :256].T[hi:BLK]
                xa[i, hi:, :] = xa[i, hi:, :] - mm(wt, w, 1, 0, EXACT)
    for i in range(n):
        write_square(xa[i, :, 256:].T[:BLK], q_out, (i // 2,), sq, 6, i % 2)


def orth_call(mt):
    n = mt.shape[0]
    f32 = jnp.float32
    return pl.pallas_call(
        orth_body,
        out_shape=jax.ShapeDtypeStruct((n, 2 * FLAT, 128), f32),
        scratch_shapes=[
            pltpu.VMEM((2 * n, BLK, 512), f32),
            pltpu.VMEM((2 * n, PAN, 2 * PAN), f32),
            pltpu.VMEM((2, BLK, 128), f32),
        ],
        name="orth",
    )(mt)


D = 768
H = 12
FF = 3072
HD = 64
LEN = 1024
norm_eps = 1e-12
rate_vector = 0.25
query_scale = 0.125
stretch_shift = 2.0 / 3.0 * math.log(0.1 / 1.1)
root_half = 1.0 / math.sqrt(2.0)
normal_peak = 1.0 / math.sqrt(2.0 * math.pi)


def keep_prob(logits):
    return jax.nn.sigmoid(logits - stretch_shift)


def norm_forward(hidden, gain_row, shift_row, keeper):
    row_mean = jnp.mean(hidden, axis=-1, keepdims=True)
    centred = hidden - row_mean
    variance = jnp.mean(centred * centred, axis=-1, keepdims=True)
    inverse = lax.rsqrt(variance + norm_eps)
    normed = centred * inverse
    return (keeper * (normed * gain_row + shift_row), normed, inverse)


def norm_backward(incoming, normed, inverse, gain_row, keeper):
    scaled = incoming * keeper
    d_gain = jnp.sum(scaled * normed, axis=0)
    d_shift = jnp.sum(scaled, axis=0)
    d_normed = scaled * gain_row
    d_input = inverse * (
        d_normed
        - jnp.mean(d_normed, axis=-1, keepdims=True)
        - normed * jnp.mean(d_normed * normed, axis=-1, keepdims=True)
    )
    return (d_input, d_gain, d_shift)


def project_body(*refs):
    xs, (w, bias, q_out, k_out, v_out) = refs[:-5], refs[-5:]
    weight = w[...]
    for s, x in enumerate(xs):
        rows = slice(s * x.shape[0], (s + 1) * x.shape[0])
        out = dot(x[...], weight, 1, 0)
        cols = q_out.shape[1]
        q_out[rows] = ((out[:, :cols] + bias[0:1]) * query_scale).astype(jnp.bfloat16)
        k_out[rows] = out[:, cols : 2 * cols].astype(jnp.bfloat16)
        v_out[rows] = (out[:, 2 * cols :] + bias[1:2]).astype(jnp.bfloat16)


def project_call(pieces, weight, bias):
    rows = sum(p.shape[0] for p in pieces)
    out = jax.ShapeDtypeStruct((rows, bias.shape[1]), jnp.bfloat16)
    return pl.pallas_call(project_body, out_shape=[out] * 3, name="project")(
        *pieces, weight, bias
    )


def dot(a, b, da, db):
    return lax.dot_general(
        a, b, (((da,), (db,)), ((), ())), preferred_element_type=jnp.float32
    )


def partners(piece, shards):
    return [piece ^ s for s in range(shards) if s != 2]


def item_bias(seg_col, seg_row, piece, peers, span):
    mine = seg_row[0:1, piece * span : (piece + 1) * span]
    return [
        jnp.where(seg_col[c * span : (c + 1) * span, :] == mine, 0.0, -1e30) for c in peers
    ]


def attend_body(q, k, v, seg_col, seg_row, gate_col, w, *outs, pieces, shards):
    span = q.shape[0] // shards
    cg_out, lse_out = outs[0], outs[1]
    heads = q.shape[1] // HD
    weight = w[...]
    lse_out[...] = jnp.zeros_like(lse_out)
    for at, p in enumerate(pieces):
        peers = partners(p, shards)
        bias = item_bias(seg_col, seg_row, p, peers, span)
        rows = slice(p * span, (p + 1) * span)
        mine = slice(at * span, (at + 1) * span)
        parts = []
        for h in range(heads):
            cut = slice(h * HD, (h + 1) * HD)
            qp = q[rows, cut]
            scores = [
                dot(k[c * span : (c + 1) * span, cut], qp, 1, 1) + b for c, b in zip(peers, bias)
            ]
            top = functools.reduce(jnp.maximum, [jnp.max(s, axis=0, keepdims=True) for s in scores])
            powers = [jnp.exp(s - top) for s in scores]
            total = functools.reduce(
                jnp.add, [jnp.sum(e, axis=0, keepdims=True) for e in powers]
            )
            inverse = 1.0 / total
            context = functools.reduce(
                jnp.add,
                [
                    dot(
                        v[c * span : (c + 1) * span, cut],
                        (e * inverse).astype(jnp.bfloat16),
                        0,
                        0,
                    )
                    for c, e in zip(peers, powers)
                ],
            )
            parts.append(context)
            lse_out[h : h + 1, mine] = top + jnp.log(total)
        gated = (jnp.concatenate(parts, axis=0) * gate_col[...]).T.astype(jnp.bfloat16)
        cg_out[mine] = gated
        outs[2 + at][...] = dot(gated, weight, 1, 0).astype(jnp.bfloat16)


def attend_call(q, k, v, seg_col, seg_row, gate_col, weight, pieces, shards):
    span = q.shape[0] // shards
    bf16 = jnp.bfloat16
    count = len(pieces)
    outs = [
        jax.ShapeDtypeStruct((count * span, q.shape[1]), bf16),
        jax.ShapeDtypeStruct((8, count * span), jnp.float32),
    ] + [jax.ShapeDtypeStruct((span, weight.shape[1]), bf16)] * count
    return pl.pallas_call(
        functools.partial(attend_body, pieces=pieces, shards=shards), out_shape=outs, name="attend"
    )(q, k, v, seg_col, seg_row, gate_col, weight)


def unwind_body(*refs, shards):
    eas = refs[:shards]
    q, k, v, lse, seg_col, seg_row, gate_row, w, g_out, sum_out, dk_acc, dv_acc = refs[shards:]
    span = q.shape[0] // shards
    cols = q.shape[1]
    heads = cols // HD
    weight = w[...]
    dk_acc[...] = jnp.zeros_like(dk_acc)
    dv_acc[...] = jnp.zeros_like(dv_acc)
    dq_sum = jnp.zeros((1, cols), jnp.float32)
    for p in range(shards):
        peers = partners(p, shards)
        bias = item_bias(seg_col, seg_row, p, peers, span)
        rows = slice(p * span, (p + 1) * span)
        d_ctx = (dot(eas[p][...], weight, 1, 1) * gate_row[...]).astype(jnp.bfloat16)
        parts = []
        for h in range(heads):
            cut = slice(h * HD, (h + 1) * HD)
            qp = q[rows, cut]
            do = d_ctx[:, cut]
            level = lse[h : h + 1, rows]
            probs, slopes = [], []
            for c, b in zip(peers, bias):
                ks = slice(c * span, (c + 1) * span)
                prob = jnp.exp(dot(k[ks, cut], qp, 1, 1) + (b - level))
                dv_acc[h, ks] = dv_acc[h, ks] + dot(prob.astype(jnp.bfloat16), do, 1, 0)
                probs.append(prob)
                slopes.append(dot(v[ks, cut], do, 1, 1))
            inner = functools.reduce(
                jnp.add, [jnp.sum(a * b, axis=0, keepdims=True) for a, b in zip(probs, slopes)]
            )
            dq = jnp.zeros((HD, span), jnp.float32)
            for c, a, b in zip(peers, probs, slopes):
                ks = slice(c * span, (c + 1) * span)
                ds = (a * (b - inner)).astype(jnp.bfloat16)
                dk_acc[h, ks] = dk_acc[h, ks] + dot(ds, qp, 1, 0)
                dq = dq + dot(k[ks, cut], ds, 0, 0)
            parts.append(dq)
        dq_all = jnp.concatenate(parts, axis=0).T.astype(jnp.bfloat16) * query_scale
        dq_all = dq_all.astype(jnp.bfloat16)
        g_out[rows, :cols] = dq_all
        dq_sum = dq_sum + jnp.sum(dq_all.astype(jnp.float32), axis=0, keepdims=True)
    dk = jnp.concatenate([dk_acc[h] for h in range(heads)], axis=1).astype(jnp.bfloat16)
    dv = jnp.concatenate([dv_acc[h] for h in range(heads)], axis=1).astype(jnp.bfloat16)
    g_out[:, cols:] = jnp.concatenate([dk, dv], axis=1)
    sum_out[0:1] = dq_sum
    sum_out[1:2] = jnp.sum(dv.astype(jnp.float32), axis=0, keepdims=True)


def unwind_call(eas, q, k, v, lse, seg_col, seg_row, gate_row, weight):
    rows, cols = q.shape
    return pl.pallas_call(
        functools.partial(unwind_body, shards=len(eas)),
        out_shape=[
            jax.ShapeDtypeStruct((rows, 3 * cols), jnp.bfloat16),
            jax.ShapeDtypeStruct((2, cols), jnp.float32),
        ],
        scratch_shapes=[
            pltpu.VMEM((cols // HD, rows, HD), jnp.float32),
            pltpu.VMEM((cols // HD, rows, HD), jnp.float32),
        ],
        name="unwind",
    )(*eas, q, k, v, lse, seg_col, seg_row, gate_row, weight)


def raise_body(m, w1, w2, bias, gate, h_out, slope_out, p_out):
    u = dot(m[...], w1[...], 1, 0) + bias[...]
    half = 0.5 * (1.0 + lax.erf(u * root_half))
    low = (u * half * gate[...]).astype(jnp.bfloat16)
    h_out[...] = low
    slope = half + u * jnp.exp(-0.5 * u * u) * normal_peak
    slope_out[...] = slope * gate[...]
    p_out[...] = dot(low, w2[...], 1, 0).astype(jnp.bfloat16)


def raise_call(piece, w1, w2, bias, gate):
    rows, units = piece.shape[0], w1.shape[1]
    return pl.pallas_call(
        raise_body,
        out_shape=[
            jax.ShapeDtypeStruct((rows, units), jnp.bfloat16),
            jax.ShapeDtypeStruct((rows, units), jnp.float32),
            jax.ShapeDtypeStruct(piece.shape, jnp.bfloat16),
        ],
        name="raise",
    )(piece, w1, w2, bias, gate)


def lower_body(e, w1, w2, slope, d_out, p_out, s_out):
    du = (dot(e[...], w2[...], 1, 1) * slope[...]).astype(jnp.bfloat16)
    d_out[...] = du
    p_out[...] = dot(du, w1[...], 1, 1).astype(jnp.bfloat16)
    s_out[...] = jnp.sum(du.astype(jnp.float32), axis=0, keepdims=True)


def lower_call(piece, w1, w2, slope):
    rows, units = slope.shape
    return pl.pallas_call(
        lower_body,
        out_shape=[
            jax.ShapeDtypeStruct((rows, units), jnp.bfloat16),
            jax.ShapeDtypeStruct(piece.shape, jnp.bfloat16),
            jax.ShapeDtypeStruct((1, units), jnp.float32),
        ],
        name="lower",
    )(piece, w1, w2, slope)


def pack_row(grad, put, block):
    for i in range(grad.shape[0] // BLK):
        for side in range(2):
            at = i * BLK + side * QUART
            top = grad[at : at + QUART, :].astype(jnp.bfloat16)
            low = grad[at + HALF : at + HALF + QUART, :].astype(jnp.bfloat16)
            for j in range(grad.shape[1] // BLK):
                cut = slice(j * BLK, (j + 1) * BLK)
                put(
                    side,
                    block + i * (grad.shape[1] // BLK) + j,
                    jnp.concatenate([top[:, cut], low[:, cut]], axis=1),
                )


def inner_body(*refs, shards):
    groups = [refs[i * shards : (i + 1) * shards] for i in range(4)]
    outs = refs[4 * shards :]

    def put(side, block, value):
        outs[side][block] = value

    block = 0
    for left, right in ((groups[0], groups[1]), (groups[2], groups[3])):
        grad = functools.reduce(
            jnp.add, [dot(a[...], b[...], 0, 0) for a, b in zip(left, right)]
        )
        pack_row(grad, put, block)
        block += grad.shape[0] * grad.shape[1] // (BLK * BLK)


def inner_call(mids, d_raised, hidden, branch):
    shards = len(mids)
    blocks = 2 * mids[0].shape[1] * hidden[0].shape[1] // (BLK * BLK)
    out = jax.ShapeDtypeStruct((blocks, QUART, 2 * BLK), jnp.bfloat16)
    return pl.pallas_call(
        functools.partial(inner_body, shards=shards), out_shape=[out, out], name="inner"
    )(*mids, *d_raised, *hidden, *branch)


def outer_body(pos_a, pos_b, *refs, shards, blocks):
    xs, eas = refs[:shards], refs[shards : 2 * shards]
    cg, g, ffn_a, ffn_b = refs[2 * shards : 2 * shards + 4]
    outs = refs[2 * shards + 4 : 2 * shards + 8]
    bufs, sems = refs[2 * shards + 8 : 2 * shards + 10], refs[2 * shards + 10]
    poses = (pos_a, pos_b)
    span = xs[0].shape[0]
    total = bufs[0].shape[0]
    if total > blocks:
        for buf in bufs:
            buf[...] = jnp.zeros_like(buf)

    def put(side, block, value):
        bufs[side][poses[side][block]] = value

    first = blocks - ffn_a.shape[0]
    for side, src in enumerate((ffn_a, ffn_b)):
        for b in range(ffn_a.shape[0]):
            put(side, first + b, src[b])
    cut = [slice(s * span, (s + 1) * span) for s in range(shards)]
    grad = functools.reduce(jnp.add, [dot(x[...], g[c], 0, 0) for x, c in zip(xs, cut)])
    pack_row(grad, put, 0)
    block = grad.shape[0] * grad.shape[1] // (BLK * BLK)
    grad = functools.reduce(jnp.add, [dot(cg[c], e[...], 0, 0) for e, c in zip(eas, cut)])
    pack_row(grad, put, block)
    half = total // 2
    copies = []
    for side in range(2):
        for part in (1, 0):
            copy = pltpu.make_async_copy(
                bufs[side].at[pl.ds(part * half, half)], outs[2 * side + part], sems.at[side, part]
            )
            copy.start()
            copies.append(copy)
    for copy in copies:
        copy.wait()


def outer_call(pos_a, pos_b, xs, eas, cg, g, ffn_a, ffn_b, total):
    shards = len(xs)
    blocks = (xs[0].shape[1] * g.shape[1] + cg.shape[1] * eas[0].shape[1]) // (BLK * BLK)
    blocks += ffn_a.shape[0]
    part = jax.ShapeDtypeStruct((total // 2, QUART, 2 * BLK), jnp.bfloat16)
    buf = pltpu.VMEM((total, QUART, 2 * BLK), jnp.bfloat16)
    return pl.pallas_call(
        functools.partial(outer_body, shards=shards, blocks=blocks),
        in_specs=[pl.BlockSpec(memory_space=pltpu.SMEM)] * 2
        + [pl.BlockSpec(memory_space=pltpu.VMEM)] * (2 * shards + 4),
        out_specs=[pl.BlockSpec(memory_space=pl.ANY)] * 4,
        out_shape=[part] * 4,
        scratch_shapes=[buf, buf, pltpu.SemaphoreType.DMA((2, 2))],
        name="outer",
    )(pos_a, pos_b, *xs, *eas, cg, g, ffn_a, ffn_b)


def adam_moments(gradient, first_moment, second_moment, count_now):
    first_moment = beta_one * first_moment + (1.0 - beta_one) * gradient
    second_moment = beta_two * second_moment + (1.0 - beta_two) * gradient * gradient
    scaled = (
        first_moment
        / (1.0 - beta_one**count_now)
        / (jnp.sqrt(second_moment / (1.0 - beta_two**count_now)) + adam_eps)
    )
    return (first_moment, second_moment, scaled)


def bit_pairs(bit, size):
    return [(i, i ^ (1 << bit)) for i in range(size)]


def bit_count(size):
    return size.bit_length() - 1


def second_order(bits):
    return ([bits[1], bits[0]] + bits[2:]) if len(bits) > 1 else bits


def cast_body(w_ref, a_out, b_out, scratch):
    m = read_square(w_ref, (0,), scratch, 3, 0)
    packed = jnp.concatenate([m[:HALF], m[HALF:]], axis=1).astype(jnp.bfloat16)
    a_out[0] = packed[:QUART]
    b_out[0] = packed[QUART:]


def cast_call(flat):
    n = flat.shape[0]
    piece = jax.ShapeDtypeStruct((n, QUART, 2 * BLK), jnp.bfloat16)
    spec = pl.BlockSpec((1, QUART, 2 * BLK), lambda i: (i, 0, 0))
    return pl.pallas_call(
        cast_body,
        grid=(n,),
        in_specs=[pl.BlockSpec((1, FLAT, 128), lambda i: (i, 0, 0))],
        out_specs=[spec, spec],
        out_shape=[piece, piece],
        scratch_shapes=[pltpu.VMEM((2, BLK, 128), jnp.float32)],
        name="cast",
    )(flat)


def spread(block, order, size):
    pieces = [block[None]]
    rel = [[0]]
    for bit in order:
        moved = [lax.ppermute(p, "dp", bit_pairs(bit, size)) for p in pieces]
        rel = rel + [[r ^ (1 << bit) for r in group] for group in rel]
        pieces = pieces + moved
        if size > 8:
            pieces = [jnp.concatenate(pieces)]
            rel = [sum(rel, [])]
    return pieces, sum(rel, [])


def build_body(pos_a, pos_b, *refs, count):
    ins_a, ins_b = refs[:count], refs[count : 2 * count]
    outs = refs[2 * count : 2 * count + 4]
    buf_a, buf_b, sems = refs[2 * count + 4 :]
    copies = []
    for side, (ins, buf) in enumerate(((ins_a, buf_a), (ins_b, buf_b))):
        at = 0
        for i, src in enumerate(ins):
            m = src.shape[0]
            copy = pltpu.make_async_copy(src, buf.at[pl.ds(at, m)], sems.at[side, i])
            copy.start()
            copies.append(copy)
            at += m
    for copy in copies:
        copy.wait()
    base = 0
    for out in outs:
        rows, cols = out.shape[0] // BLK, out.shape[1] // BLK
        for i in range(rows):
            for side, (buf, pos) in enumerate(((buf_a, pos_a), (buf_b, pos_b))):
                got = [buf[pos[base + i * cols + j]] for j in range(cols)]
                at = i * BLK + side * QUART
                out[at : at + QUART, :] = jnp.concatenate([g[:, :BLK] for g in got], axis=1)
                at += HALF
                out[at : at + QUART, :] = jnp.concatenate([g[:, BLK:] for g in got], axis=1)
        base += rows * cols


def build_call(pos_a, pos_b, pieces_a, pieces_b, shapes):
    flat_a = [p.reshape(-1, QUART, 2 * BLK) for p in pieces_a]
    flat_b = [p.reshape(-1, QUART, 2 * BLK) for p in pieces_b]
    count = len(flat_a)
    total = sum(p.shape[0] for p in flat_a)
    bf16 = jnp.bfloat16
    kernel = functools.partial(build_body, count=count)
    return pl.pallas_call(
        kernel,
        in_specs=[pl.BlockSpec(memory_space=pltpu.SMEM)] * 2
        + [pl.BlockSpec(memory_space=pl.ANY)] * (2 * count),
        out_shape=[jax.ShapeDtypeStruct(s, bf16) for s in shapes],
        scratch_shapes=[
            pltpu.VMEM((total, QUART, 2 * BLK), bf16),
            pltpu.VMEM((total, QUART, 2 * BLK), bf16),
            pltpu.SemaphoreType.DMA((2, count)),
        ],
        name="build",
    )(pos_a, pos_b, *flat_a, *flat_b)


def fold(keep, send, order, size):
    for step, bit in enumerate(order):
        got = lax.ppermute(send, "dp", bit_pairs(bit, size))
        if step == len(order) - 1:
            return keep, got
        half = keep.shape[0] // 2
        cur = (keep.astype(jnp.float32) + got.astype(jnp.float32)).astype(jnp.bfloat16)
        keep, send = cur[:half], cur[half:]


def fold_position(owner, slot, order, slots, me):
    rel = owner ^ me
    index = jnp.zeros_like(rel)
    for bit in order:
        index = index * 2 + ((rel >> bit) & 1)
    return index * slots + slot


def butterfly(value, axis, size):
    for bit in range(bit_count(size)):
        value = value + lax.ppermute(value, axis, bit_pairs(bit, size))
    return value


def swap(piece, s, shards):
    return lax.ppermute(piece, "tensor", [(i, i ^ s) for i in range(shards)])


def shift(piece, pairs):
    return lax.ppermute(piece, "tensor", pairs)


def gather_rows(rows, shards):
    if shards != 4:
        return [rows] + [swap(rows, s, shards) for s in range(1, shards)]
    two = swap(rows, 2, shards)
    one = swap(rows, 1, shards)
    relay = shift(two, [(2, 3), (1, 0)])
    inner = shift(rows, [(1, 2), (2, 1)])
    return [rows, one, two, inner + relay]


def scatter_rows(pieces, shards, relayed=False):
    if relayed and shards == 4:
        relay = shift(pieces[3], [(0, 1), (3, 2)])
        far = (pieces[2].astype(jnp.float32) + relay.astype(jnp.float32)).astype(jnp.bfloat16)
        others = [
            swap(far, 2, shards),
            swap(pieces[1], 1, shards),
            shift(pieces[3], [(1, 2), (2, 1)]),
        ]
    else:
        others = [swap(pieces[s], s, shards) for s in range(1, shards)]
    total = pieces[0].astype(jnp.float32)
    for piece in others:
        total = total + piece.astype(jnp.float32)
    return total


def body(
    tokens,
    cotangent,
    segments,
    gates_local,
    gates_shared,
    gate_logits,
    shared_logits,
    masters,
    moment_one,
    moment_two,
    block_bases,
    block_stats,
    unit_params,
    unit_first,
    unit_second,
    norm_params,
    norm_first,
    norm_second,
    slot_ids,
    step_count,
):
    shards = lax.axis_size("tensor")
    owners = lax.axis_size("dp")
    head_count = H // shards
    head_cols = head_count * HD
    unit_count = FF // shards
    slot_count = masters.shape[1]
    me = lax.axis_index("dp")
    place = lax.axis_index("tensor")
    bits = list(range(bit_count(owners)))
    head_keep = keep_prob(gate_logits[0, :head_count])
    unit_keep = keep_prob(gate_logits[0, head_count:])
    shared_keep = keep_prob(shared_logits)
    keep_row = jnp.zeros((1, D), jnp.float32)
    keep_row = keep_row.at[0, 0].set(jnp.sum(head_keep)).at[0, 1].set(jnp.sum(unit_keep))
    flat_view = (slot_count, FLAT, 128)
    cast_a, cast_b = cast_call(masters.reshape(flat_view))
    order_a = bits[1:] + bits[:1]
    order_b = second_order(bits[1:]) + bits[:1]
    tokens, cast_a = lax.optimization_barrier((tokens, cast_a))
    pieces_a, rel_a = spread(cast_a, order_a, owners)
    pieces_b, rel_b = spread(cast_b, order_b, owners)
    owner_of = slot_ids // slot_count
    slot_of = slot_ids % slot_count
    rel_of = owner_of ^ me

    def piece_spot(rel_list):
        table = [0] * owners
        for spot, rel in enumerate(rel_list):
            table[rel] = spot
        return jnp.asarray(table, jnp.int32)[rel_of] * slot_count + slot_of

    qkv_weight, out_weight, up_weight, down_weight = build_call(
        piece_spot(rel_a),
        piece_spot(rel_b),
        pieces_a,
        pieces_b,
        ((D, 3 * head_cols), (head_cols, D), (D, unit_count), (unit_count, D)),
    )
    unit_low = unit_params.astype(jnp.bfloat16)
    unit_pieces, _ = spread(unit_low[0], bits, owners)
    unit_all = jnp.concatenate(unit_pieces, axis=0)
    unit_bias = unit_all[jnp.arange(owners) ^ me].reshape(-1).astype(jnp.float32)
    head_gate = gates_local[0, :head_count]
    unit_gate = gates_local[0, head_count:]
    keeper = gates_shared[:D]
    mha_gate = gates_shared[D]
    ffn_gate = gates_shared[D + 1]
    gain_one = norm_params[0]
    shift_one = norm_params[1]
    bias_attn = norm_params[2]
    gain_two = norm_params[3]
    shift_two = norm_params[4]
    bias_ffn = norm_params[5]
    token_pieces = gather_rows(tokens, shards)
    span = LEN // shards
    parts = segments.reshape(shards, span)
    turned_row = parts[jnp.arange(shards) ^ place].reshape(1, LEN)
    turned_col = turned_row.reshape(LEN, 1)
    queries, key_rows, value_rows = project_call(
        token_pieces, qkv_weight, unit_bias[: 2 * head_cols].reshape(2, head_cols)
    )
    gate_row = jnp.repeat(head_gate, HD).reshape(1, head_cols)
    gated_ctx, level, *partial = attend_call(
        queries,
        key_rows,
        value_rows,
        turned_col,
        turned_row,
        gate_row.reshape(head_cols, 1),
        out_weight,
        tuple(range(shards)),
        shards,
    )
    attn_sum = scatter_rows(partial, shards, True)
    residual = tokens.astype(jnp.float32)
    hidden_one = residual + mha_gate * (attn_sum + bias_attn)
    middle, normed_one, inverse_one = norm_forward(hidden_one, gain_one, shift_one, keeper)
    middle_pieces = gather_rows(middle.astype(jnp.bfloat16), shards)
    up_bias = unit_bias[2 * head_cols :].reshape(1, unit_count)
    gate_units = unit_gate.reshape(1, unit_count)
    raised = [
        raise_call(piece, up_weight, down_weight, up_bias, gate_units) for piece in middle_pieces
    ]
    ffn_sum = scatter_rows([r[2] for r in raised], shards)
    hidden_two = middle + ffn_gate * (ffn_sum + bias_ffn)
    layer_out, normed_two, inverse_two = norm_forward(hidden_two, gain_two, shift_two, keeper)
    upstream = cotangent.astype(jnp.float32)
    grad_two, d_gain_two, d_shift_two = norm_backward(
        upstream, normed_two, inverse_two, gain_two, keeper
    )
    d_bias_ffn = ffn_gate * jnp.sum(grad_two, axis=0)
    branch_low = (ffn_gate * grad_two).astype(jnp.bfloat16)
    branch_pieces = gather_rows(branch_low, shards)
    lowered = [
        lower_call(piece, up_weight, down_weight, r[1]) for piece, r in zip(branch_pieces, raised)
    ]
    d_up_bias = functools.reduce(jnp.add, [part[2][0] for part in lowered])
    grad_middle = grad_two + scatter_rows([part[1] for part in lowered], shards)
    grad_one, d_gain_one, d_shift_one = norm_backward(
        grad_middle, normed_one, inverse_one, gain_one, keeper
    )
    d_bias_attn = mha_gate * jnp.sum(grad_one, axis=0)
    attn_low = (mha_gate * grad_one).astype(jnp.bfloat16)
    attn_pieces = gather_rows(attn_low, shards)
    ffn_a, ffn_b = inner_call(
        middle_pieces, [part[0] for part in lowered], [r[0] for r in raised], branch_pieces
    )
    d_qkv, head_sums = unwind_call(
        attn_pieces,
        queries,
        key_rows,
        value_rows,
        level,
        turned_col,
        turned_row,
        gate_row,
        out_weight,
    )
    d_units = jnp.concatenate([head_sums[0], head_sums[1], d_up_bias])
    fold_a = bits
    fold_b = bits[:1] + second_order(bits[1:])
    keep_a, send_a, keep_b, send_b = outer_call(
        fold_position(owner_of, slot_of, fold_a, slot_count, me),
        fold_position(owner_of, slot_of, fold_b, slot_count, me),
        token_pieces,
        attn_pieces,
        gated_ctx,
        d_qkv,
        ffn_a,
        ffn_b,
        owners * slot_count,
    )
    norm_local = jnp.concatenate(
        [
            jnp.stack([d_gain_one, d_shift_one, d_bias_attn, d_gain_two, d_shift_two, d_bias_ffn]),
            keep_row,
        ]
    )
    small = jnp.concatenate([norm_local.reshape(-1), d_units]).reshape(-1, 128)
    small, send_a = lax.optimization_barrier((small, send_a))
    keep_a, got_a = fold(keep_a, send_a, fold_a, owners)
    keep_b, got_b = fold(keep_b, send_b, fold_b, owners)
    small = butterfly(small, "dp", owners)
    norm_rows = norm_local.size // 128
    share = unit_params.shape[1]
    unit_grad = lax.dynamic_slice(small[norm_rows:].reshape(-1), (me * share,), (share,))
    token_part = jnp.einsum(
        "rc,dc->rd", d_qkv, qkv_weight, preferred_element_type=jnp.float32
    ).astype(jnp.bfloat16)
    token_part = [token_part[s * span : (s + 1) * span] for s in range(shards)]
    token_part, got_a, got_b, small = lax.optimization_barrier((token_part, got_a, got_b, small))
    token_far = [swap(token_part[s], s, shards) for s in range(1, shards)]
    summed = small[:norm_rows]
    for bit in range(bit_count(shards)):
        summed = summed + swap(summed, 1 << bit, shards)
    summed = summed.reshape(-1, D)
    norm_grads = summed[:6]
    keep_sums = summed[6, :2] * (1.0 / owners)
    count_now = step_count[0].astype(jnp.float32)

    def pair_view(x):
        x = x.reshape(slot_count, 2, FLAT, 128)
        return x.transpose(0, 2, 1, 3).reshape(slot_count, 2 * FLAT, 128)

    def pair_back(x):
        x = x.reshape(slot_count, FLAT, 2, 128).transpose(0, 2, 1, 3)
        return x.reshape(1, slot_count, 2, BLK * BLK)

    correction = (1.0 / (1.0 - beta_one**count_now)).reshape(1, 1)
    owned, masters_new, moment_one_new, moment_two_new, stats_new, turned = soap_call(
        correction,
        keep_a,
        got_a,
        keep_b,
        got_b,
        masters.reshape(flat_view),
        moment_one.reshape(flat_view),
        moment_two.reshape(flat_view),
        pair_view(block_bases),
        pair_view(block_stats),
    )
    bases_new = orth_call(turned)
    bases_new, token_far = lax.optimization_barrier((bases_new, token_far))
    token_grad = grad_one + token_part[0].astype(jnp.float32)
    for far in token_far:
        token_grad = token_grad + far.astype(jnp.float32)
    flat_shape = (1, slot_count, BLK * BLK)
    unit_first_new, unit_second_new, unit_scaled = adam_moments(
        unit_grad, unit_first[0], unit_second[0], count_now
    )
    norm_first_new, norm_second_new, norm_scaled = adam_moments(
        norm_grads, norm_first, norm_second, count_now
    )
    hidden_sum = jnp.sum(shared_keep[:D])
    param_count = 1e-06 * (
        shared_keep[D] * keep_sums[0] * (4 * HD) * hidden_sum
        + shared_keep[D + 1] * keep_sums[1] * 2 * hidden_sum
    )
    return (
        layer_out.astype(jnp.bfloat16),
        token_grad,
        owned.reshape(flat_shape),
        masters_new.reshape(flat_shape),
        moment_one_new.reshape(flat_shape),
        moment_two_new.reshape(flat_shape),
        pair_back(bases_new),
        pair_back(stats_new),
        (unit_params[0] - rate_vector * unit_scaled)[None],
        unit_first_new[None],
        unit_second_new[None],
        norm_grads,
        norm_params - rate_vector * norm_scaled,
        norm_first_new,
        norm_second_new,
        param_count.reshape(1),
    )


def solution(mesh):
    placed = (
        P(("dp", "tensor"), None),
        P(("dp", "tensor"), None),
        P("dp", None),
        P("tensor", None),
        P(),
        P("tensor", None),
        P(),
        P("tensor", "dp", None),
        P("tensor", "dp", None),
        P("tensor", "dp", None),
        P("tensor", "dp", None, None),
        P("tensor", "dp", None, None),
        P("tensor", "dp"),
        P("tensor", "dp"),
        P("tensor", "dp"),
        P(),
        P(),
        P(),
        P(),
        P(),
    )
    return jax.shard_map(
        body,
        mesh=mesh,
        in_specs=placed,
        out_specs=(
            P(("dp", "tensor"), None),
            P(("dp", "tensor"), None),
            P("tensor", "dp", None),
            P("tensor", "dp", None),
            P("tensor", "dp", None),
            P("tensor", "dp", None),
            P("tensor", "dp", None, None),
            P("tensor", "dp", None, None),
            P("tensor", "dp"),
            P("tensor", "dp"),
            P("tensor", "dp"),
            P(),
            P(),
            P(),
            P(),
            P(),
        ),
        check_vma=False,
    )
```

```python
import math
import functools
import jax
import jax.numpy as jnp
from jax import lax
from jax.sharding import PartitionSpec as P
from jax.experimental import pallas as pl
from jax.experimental.pallas import tpu as pltpu

BLK = 192
HALF = 96
QUART = 48
FLAT = 288
PAN = 64
beta_one = 0.95
beta_two = 0.95
beta_stat = 0.95
adam_eps = 1e-08
rate_matrix = 0.1
HIGH = lax.Precision.HIGH
EXACT = lax.Precision.HIGHEST


def mm(a, b, da, db, precision):
    return lax.dot_general(
        a, b, (((da,), (db,)), ((), ())), precision=precision, preferred_element_type=jnp.float32
    )


def read_square(src, lead, scratch, stride, first):
    def rows(q):
        return src[lead + (pl.ds(first + q * (stride // 3), HALF, stride=stride), slice(None))]

    a, b, c = rows(0), rows(1), rows(2)
    scratch[0, pl.ds(0, HALF, stride=2), :] = a
    scratch[1, pl.ds(0, HALF, stride=2), :] = b
    scratch[0, pl.ds(1, HALF, stride=2), :] = jnp.concatenate([b[:, 64:], c[:, :64]], axis=1)
    scratch[1, pl.ds(1, HALF, stride=2), :] = jnp.concatenate([c[:, 64:], c[:, 64:]], axis=1)
    return jnp.concatenate([scratch[0], scratch[1, :, :64]], axis=1)


def write_square(value, dst, lead, scratch, stride, first):
    scratch[0] = value[:, :128]
    scratch[1, :, :64] = value[:, 128:]
    e0 = scratch[0, pl.ds(0, HALF, stride=2), :]
    e1 = scratch[1, pl.ds(0, HALF, stride=2), :]
    o0 = scratch[0, pl.ds(1, HALF, stride=2), :]
    o1 = scratch[1, pl.ds(1, HALF, stride=2), :]
    step = stride // 3
    dst[lead + (pl.ds(first, HALF, stride=stride), slice(None))] = e0
    dst[lead + (pl.ds(first + step, HALF, stride=stride), slice(None))] = jnp.concatenate(
        [e1[:, :64], o0[:, :64]], axis=1
    )
    dst[lead + (pl.ds(first + 2 * step, HALF, stride=stride), slice(None))] = jnp.concatenate(
        [o0[:, 64:], o1[:, :64]], axis=1
    )


def soap_body(
    scale_ref, ka, ra, kb, rb, w_ref, m1_ref, m2_ref, b_ref, s_ref,
    g_out, w_out, m1_out, m2_out, s_out, mt_out, *scr,
):
    scratch = list(scr)
    ga = ka[0].astype(jnp.float32) + ra[0].astype(jnp.float32)
    gb = kb[0].astype(jnp.float32) + rb[0].astype(jnp.float32)
    g = jnp.concatenate([ga[:, :BLK], gb[:, :BLK], ga[:, BLK:], gb[:, BLK:]], axis=0)
    write_square(g, g_out, (0,), scratch[0], 3, 0)
    ql = read_square(b_ref, (0,), scratch[1], 6, 0)
    qr = read_square(b_ref, (0,), scratch[2], 6, 1)
    t3 = mm(g, qr, 1, 0, HIGH)
    r = mm(ql, t3, 0, 0, HIGH)
    rs, as_ = scratch[3], scratch[4]
    write_square(r, m1_out, (0,), rs, 3, 0)
    flat = m1_out[0]
    m1 = beta_one * m1_ref[0] + (1.0 - beta_one) * flat
    m2 = beta_two * m2_ref[0] + (1.0 - beta_two) * flat * flat
    m1_out[0] = m1
    m2_out[0] = m2
    corr = scale_ref[0, 0]
    w_out[0] = (m1 * corr) / (jnp.sqrt(m2 * corr) + adam_eps)
    a = read_square(w_out, (0,), as_, 3, 0)
    restored = mm(mm(ql, a, 1, 0, HIGH), qr, 1, 1, HIGH)
    write_square(restored, w_out, (0,), rs, 3, 0)
    w_out[0] = w_ref[0] - rate_matrix * w_out[0]
    sl = read_square(s_ref, (0,), scratch[5], 6, 0)
    sl = beta_stat * sl + (1.0 - beta_stat) * mm(g, g, 1, 1, HIGH)
    write_square(sl, s_out, (0,), scratch[6], 6, 0)
    mt_out[0, 0] = mm(ql, sl, 0, 0, EXACT)
    sr = read_square(s_ref, (0,), scratch[7], 6, 1)
    sr = beta_stat * sr + (1.0 - beta_stat) * mm(g, g, 0, 0, HIGH)
    write_square(sr, s_out, (0,), scratch[6], 6, 1)
    mt_out[0, 1] = mm(qr, sr, 0, 0, EXACT)


def soap_call(scale, ka, ra, kb, rb, w, m1, m2, b, s):
    n = w.shape[0]
    f32 = jnp.float32

    def spec(shape):
        zeros = (0,) * (len(shape) - 1)
        return pl.BlockSpec((1,) + shape[1:], lambda i: (i,) + zeros)

    ins = [ka, ra, kb, rb, w, m1, m2, b, s]
    outs = [
        jax.ShapeDtypeStruct((n, FLAT, 128), f32),
        jax.ShapeDtypeStruct((n, FLAT, 128), f32),
        jax.ShapeDtypeStruct((n, FLAT, 128), f32),
        jax.ShapeDtypeStruct((n, FLAT, 128), f32),
        jax.ShapeDtypeStruct((n, 2 * FLAT, 128), f32),
        jax.ShapeDtypeStruct((n, 2, BLK, BLK), f32),
    ]
    return pl.pallas_call(
        soap_body,
        grid=(n,),
        in_specs=[pl.BlockSpec(memory_space=pltpu.SMEM)] + [spec(x.shape) for x in ins],
        out_specs=[spec(o.shape) for o in outs],
        out_shape=outs,
        scratch_shapes=[pltpu.VMEM((2, BLK, 128), f32)] * 8,
        name="soap",
    )(scale, *ins)


def orth_body(mt_ref, q_out, xa, xs, sq):
    n = mt_ref.shape[0] * 2
    for i in range(n):
        m = mt_ref[i // 2, i % 2]
        xa[i, :, 256 : 256 + BLK] = m
        xa[i, :, 0:BLK] = mm(m, m, 1, 1, EXACT)
    lane = lax.broadcasted_iota(jnp.int32, (1, 1, 2 * PAN), 2)
    eye = (
        lax.broadcasted_iota(jnp.int32, (n, PAN, PAN), 1)
        == lax.broadcasted_iota(jnp.int32, (n, PAN, PAN), 2)
    ).astype(jnp.float32)

    def pick(v, j):
        return jnp.sum(jnp.where(lane == j, v, 0.0), axis=2, keepdims=True)

    for k in range(BLK // PAN):
        lo, hi = k * PAN, (k + 1) * PAN
        xs[...] = jnp.concatenate([xa[:, lo:hi, lo:hi], eye], axis=2)
        for first in range(0, PAN, 8):
            row_id = lax.broadcasted_iota(jnp.int32, (1, PAN - first, 1), 1) + first

            def step(s, carry):
                x = xs[:, first:, :]
                j = first + 2 * s
                r0 = xs[:, pl.ds(j, 1), :]
                r1 = xs[:, pl.ds(j + 1, 1), :]
                c0, c1 = pick(x, j), pick(x, j + 1)
                p, q, d = pick(r0, j), pick(r0, j + 1), pick(r1, j + 1)
                ip = 1.0 / p
                e = q * ip
                r1 = r1 - e * r0
                ip1 = 1.0 / (d - e * q)
                f0 = c0 * ip
                f1 = (c1 - f0 * q) * ip1
                f0 = jnp.where(row_id > j, f0, 0.0)
                f1 = jnp.where(row_id > j + 1, f1, 0.0)
                xs[:, first:, :] = x - (f0 * r0 + f1 * r1)
                return carry

            lax.fori_loop(0, 4, step, 0)
        x = xs[...]
        row_id = lax.broadcasted_iota(jnp.int32, (1, PAN, 1), 1)
        diag = jnp.sum(jnp.where(lane == row_id, x, 0.0), axis=2, keepdims=True)
        t = x[:, :, PAN:] * lax.rsqrt(diag)
        for i in range(n):
            w = mm(t[i], xa[i, lo:hi, :], 1, 0, EXACT)
            xa[i, lo:hi, :] = w
            if hi < BLK:
                wt = w[:, :256].T[hi:BLK]
                xa[i, hi:, :] = xa[i, hi:, :] - mm(wt, w, 1, 0, EXACT)
    for i in range(n):
        write_square(xa[i, :, 256:].T[:BLK], q_out, (i // 2,), sq, 6, i % 2)


def orth_call(mt):
    n = mt.shape[0]
    f32 = jnp.float32
    return pl.pallas_call(
        orth_body,
        out_shape=jax.ShapeDtypeStruct((n, 2 * FLAT, 128), f32),
        scratch_shapes=[
            pltpu.VMEM((2 * n, BLK, 512), f32),
            pltpu.VMEM((2 * n, PAN, 2 * PAN), f32),
            pltpu.VMEM((2, BLK, 128), f32),
        ],
        name="orth",
    )(mt)


D = 768
H = 12
FF = 3072
HD = 64
LEN = 1024
norm_eps = 1e-12
rate_vector = 0.25
query_scale = 0.125
stretch_shift = 2.0 / 3.0 * math.log(0.1 / 1.1)
root_half = 1.0 / math.sqrt(2.0)
normal_peak = 1.0 / math.sqrt(2.0 * math.pi)


def keep_prob(logits):
    return jax.nn.sigmoid(logits - stretch_shift)


def norm_forward(hidden, gain_row, shift_row, keeper):
    row_mean = jnp.mean(hidden, axis=-1, keepdims=True)
    centred = hidden - row_mean
    variance = jnp.mean(centred * centred, axis=-1, keepdims=True)
    inverse = lax.rsqrt(variance + norm_eps)
    normed = centred * inverse
    return (keeper * (normed * gain_row + shift_row), normed, inverse)


def norm_backward(incoming, normed, inverse, gain_row, keeper):
    scaled = incoming * keeper
    d_gain = jnp.sum(scaled * normed, axis=0)
    d_shift = jnp.sum(scaled, axis=0)
    d_normed = scaled * gain_row
    d_input = inverse * (
        d_normed
        - jnp.mean(d_normed, axis=-1, keepdims=True)
        - normed * jnp.mean(d_normed * normed, axis=-1, keepdims=True)
    )
    return (d_input, d_gain, d_shift)


def project_body(*refs):
    xs, (w, bias, q_out, k_out, v_out) = refs[:-5], refs[-5:]
    weight = w[...]
    for s, x in enumerate(xs):
        rows = slice(s * x.shape[0], (s + 1) * x.shape[0])
        out = dot(x[...], weight, 1, 0)
        cols = q_out.shape[1]
        q_out[rows] = ((out[:, :cols] + bias[0:1]) * query_scale).astype(jnp.bfloat16)
        k_out[rows] = out[:, cols : 2 * cols].astype(jnp.bfloat16)
        v_out[rows] = (out[:, 2 * cols :] + bias[1:2]).astype(jnp.bfloat16)


def project_call(pieces, weight, bias):
    rows = sum(p.shape[0] for p in pieces)
    out = jax.ShapeDtypeStruct((rows, bias.shape[1]), jnp.bfloat16)
    return pl.pallas_call(project_body, out_shape=[out] * 3, name="project")(
        *pieces, weight, bias
    )


def dot(a, b, da, db):
    return lax.dot_general(
        a, b, (((da,), (db,)), ((), ())), preferred_element_type=jnp.float32
    )


def partners(piece, shards):
    return [piece ^ s for s in range(shards) if s != 2]


def item_bias(seg_col, seg_row, piece, peers, span):
    mine = seg_row[0:1, piece * span : (piece + 1) * span]
    return [
        jnp.where(seg_col[c * span : (c + 1) * span, :] == mine, 0.0, -1e30) for c in peers
    ]


def attend_body(q, k, v, seg_col, seg_row, gate_col, w, *outs, pieces, shards):
    span = q.shape[0] // shards
    cg_out, lse_out = outs[0], outs[1]
    heads = q.shape[1] // HD
    weight = w[...]
    lse_out[...] = jnp.zeros_like(lse_out)
    for at, p in enumerate(pieces):
        peers = partners(p, shards)
        bias = item_bias(seg_col, seg_row, p, peers, span)
        rows = slice(p * span, (p + 1) * span)
        mine = slice(at * span, (at + 1) * span)
        parts = []
        for h in range(heads):
            cut = slice(h * HD, (h + 1) * HD)
            qp = q[rows, cut]
            scores = [
                dot(k[c * span : (c + 1) * span, cut], qp, 1, 1) + b for c, b in zip(peers, bias)
            ]
            top = functools.reduce(jnp.maximum, [jnp.max(s, axis=0, keepdims=True) for s in scores])
            powers = [jnp.exp(s - top) for s in scores]
            total = functools.reduce(
                jnp.add, [jnp.sum(e, axis=0, keepdims=True) for e in powers]
            )
            inverse = 1.0 / total
            context = functools.reduce(
                jnp.add,
                [
                    dot(
                        v[c * span : (c + 1) * span, cut],
                        (e * inverse).astype(jnp.bfloat16),
                        0,
                        0,
                    )
                    for c, e in zip(peers, powers)
                ],
            )
            parts.append(context)
            lse_out[h : h + 1, mine] = top + jnp.log(total)
        gated = (jnp.concatenate(parts, axis=0) * gate_col[...]).T.astype(jnp.bfloat16)
        cg_out[mine] = gated
        outs[2 + at][...] = dot(gated, weight, 1, 0).astype(jnp.bfloat16)


def attend_call(q, k, v, seg_col, seg_row, gate_col, weight, pieces, shards):
    span = q.shape[0] // shards
    bf16 = jnp.bfloat16
    count = len(pieces)
    outs = [
        jax.ShapeDtypeStruct((count * span, q.shape[1]), bf16),
        jax.ShapeDtypeStruct((8, count * span), jnp.float32),
    ] + [jax.ShapeDtypeStruct((span, weight.shape[1]), bf16)] * count
    return pl.pallas_call(
        functools.partial(attend_body, pieces=pieces, shards=shards), out_shape=outs, name="attend"
    )(q, k, v, seg_col, seg_row, gate_col, weight)


def unwind_body(*refs, shards):
    eas = refs[:shards]
    q, k, v, lse, seg_col, seg_row, gate_row, w, g_out, sum_out, dk_acc, dv_acc = refs[shards:]
    span = q.shape[0] // shards
    cols = q.shape[1]
    heads = cols // HD
    weight = w[...]
    dk_acc[...] = jnp.zeros_like(dk_acc)
    dv_acc[...] = jnp.zeros_like(dv_acc)
    dq_sum = jnp.zeros((1, cols), jnp.float32)
    for p in range(shards):
        peers = partners(p, shards)
        bias = item_bias(seg_col, seg_row, p, peers, span)
        rows = slice(p * span, (p + 1) * span)
        d_ctx = (dot(eas[p][...], weight, 1, 1) * gate_row[...]).astype(jnp.bfloat16)
        parts = []
        for h in range(heads):
            cut = slice(h * HD, (h + 1) * HD)
            qp = q[rows, cut]
            do = d_ctx[:, cut]
            level = lse[h : h + 1, rows]
            probs, slopes = [], []
            for c, b in zip(peers, bias):
                ks = slice(c * span, (c + 1) * span)
                prob = jnp.exp(dot(k[ks, cut], qp, 1, 1) + (b - level))
                dv_acc[h, ks] = dv_acc[h, ks] + dot(prob.astype(jnp.bfloat16), do, 1, 0)
                probs.append(prob)
                slopes.append(dot(v[ks, cut], do, 1, 1))
            inner = functools.reduce(
                jnp.add, [jnp.sum(a * b, axis=0, keepdims=True) for a, b in zip(probs, slopes)]
            )
            dq = jnp.zeros((HD, span), jnp.float32)
            for c, a, b in zip(peers, probs, slopes):
                ks = slice(c * span, (c + 1) * span)
                ds = (a * (b - inner)).astype(jnp.bfloat16)
                dk_acc[h, ks] = dk_acc[h, ks] + dot(ds, qp, 1, 0)
                dq = dq + dot(k[ks, cut], ds, 0, 0)
            parts.append(dq)
        dq_all = jnp.concatenate(parts, axis=0).T.astype(jnp.bfloat16) * query_scale
        dq_all = dq_all.astype(jnp.bfloat16)
        g_out[rows, :cols] = dq_all
        dq_sum = dq_sum + jnp.sum(dq_all.astype(jnp.float32), axis=0, keepdims=True)
    dk = jnp.concatenate([dk_acc[h] for h in range(heads)], axis=1).astype(jnp.bfloat16)
    dv = jnp.concatenate([dv_acc[h] for h in range(heads)], axis=1).astype(jnp.bfloat16)
    g_out[:, cols:] = jnp.concatenate([dk, dv], axis=1)
    sum_out[0:1] = dq_sum
    sum_out[1:2] = jnp.sum(dv.astype(jnp.float32), axis=0, keepdims=True)


def unwind_call(eas, q, k, v, lse, seg_col, seg_row, gate_row, weight):
    rows, cols = q.shape
    return pl.pallas_call(
        functools.partial(unwind_body, shards=len(eas)),
        out_shape=[
            jax.ShapeDtypeStruct((rows, 3 * cols), jnp.bfloat16),
            jax.ShapeDtypeStruct((2, cols), jnp.float32),
        ],
        scratch_shapes=[
            pltpu.VMEM((cols // HD, rows, HD), jnp.float32),
            pltpu.VMEM((cols // HD, rows, HD), jnp.float32),
        ],
        name="unwind",
    )(*eas, q, k, v, lse, seg_col, seg_row, gate_row, weight)


def raise_body(m, w1, w2, bias, gate, h_out, slope_out, p_out):
    u = dot(m[...], w1[...], 1, 0) + bias[...]
    half = 0.5 * (1.0 + lax.erf(u * root_half))
    low = (u * half * gate[...]).astype(jnp.bfloat16)
    h_out[...] = low
    slope = half + u * jnp.exp(-0.5 * u * u) * normal_peak
    slope_out[...] = slope * gate[...]
    p_out[...] = dot(low, w2[...], 1, 0).astype(jnp.bfloat16)


def raise_call(piece, w1, w2, bias, gate):
    rows, units = piece.shape[0], w1.shape[1]
    return pl.pallas_call(
        raise_body,
        out_shape=[
            jax.ShapeDtypeStruct((rows, units), jnp.bfloat16),
            jax.ShapeDtypeStruct((rows, units), jnp.float32),
            jax.ShapeDtypeStruct(piece.shape, jnp.bfloat16),
        ],
        name="raise",
    )(piece, w1, w2, bias, gate)


def lower_body(e, w1, w2, slope, d_out, p_out, s_out):
    du = (dot(e[...], w2[...], 1, 1) * slope[...]).astype(jnp.bfloat16)
    d_out[...] = du
    p_out[...] = dot(du, w1[...], 1, 1).astype(jnp.bfloat16)
    s_out[...] = jnp.sum(du.astype(jnp.float32), axis=0, keepdims=True)


def lower_call(piece, w1, w2, slope):
    rows, units = slope.shape
    return pl.pallas_call(
        lower_body,
        out_shape=[
            jax.ShapeDtypeStruct((rows, units), jnp.bfloat16),
            jax.ShapeDtypeStruct(piece.shape, jnp.bfloat16),
            jax.ShapeDtypeStruct((1, units), jnp.float32),
        ],
        name="lower",
    )(piece, w1, w2, slope)


def pack_row(grad, put, block):
    for i in range(grad.shape[0] // BLK):
        for side in range(2):
            at = i * BLK + side * QUART
            top = grad[at : at + QUART, :].astype(jnp.bfloat16)
            low = grad[at + HALF : at + HALF + QUART, :].astype(jnp.bfloat16)
            for j in range(grad.shape[1] // BLK):
                cut = slice(j * BLK, (j + 1) * BLK)
                put(
                    side,
                    block + i * (grad.shape[1] // BLK) + j,
                    jnp.concatenate([top[:, cut], low[:, cut]], axis=1),
                )


def inner_body(*refs, shards):
    groups = [refs[i * shards : (i + 1) * shards] for i in range(4)]
    outs = refs[4 * shards :]

    def put(side, block, value):
        outs[side][block] = value

    block = 0
    for left, right in ((groups[0], groups[1]), (groups[2], groups[3])):
        grad = functools.reduce(
            jnp.add, [dot(a[...], b[...], 0, 0) for a, b in zip(left, right)]
        )
        pack_row(grad, put, block)
        block += grad.shape[0] * grad.shape[1] // (BLK * BLK)


def inner_call(mids, d_raised, hidden, branch):
    shards = len(mids)
    blocks = 2 * mids[0].shape[1] * hidden[0].shape[1] // (BLK * BLK)
    out = jax.ShapeDtypeStruct((blocks, QUART, 2 * BLK), jnp.bfloat16)
    return pl.pallas_call(
        functools.partial(inner_body, shards=shards), out_shape=[out, out], name="inner"
    )(*mids, *d_raised, *hidden, *branch)


def outer_body(pos_a, pos_b, *refs, shards, blocks):
    xs, eas = refs[:shards], refs[shards : 2 * shards]
    cg, g, ffn_a, ffn_b = refs[2 * shards : 2 * shards + 4]
    outs = refs[2 * shards + 4 : 2 * shards + 8]
    bufs, sems = refs[2 * shards + 8 : 2 * shards + 10], refs[2 * shards + 10]
    poses = (pos_a, pos_b)
    span = xs[0].shape[0]
    total = bufs[0].shape[0]
    if total > blocks:
        for buf in bufs:
            buf[...] = jnp.zeros_like(buf)

    def put(side, block, value):
        bufs[side][poses[side][block]] = value

    first = blocks - ffn_a.shape[0]
    for side, src in enumerate((ffn_a, ffn_b)):
        for b in range(ffn_a.shape[0]):
            put(side, first + b, src[b])
    cut = [slice(s * span, (s + 1) * span) for s in range(shards)]
    grad = functools.reduce(jnp.add, [dot(x[...], g[c], 0, 0) for x, c in zip(xs, cut)])
    pack_row(grad, put, 0)
    block = grad.shape[0] * grad.shape[1] // (BLK * BLK)
    grad = functools.reduce(jnp.add, [dot(cg[c], e[...], 0, 0) for e, c in zip(eas, cut)])
    pack_row(grad, put, block)
    half = total // 2
    copies = []
    for side in range(2):
        for part in (1, 0):
            copy = pltpu.make_async_copy(
                bufs[side].at[pl.ds(part * half, half)], outs[2 * side + part], sems.at[side, part]
            )
            copy.start()
            copies.append(copy)
    for copy in copies:
        copy.wait()


def outer_call(pos_a, pos_b, xs, eas, cg, g, ffn_a, ffn_b, total):
    shards = len(xs)
    blocks = (xs[0].shape[1] * g.shape[1] + cg.shape[1] * eas[0].shape[1]) // (BLK * BLK)
    blocks += ffn_a.shape[0]
    part = jax.ShapeDtypeStruct((total // 2, QUART, 2 * BLK), jnp.bfloat16)
    buf = pltpu.VMEM((total, QUART, 2 * BLK), jnp.bfloat16)
    return pl.pallas_call(
        functools.partial(outer_body, shards=shards, blocks=blocks),
        in_specs=[pl.BlockSpec(memory_space=pltpu.SMEM)] * 2
        + [pl.BlockSpec(memory_space=pltpu.VMEM)] * (2 * shards + 4),
        out_specs=[pl.BlockSpec(memory_space=pl.ANY)] * 4,
        out_shape=[part] * 4,
        scratch_shapes=[buf, buf, pltpu.SemaphoreType.DMA((2, 2))],
        name="outer",
    )(pos_a, pos_b, *xs, *eas, cg, g, ffn_a, ffn_b)


def adam_moments(gradient, first_moment, second_moment, count_now):
    first_moment = beta_one * first_moment + (1.0 - beta_one) * gradient
    second_moment = beta_two * second_moment + (1.0 - beta_two) * gradient * gradient
    scaled = (
        first_moment
        / (1.0 - beta_one**count_now)
        / (jnp.sqrt(second_moment / (1.0 - beta_two**count_now)) + adam_eps)
    )
    return (first_moment, second_moment, scaled)


def bit_pairs(bit, size):
    return [(i, i ^ (1 << bit)) for i in range(size)]


def bit_count(size):
    return size.bit_length() - 1


def second_order(bits):
    return ([bits[1], bits[0]] + bits[2:]) if len(bits) > 1 else bits


def cast_body(w_ref, a_out, b_out, scratch):
    m = read_square(w_ref, (0,), scratch, 3, 0)
    packed = jnp.concatenate([m[:HALF], m[HALF:]], axis=1).astype(jnp.bfloat16)
    a_out[0] = packed[:QUART]
    b_out[0] = packed[QUART:]


def cast_call(flat):
    n = flat.shape[0]
    piece = jax.ShapeDtypeStruct((n, QUART, 2 * BLK), jnp.bfloat16)
    spec = pl.BlockSpec((1, QUART, 2 * BLK), lambda i: (i, 0, 0))
    return pl.pallas_call(
        cast_body,
        grid=(n,),
        in_specs=[pl.BlockSpec((1, FLAT, 128), lambda i: (i, 0, 0))],
        out_specs=[spec, spec],
        out_shape=[piece, piece],
        scratch_shapes=[pltpu.VMEM((2, BLK, 128), jnp.float32)],
        name="cast",
    )(flat)


def spread(block, order, size):
    pieces = [block[None]]
    rel = [[0]]
    for bit in order:
        moved = [lax.ppermute(p, "dp", bit_pairs(bit, size)) for p in pieces]
        rel = rel + [[r ^ (1 << bit) for r in group] for group in rel]
        pieces = pieces + moved
        if size > 8:
            pieces = [jnp.concatenate(pieces)]
            rel = [sum(rel, [])]
    return pieces, sum(rel, [])


def build_body(pos_a, pos_b, *refs, count):
    ins_a, ins_b = refs[:count], refs[count : 2 * count]
    outs = refs[2 * count : 2 * count + 4]
    buf_a, buf_b, sems = refs[2 * count + 4 :]
    copies = []
    for side, (ins, buf) in enumerate(((ins_a, buf_a), (ins_b, buf_b))):
        at = 0
        for i, src in enumerate(ins):
            m = src.shape[0]
            copy = pltpu.make_async_copy(src, buf.at[pl.ds(at, m)], sems.at[side, i])
            copy.start()
            copies.append(copy)
            at += m
    for copy in copies:
        copy.wait()
    base = 0
    for out in outs:
        rows, cols = out.shape[0] // BLK, out.shape[1] // BLK
        for i in range(rows):
            for side, (buf, pos) in enumerate(((buf_a, pos_a), (buf_b, pos_b))):
                got = [buf[pos[base + i * cols + j]] for j in range(cols)]
                at = i * BLK + side * QUART
                out[at : at + QUART, :] = jnp.concatenate([g[:, :BLK] for g in got], axis=1)
                at += HALF
                out[at : at + QUART, :] = jnp.concatenate([g[:, BLK:] for g in got], axis=1)
        base += rows * cols


def build_call(pos_a, pos_b, pieces_a, pieces_b, shapes):
    flat_a = [p.reshape(-1, QUART, 2 * BLK) for p in pieces_a]
    flat_b = [p.reshape(-1, QUART, 2 * BLK) for p in pieces_b]
    count = len(flat_a)
    total = sum(p.shape[0] for p in flat_a)
    bf16 = jnp.bfloat16
    kernel = functools.partial(build_body, count=count)
    return pl.pallas_call(
        kernel,
        in_specs=[pl.BlockSpec(memory_space=pltpu.SMEM)] * 2
        + [pl.BlockSpec(memory_space=pl.ANY)] * (2 * count),
        out_shape=[jax.ShapeDtypeStruct(s, bf16) for s in shapes],
        scratch_shapes=[
            pltpu.VMEM((total, QUART, 2 * BLK), bf16),
            pltpu.VMEM((total, QUART, 2 * BLK), bf16),
            pltpu.SemaphoreType.DMA((2, count)),
        ],
        name="build",
    )(pos_a, pos_b, *flat_a, *flat_b)


def fold(keep, send, order, size):
    for step, bit in enumerate(order):
        got = lax.ppermute(send, "dp", bit_pairs(bit, size))
        if step == len(order) - 1:
            return keep, got
        half = keep.shape[0] // 2
        cur = (keep.astype(jnp.float32) + got.astype(jnp.float32)).astype(jnp.bfloat16)
        keep, send = cur[:half], cur[half:]


def fold_position(owner, slot, order, slots, me):
    rel = owner ^ me
    index = jnp.zeros_like(rel)
    for bit in order:
        index = index * 2 + ((rel >> bit) & 1)
    return index * slots + slot


def butterfly(value, axis, size):
    for bit in range(bit_count(size)):
        value = value + lax.ppermute(value, axis, bit_pairs(bit, size))
    return value


def swap(piece, s, shards):
    return lax.ppermute(piece, "tensor", [(i, i ^ s) for i in range(shards)])


def shift(piece, pairs):
    return lax.ppermute(piece, "tensor", pairs)


def gather_rows(rows, shards, relayed=True):
    if not relayed or shards != 4:
        far = {s: swap(rows, s, shards) for s in reversed(range(1, shards))}
        return [rows] + [far[s] for s in range(1, shards)]
    two = swap(rows, 2, shards)
    one = swap(rows, 1, shards)
    relay = shift(two, [(2, 3), (1, 0)])
    inner = shift(rows, [(1, 2), (2, 1)])
    return [rows, one, two, inner + relay]


def scatter_rows(pieces, shards, relayed=False):
    if relayed and shards == 4:
        relay = shift(pieces[3], [(0, 1), (3, 2)])
        far = (pieces[2].astype(jnp.float32) + relay.astype(jnp.float32)).astype(jnp.bfloat16)
        others = [
            swap(far, 2, shards),
            swap(pieces[1], 1, shards),
            shift(pieces[3], [(1, 2), (2, 1)]),
        ]
    else:
        others = [swap(pieces[s], s, shards) for s in range(1, shards)]
    total = pieces[0].astype(jnp.float32)
    for piece in others:
        total = total + piece.astype(jnp.float32)
    return total


def body(
    tokens,
    cotangent,
    segments,
    gates_local,
    gates_shared,
    gate_logits,
    shared_logits,
    masters,
    moment_one,
    moment_two,
    block_bases,
    block_stats,
    unit_params,
    unit_first,
    unit_second,
    norm_params,
    norm_first,
    norm_second,
    slot_ids,
    step_count,
):
    shards = lax.axis_size("tensor")
    owners = lax.axis_size("dp")
    head_count = H // shards
    head_cols = head_count * HD
    unit_count = FF // shards
    slot_count = masters.shape[1]
    me = lax.axis_index("dp")
    place = lax.axis_index("tensor")
    bits = list(range(bit_count(owners)))
    head_keep = keep_prob(gate_logits[0, :head_count])
    unit_keep = keep_prob(gate_logits[0, head_count:])
    shared_keep = keep_prob(shared_logits)
    lanes = lax.broadcasted_iota(jnp.int32, (1, D), 1)
    keep_row = jnp.where(
        lanes == 0, jnp.sum(head_keep), jnp.where(lanes == 1, jnp.sum(unit_keep), 0.0)
    )
    flat_view = (slot_count, FLAT, 128)
    cast_a, cast_b = cast_call(masters.reshape(flat_view))
    order_a = bits[1:] + bits[:1]
    order_b = second_order(bits[1:]) + bits[:1]
    tokens, cast_a = lax.optimization_barrier((tokens, cast_a))
    pieces_a, rel_a = spread(cast_a, order_a, owners)
    pieces_b, rel_b = spread(cast_b, order_b, owners)
    owner_of = slot_ids // slot_count
    slot_of = slot_ids % slot_count
    rel_of = owner_of ^ me

    def piece_spot(rel_list):
        table = [0] * owners
        for spot, rel in enumerate(rel_list):
            table[rel] = spot
        return jnp.asarray(table, jnp.int32)[rel_of] * slot_count + slot_of

    qkv_weight, out_weight, up_weight, down_weight = build_call(
        piece_spot(rel_a),
        piece_spot(rel_b),
        pieces_a,
        pieces_b,
        ((D, 3 * head_cols), (head_cols, D), (D, unit_count), (unit_count, D)),
    )
    unit_low = unit_params.astype(jnp.bfloat16)
    unit_pieces, _ = spread(unit_low[0], bits, owners)
    unit_all = jnp.concatenate(unit_pieces, axis=0)
    unit_bias = unit_all[jnp.arange(owners) ^ me].reshape(-1).astype(jnp.float32)
    head_gate = gates_local[0, :head_count]
    unit_gate = gates_local[0, head_count:]
    keeper = gates_shared[:D]
    mha_gate = gates_shared[D]
    ffn_gate = gates_shared[D + 1]
    gain_one = norm_params[0]
    shift_one = norm_params[1]
    bias_attn = norm_params[2]
    gain_two = norm_params[3]
    shift_two = norm_params[4]
    bias_ffn = norm_params[5]
    token_pieces = gather_rows(tokens, shards, False)
    span = LEN // shards
    parts = segments.reshape(shards, span)
    turned_row = parts[jnp.arange(shards) ^ place].reshape(1, LEN)
    turned_col = turned_row.reshape(LEN, 1)
    queries, key_rows, value_rows = project_call(
        token_pieces, qkv_weight, unit_bias[: 2 * head_cols].reshape(2, head_cols)
    )
    gate_row = jnp.repeat(head_gate, HD).reshape(1, head_cols)
    gated_ctx, level, *partial = attend_call(
        queries,
        key_rows,
        value_rows,
        turned_col,
        turned_row,
        gate_row.reshape(head_cols, 1),
        out_weight,
        tuple(range(shards)),
        shards,
    )
    attn_sum = scatter_rows(partial, shards, True)
    residual = tokens.astype(jnp.float32)
    hidden_one = residual + mha_gate * (attn_sum + bias_attn)
    middle, normed_one, inverse_one = norm_forward(hidden_one, gain_one, shift_one, keeper)
    middle_pieces = gather_rows(middle.astype(jnp.bfloat16), shards)
    up_bias = unit_bias[2 * head_cols :].reshape(1, unit_count)
    gate_units = unit_gate.reshape(1, unit_count)
    raised = [
        raise_call(piece, up_weight, down_weight, up_bias, gate_units) for piece in middle_pieces
    ]
    ffn_sum = scatter_rows([r[2] for r in raised], shards)
    hidden_two = middle + ffn_gate * (ffn_sum + bias_ffn)
    layer_out, normed_two, inverse_two = norm_forward(hidden_two, gain_two, shift_two, keeper)
    upstream = cotangent.astype(jnp.float32)
    grad_two, d_gain_two, d_shift_two = norm_backward(
        upstream, normed_two, inverse_two, gain_two, keeper
    )
    d_bias_ffn = ffn_gate * jnp.sum(grad_two, axis=0)
    branch_low = (ffn_gate * grad_two).astype(jnp.bfloat16)
    branch_pieces = gather_rows(branch_low, shards)
    lowered = [
        lower_call(piece, up_weight, down_weight, r[1]) for piece, r in zip(branch_pieces, raised)
    ]
    d_up_bias = functools.reduce(jnp.add, [part[2][0] for part in lowered])
    grad_middle = grad_two + scatter_rows([part[1] for part in lowered], shards)
    grad_one, d_gain_one, d_shift_one = norm_backward(
        grad_middle, normed_one, inverse_one, gain_one, keeper
    )
    d_bias_attn = mha_gate * jnp.sum(grad_one, axis=0)
    attn_low = (mha_gate * grad_one).astype(jnp.bfloat16)
    attn_pieces = gather_rows(attn_low, shards)
    norm_local = jnp.concatenate(
        [
            jnp.stack([d_gain_one, d_shift_one, d_bias_attn, d_gain_two, d_shift_two, d_bias_ffn]),
            keep_row,
        ]
    )
    summed = butterfly(butterfly(norm_local, "tensor", shards), "dp", owners)
    norm_grads = summed[:6]
    keep_sums = summed[6, :2] * (1.0 / owners)
    ffn_a, ffn_b = inner_call(
        middle_pieces, [part[0] for part in lowered], [r[0] for r in raised], branch_pieces
    )
    d_qkv, head_sums = unwind_call(
        attn_pieces,
        queries,
        key_rows,
        value_rows,
        level,
        turned_col,
        turned_row,
        gate_row,
        out_weight,
    )
    d_units = jnp.concatenate([head_sums[0], head_sums[1], d_up_bias])
    fold_a = bits
    fold_b = bits[:1] + second_order(bits[1:])
    keep_a, send_a, keep_b, send_b = outer_call(
        fold_position(owner_of, slot_of, fold_a, slot_count, me),
        fold_position(owner_of, slot_of, fold_b, slot_count, me),
        token_pieces,
        attn_pieces,
        gated_ctx,
        d_qkv,
        ffn_a,
        ffn_b,
        owners * slot_count,
    )
    keep_a, got_a = fold(keep_a, send_a, fold_a, owners)
    keep_b, got_b = fold(keep_b, send_b, fold_b, owners)
    share = unit_params.shape[1]
    units = d_units.reshape(-1, 128)
    unit_grad = lax.dynamic_slice(
        butterfly(units, "dp", owners).reshape(-1), (me * share,), (share,)
    )
    token_part = jnp.einsum(
        "rc,dc->rd", d_qkv, qkv_weight, preferred_element_type=jnp.float32
    ).astype(jnp.bfloat16)
    token_part = [token_part[s * span : (s + 1) * span] for s in range(shards)]
    token_part, got_a, got_b, unit_grad = lax.optimization_barrier(
        (token_part, got_a, got_b, unit_grad)
    )
    token_far = [swap(token_part[s], s, shards) for s in range(1, shards)]
    count_now = step_count[0].astype(jnp.float32)

    def pair_view(x):
        x = x.reshape(slot_count, 2, FLAT, 128)
        return x.transpose(0, 2, 1, 3).reshape(slot_count, 2 * FLAT, 128)

    def pair_back(x):
        x = x.reshape(slot_count, FLAT, 2, 128).transpose(0, 2, 1, 3)
        return x.reshape(1, slot_count, 2, BLK * BLK)

    correction = (1.0 / (1.0 - beta_one**count_now)).reshape(1, 1)
    owned, masters_new, moment_one_new, moment_two_new, stats_new, turned = soap_call(
        correction,
        keep_a,
        got_a,
        keep_b,
        got_b,
        masters.reshape(flat_view),
        moment_one.reshape(flat_view),
        moment_two.reshape(flat_view),
        pair_view(block_bases),
        pair_view(block_stats),
    )
    bases_new = orth_call(turned)
    bases_new, token_far = lax.optimization_barrier((bases_new, token_far))
    token_grad = grad_one + token_part[0].astype(jnp.float32)
    for far in token_far:
        token_grad = token_grad + far.astype(jnp.float32)
    flat_shape = (1, slot_count, BLK * BLK)
    unit_first_new, unit_second_new, unit_scaled = adam_moments(
        unit_grad, unit_first[0], unit_second[0], count_now
    )
    norm_first_new, norm_second_new, norm_scaled = adam_moments(
        norm_grads, norm_first, norm_second, count_now
    )
    hidden_sum = jnp.sum(shared_keep[:D])
    param_count = 1e-06 * (
        shared_keep[D] * keep_sums[0] * (4 * HD) * hidden_sum
        + shared_keep[D + 1] * keep_sums[1] * 2 * hidden_sum
    )
    return (
        layer_out.astype(jnp.bfloat16),
        token_grad,
        owned.reshape(flat_shape),
        masters_new.reshape(flat_shape),
        moment_one_new.reshape(flat_shape),
        moment_two_new.reshape(flat_shape),
        pair_back(bases_new),
        pair_back(stats_new),
        (unit_params[0] - rate_vector * unit_scaled)[None],
        unit_first_new[None],
        unit_second_new[None],
        norm_grads,
        norm_params - rate_vector * norm_scaled,
        norm_first_new,
        norm_second_new,
        param_count.reshape(1),
    )


def solution(mesh):
    placed = (
        P(("dp", "tensor"), None),
        P(("dp", "tensor"), None),
        P("dp", None),
        P("tensor", None),
        P(),
        P("tensor", None),
        P(),
        P("tensor", "dp", None),
        P("tensor", "dp", None),
        P("tensor", "dp", None),
        P("tensor", "dp", None, None),
        P("tensor", "dp", None, None),
        P("tensor", "dp"),
        P("tensor", "dp"),
        P("tensor", "dp"),
        P(),
        P(),
        P(),
        P(),
        P(),
    )
    return jax.shard_map(
        body,
        mesh=mesh,
        in_specs=placed,
        out_specs=(
            P(("dp", "tensor"), None),
            P(("dp", "tensor"), None),
            P("tensor", "dp", None),
            P("tensor", "dp", None),
            P("tensor", "dp", None),
            P("tensor", "dp", None),
            P("tensor", "dp", None, None),
            P("tensor", "dp", None, None),
            P("tensor", "dp"),
            P("tensor", "dp"),
            P("tensor", "dp"),
            P(),
            P(),
            P(),
            P(),
            P(),
        ),
        check_vma=False,
    )
```

```python
import math
import functools
import jax
import jax.numpy as jnp
from jax import lax
from jax.sharding import PartitionSpec as P
from jax.experimental import pallas as pl
from jax.experimental.pallas import tpu as pltpu

BLK = 192
HALF = 96
QUART = 48
FLAT = 288
PAN = 64
beta_one = 0.95
beta_two = 0.95
beta_stat = 0.95
adam_eps = 1e-08
rate_matrix = 0.1
HIGH = lax.Precision.HIGH
EXACT = lax.Precision.HIGHEST


def mm(a, b, da, db, precision):
    return lax.dot_general(
        a, b, (((da,), (db,)), ((), ())), precision=precision, preferred_element_type=jnp.float32
    )


def read_square(src, lead, scratch, stride, first):
    def rows(q):
        return src[lead + (pl.ds(first + q * (stride // 3), HALF, stride=stride), slice(None))]

    a, b, c = rows(0), rows(1), rows(2)
    scratch[0, pl.ds(0, HALF, stride=2), :] = a
    scratch[1, pl.ds(0, HALF, stride=2), :] = b
    scratch[0, pl.ds(1, HALF, stride=2), :] = jnp.concatenate([b[:, 64:], c[:, :64]], axis=1)
    scratch[1, pl.ds(1, HALF, stride=2), :] = jnp.concatenate([c[:, 64:], c[:, 64:]], axis=1)
    return jnp.concatenate([scratch[0], scratch[1, :, :64]], axis=1)


def write_square(value, dst, lead, scratch, stride, first):
    scratch[0] = value[:, :128]
    scratch[1, :, :64] = value[:, 128:]
    e0 = scratch[0, pl.ds(0, HALF, stride=2), :]
    e1 = scratch[1, pl.ds(0, HALF, stride=2), :]
    o0 = scratch[0, pl.ds(1, HALF, stride=2), :]
    o1 = scratch[1, pl.ds(1, HALF, stride=2), :]
    step = stride // 3
    dst[lead + (pl.ds(first, HALF, stride=stride), slice(None))] = e0
    dst[lead + (pl.ds(first + step, HALF, stride=stride), slice(None))] = jnp.concatenate(
        [e1[:, :64], o0[:, :64]], axis=1
    )
    dst[lead + (pl.ds(first + 2 * step, HALF, stride=stride), slice(None))] = jnp.concatenate(
        [o0[:, 64:], o1[:, :64]], axis=1
    )


def soap_body(
    scale_ref, ka, ra, kb, rb, w_ref, m1_ref, m2_ref, b_ref, s_ref,
    g_out, w_out, m1_out, m2_out, s_out, mt_out, *scr,
):
    scratch = list(scr)
    ga = ka[0].astype(jnp.float32) + ra[0].astype(jnp.float32)
    gb = kb[0].astype(jnp.float32) + rb[0].astype(jnp.float32)
    g = jnp.concatenate([ga[:, :BLK], gb[:, :BLK], ga[:, BLK:], gb[:, BLK:]], axis=0)
    write_square(g, g_out, (0,), scratch[0], 3, 0)
    ql = read_square(b_ref, (0,), scratch[1], 6, 0)
    qr = read_square(b_ref, (0,), scratch[2], 6, 1)
    t3 = mm(g, qr, 1, 0, HIGH)
    r = mm(ql, t3, 0, 0, HIGH)
    rs, as_ = scratch[3], scratch[4]
    write_square(r, m1_out, (0,), rs, 3, 0)
    flat = m1_out[0]
    m1 = beta_one * m1_ref[0] + (1.0 - beta_one) * flat
    m2 = beta_two * m2_ref[0] + (1.0 - beta_two) * flat * flat
    m1_out[0] = m1
    m2_out[0] = m2
    corr = scale_ref[0, 0]
    w_out[0] = (m1 * corr) / (jnp.sqrt(m2 * corr) + adam_eps)
    a = read_square(w_out, (0,), as_, 3, 0)
    restored = mm(mm(ql, a, 1, 0, HIGH), qr, 1, 1, HIGH)
    write_square(restored, w_out, (0,), rs, 3, 0)
    w_out[0] = w_ref[0] - rate_matrix * w_out[0]
    sl = read_square(s_ref, (0,), scratch[5], 6, 0)
    sl = beta_stat * sl + (1.0 - beta_stat) * mm(g, g, 1, 1, HIGH)
    write_square(sl, s_out, (0,), scratch[6], 6, 0)
    mt_out[0, 0] = mm(ql, sl, 0, 0, EXACT)
    sr = read_square(s_ref, (0,), scratch[7], 6, 1)
    sr = beta_stat * sr + (1.0 - beta_stat) * mm(g, g, 0, 0, HIGH)
    write_square(sr, s_out, (0,), scratch[6], 6, 1)
    mt_out[0, 1] = mm(qr, sr, 0, 0, EXACT)


def soap_call(scale, ka, ra, kb, rb, w, m1, m2, b, s):
    n = w.shape[0]
    f32 = jnp.float32

    def spec(shape):
        zeros = (0,) * (len(shape) - 1)
        return pl.BlockSpec((1,) + shape[1:], lambda i: (i,) + zeros)

    ins = [ka, ra, kb, rb, w, m1, m2, b, s]
    outs = [
        jax.ShapeDtypeStruct((n, FLAT, 128), f32),
        jax.ShapeDtypeStruct((n, FLAT, 128), f32),
        jax.ShapeDtypeStruct((n, FLAT, 128), f32),
        jax.ShapeDtypeStruct((n, FLAT, 128), f32),
        jax.ShapeDtypeStruct((n, 2 * FLAT, 128), f32),
        jax.ShapeDtypeStruct((n, 2, BLK, BLK), f32),
    ]
    return pl.pallas_call(
        soap_body,
        grid=(n,),
        in_specs=[pl.BlockSpec(memory_space=pltpu.SMEM)] + [spec(x.shape) for x in ins],
        out_specs=[spec(o.shape) for o in outs],
        out_shape=outs,
        scratch_shapes=[pltpu.VMEM((2, BLK, 128), f32)] * 8,
        name="soap",
    )(scale, *ins)


def orth_body(mt_ref, q_out, xa, xs, sq):
    n = mt_ref.shape[0] * 2
    for i in range(n):
        m = mt_ref[i // 2, i % 2]
        xa[i, :, 256 : 256 + BLK] = m
        xa[i, :, 0:BLK] = mm(m, m, 1, 1, EXACT)
    lane = lax.broadcasted_iota(jnp.int32, (1, 1, 2 * PAN), 2)
    eye = (
        lax.broadcasted_iota(jnp.int32, (n, PAN, PAN), 1)
        == lax.broadcasted_iota(jnp.int32, (n, PAN, PAN), 2)
    ).astype(jnp.float32)

    def pick(v, j):
        return jnp.sum(jnp.where(lane == j, v, 0.0), axis=2, keepdims=True)

    for k in range(BLK // PAN):
        lo, hi = k * PAN, (k + 1) * PAN
        xs[...] = jnp.concatenate([xa[:, lo:hi, lo:hi], eye], axis=2)
        for first in range(0, PAN, 8):
            row_id = lax.broadcasted_iota(jnp.int32, (1, PAN - first, 1), 1) + first

            def step(s, carry):
                x = xs[:, first:, :]
                j = first + 2 * s
                r0 = xs[:, pl.ds(j, 1), :]
                r1 = xs[:, pl.ds(j + 1, 1), :]
                c0, c1 = pick(x, j), pick(x, j + 1)
                p, q, d = pick(r0, j), pick(r0, j + 1), pick(r1, j + 1)
                ip = 1.0 / p
                e = q * ip
                r1 = r1 - e * r0
                ip1 = 1.0 / (d - e * q)
                f0 = c0 * ip
                f1 = (c1 - f0 * q) * ip1
                f0 = jnp.where(row_id > j, f0, 0.0)
                f1 = jnp.where(row_id > j + 1, f1, 0.0)
                xs[:, first:, :] = x - (f0 * r0 + f1 * r1)
                return carry

            lax.fori_loop(0, 4, step, 0)
        x = xs[...]
        row_id = lax.broadcasted_iota(jnp.int32, (1, PAN, 1), 1)
        diag = jnp.sum(jnp.where(lane == row_id, x, 0.0), axis=2, keepdims=True)
        t = x[:, :, PAN:] * lax.rsqrt(diag)
        for i in range(n):
            w = mm(t[i], xa[i, lo:hi, :], 1, 0, EXACT)
            xa[i, lo:hi, :] = w
            if hi < BLK:
                wt = w[:, :256].T[hi:BLK]
                xa[i, hi:, :] = xa[i, hi:, :] - mm(wt, w, 1, 0, EXACT)
    for i in range(n):
        write_square(xa[i, :, 256:].T[:BLK], q_out, (i // 2,), sq, 6, i % 2)


def orth_call(mt):
    n = mt.shape[0]
    f32 = jnp.float32
    return pl.pallas_call(
        orth_body,
        out_shape=jax.ShapeDtypeStruct((n, 2 * FLAT, 128), f32),
        scratch_shapes=[
            pltpu.VMEM((2 * n, BLK, 512), f32),
            pltpu.VMEM((2 * n, PAN, 2 * PAN), f32),
            pltpu.VMEM((2, BLK, 128), f32),
        ],
        name="orth",
    )(mt)


D = 768
H = 12
FF = 3072
HD = 64
LEN = 1024
norm_eps = 1e-12
rate_vector = 0.25
query_scale = 0.125
stretch_shift = 2.0 / 3.0 * math.log(0.1 / 1.1)
root_half = 1.0 / math.sqrt(2.0)
normal_peak = 1.0 / math.sqrt(2.0 * math.pi)


def keep_prob(logits):
    return jax.nn.sigmoid(logits - stretch_shift)


def norm_forward(hidden, gain_row, shift_row, keeper):
    row_mean = jnp.mean(hidden, axis=-1, keepdims=True)
    centred = hidden - row_mean
    variance = jnp.mean(centred * centred, axis=-1, keepdims=True)
    inverse = lax.rsqrt(variance + norm_eps)
    normed = centred * inverse
    return (keeper * (normed * gain_row + shift_row), normed, inverse)


def norm_backward(incoming, normed, inverse, gain_row, keeper):
    scaled = incoming * keeper
    d_gain = jnp.sum(scaled * normed, axis=0)
    d_shift = jnp.sum(scaled, axis=0)
    d_normed = scaled * gain_row
    d_input = inverse * (
        d_normed
        - jnp.mean(d_normed, axis=-1, keepdims=True)
        - normed * jnp.mean(d_normed * normed, axis=-1, keepdims=True)
    )
    return (d_input, d_gain, d_shift)


def project_body(*refs):
    xs, (w, bias, q_out, k_out, v_out) = refs[:-5], refs[-5:]
    weight = w[...]
    for s, x in enumerate(xs):
        rows = slice(s * x.shape[0], (s + 1) * x.shape[0])
        out = dot(x[...], weight, 1, 0)
        cols = q_out.shape[1]
        q_out[rows] = ((out[:, :cols] + bias[0:1]) * query_scale).astype(jnp.bfloat16)
        k_out[rows] = out[:, cols : 2 * cols].astype(jnp.bfloat16)
        v_out[rows] = (out[:, 2 * cols :] + bias[1:2]).astype(jnp.bfloat16)


def project_call(pieces, weight, bias):
    rows = sum(p.shape[0] for p in pieces)
    out = jax.ShapeDtypeStruct((rows, bias.shape[1]), jnp.bfloat16)
    return pl.pallas_call(project_body, out_shape=[out] * 3, name="project")(
        *pieces, weight, bias
    )


def dot(a, b, da, db):
    return lax.dot_general(
        a, b, (((da,), (db,)), ((), ())), preferred_element_type=jnp.float32
    )


def partners(piece, shards):
    return [piece ^ s for s in range(shards) if s != 2]


def item_bias(seg_col, seg_row, piece, peers, span):
    mine = seg_row[0:1, piece * span : (piece + 1) * span]
    return [
        jnp.where(seg_col[c * span : (c + 1) * span, :] == mine, 0.0, -1e30) for c in peers
    ]


def attend_body(q, k, v, seg_col, seg_row, gate_col, w, *outs, pieces, shards):
    span = q.shape[0] // shards
    cg_out, lse_out = outs[0], outs[1]
    heads = q.shape[1] // HD
    weight = w[...]
    lse_out[...] = jnp.zeros_like(lse_out)
    for at, p in enumerate(pieces):
        peers = partners(p, shards)
        bias = item_bias(seg_col, seg_row, p, peers, span)
        rows = slice(p * span, (p + 1) * span)
        mine = slice(at * span, (at + 1) * span)
        parts = []
        for h in range(heads):
            cut = slice(h * HD, (h + 1) * HD)
            qp = q[rows, cut]
            scores = [
                dot(k[c * span : (c + 1) * span, cut], qp, 1, 1) + b for c, b in zip(peers, bias)
            ]
            top = functools.reduce(jnp.maximum, [jnp.max(s, axis=0, keepdims=True) for s in scores])
            powers = [jnp.exp(s - top) for s in scores]
            total = functools.reduce(
                jnp.add, [jnp.sum(e, axis=0, keepdims=True) for e in powers]
            )
            inverse = 1.0 / total
            context = functools.reduce(
                jnp.add,
                [
                    dot(
                        v[c * span : (c + 1) * span, cut],
                        (e * inverse).astype(jnp.bfloat16),
                        0,
                        0,
                    )
                    for c, e in zip(peers, powers)
                ],
            )
            parts.append(context)
            lse_out[h : h + 1, mine] = top + jnp.log(total)
        gated = (jnp.concatenate(parts, axis=0) * gate_col[...]).T.astype(jnp.bfloat16)
        cg_out[mine] = gated
        outs[2 + at][...] = dot(gated, weight, 1, 0).astype(jnp.bfloat16)


def attend_call(q, k, v, seg_col, seg_row, gate_col, weight, pieces, shards):
    span = q.shape[0] // shards
    bf16 = jnp.bfloat16
    count = len(pieces)
    outs = [
        jax.ShapeDtypeStruct((count * span, q.shape[1]), bf16),
        jax.ShapeDtypeStruct((8, count * span), jnp.float32),
    ] + [jax.ShapeDtypeStruct((span, weight.shape[1]), bf16)] * count
    return pl.pallas_call(
        functools.partial(attend_body, pieces=pieces, shards=shards), out_shape=outs, name="attend"
    )(q, k, v, seg_col, seg_row, gate_col, weight)


def unwind_body(*refs, shards):
    eas = refs[:shards]
    q, k, v, lse, seg_col, seg_row, gate_row, w, g_out, sum_out, dk_acc, dv_acc = refs[shards:]
    span = q.shape[0] // shards
    cols = q.shape[1]
    heads = cols // HD
    weight = w[...]
    dk_acc[...] = jnp.zeros_like(dk_acc)
    dv_acc[...] = jnp.zeros_like(dv_acc)
    dq_sum = jnp.zeros((1, cols), jnp.float32)
    for p in range(shards):
        peers = partners(p, shards)
        bias = item_bias(seg_col, seg_row, p, peers, span)
        rows = slice(p * span, (p + 1) * span)
        d_ctx = (dot(eas[p][...], weight, 1, 1) * gate_row[...]).astype(jnp.bfloat16)
        parts = []
        for h in range(heads):
            cut = slice(h * HD, (h + 1) * HD)
            qp = q[rows, cut]
            do = d_ctx[:, cut]
            level = lse[h : h + 1, rows]
            probs, slopes = [], []
            for c, b in zip(peers, bias):
                ks = slice(c * span, (c + 1) * span)
                prob = jnp.exp(dot(k[ks, cut], qp, 1, 1) + (b - level))
                dv_acc[h, ks] = dv_acc[h, ks] + dot(prob.astype(jnp.bfloat16), do, 1, 0)
                probs.append(prob)
                slopes.append(dot(v[ks, cut], do, 1, 1))
            inner = functools.reduce(
                jnp.add, [jnp.sum(a * b, axis=0, keepdims=True) for a, b in zip(probs, slopes)]
            )
            dq = jnp.zeros((HD, span), jnp.float32)
            for c, a, b in zip(peers, probs, slopes):
                ks = slice(c * span, (c + 1) * span)
                ds = (a * (b - inner)).astype(jnp.bfloat16)
                dk_acc[h, ks] = dk_acc[h, ks] + dot(ds, qp, 1, 0)
                dq = dq + dot(k[ks, cut], ds, 0, 0)
            parts.append(dq)
        dq_all = jnp.concatenate(parts, axis=0).T.astype(jnp.bfloat16) * query_scale
        dq_all = dq_all.astype(jnp.bfloat16)
        g_out[rows, :cols] = dq_all
        dq_sum = dq_sum + jnp.sum(dq_all.astype(jnp.float32), axis=0, keepdims=True)
    dk = jnp.concatenate([dk_acc[h] for h in range(heads)], axis=1).astype(jnp.bfloat16)
    dv = jnp.concatenate([dv_acc[h] for h in range(heads)], axis=1).astype(jnp.bfloat16)
    g_out[:, cols:] = jnp.concatenate([dk, dv], axis=1)
    sum_out[0:1] = dq_sum
    sum_out[1:2] = jnp.sum(dv.astype(jnp.float32), axis=0, keepdims=True)


def unwind_call(eas, q, k, v, lse, seg_col, seg_row, gate_row, weight):
    rows, cols = q.shape
    return pl.pallas_call(
        functools.partial(unwind_body, shards=len(eas)),
        out_shape=[
            jax.ShapeDtypeStruct((rows, 3 * cols), jnp.bfloat16),
            jax.ShapeDtypeStruct((2, cols), jnp.float32),
        ],
        scratch_shapes=[
            pltpu.VMEM((cols // HD, rows, HD), jnp.float32),
            pltpu.VMEM((cols // HD, rows, HD), jnp.float32),
        ],
        name="unwind",
    )(*eas, q, k, v, lse, seg_col, seg_row, gate_row, weight)


def raise_body(m, w1, w2, bias, gate, h_out, slope_out, p_out):
    u = dot(m[...], w1[...], 1, 0) + bias[...]
    half = 0.5 * (1.0 + lax.erf(u * root_half))
    low = (u * half * gate[...]).astype(jnp.bfloat16)
    h_out[...] = low
    slope = half + u * jnp.exp(-0.5 * u * u) * normal_peak
    slope_out[...] = slope * gate[...]
    p_out[...] = dot(low, w2[...], 1, 0).astype(jnp.bfloat16)


def raise_call(piece, w1, w2, bias, gate):
    rows, units = piece.shape[0], w1.shape[1]
    return pl.pallas_call(
        raise_body,
        out_shape=[
            jax.ShapeDtypeStruct((rows, units), jnp.bfloat16),
            jax.ShapeDtypeStruct((rows, units), jnp.float32),
            jax.ShapeDtypeStruct(piece.shape, jnp.bfloat16),
        ],
        name="raise",
    )(piece, w1, w2, bias, gate)


def lower_body(e, w1, w2, slope, d_out, p_out, s_out):
    du = (dot(e[...], w2[...], 1, 1) * slope[...]).astype(jnp.bfloat16)
    d_out[...] = du
    p_out[...] = dot(du, w1[...], 1, 1).astype(jnp.bfloat16)
    s_out[...] = jnp.sum(du.astype(jnp.float32), axis=0, keepdims=True)


def lower_call(piece, w1, w2, slope):
    rows, units = slope.shape
    return pl.pallas_call(
        lower_body,
        out_shape=[
            jax.ShapeDtypeStruct((rows, units), jnp.bfloat16),
            jax.ShapeDtypeStruct(piece.shape, jnp.bfloat16),
            jax.ShapeDtypeStruct((1, units), jnp.float32),
        ],
        name="lower",
    )(piece, w1, w2, slope)


def pack_row(grad, put, block):
    for i in range(grad.shape[0] // BLK):
        for side in range(2):
            at = i * BLK + side * QUART
            top = grad[at : at + QUART, :].astype(jnp.bfloat16)
            low = grad[at + HALF : at + HALF + QUART, :].astype(jnp.bfloat16)
            for j in range(grad.shape[1] // BLK):
                cut = slice(j * BLK, (j + 1) * BLK)
                put(
                    side,
                    block + i * (grad.shape[1] // BLK) + j,
                    jnp.concatenate([top[:, cut], low[:, cut]], axis=1),
                )


def inner_body(*refs, shards):
    groups = [refs[i * shards : (i + 1) * shards] for i in range(4)]
    outs = refs[4 * shards :]

    def put(side, block, value):
        outs[side][block] = value

    block = 0
    for left, right in ((groups[0], groups[1]), (groups[2], groups[3])):
        grad = functools.reduce(
            jnp.add, [dot(a[...], b[...], 0, 0) for a, b in zip(left, right)]
        )
        pack_row(grad, put, block)
        block += grad.shape[0] * grad.shape[1] // (BLK * BLK)


def inner_call(mids, d_raised, hidden, branch):
    shards = len(mids)
    blocks = 2 * mids[0].shape[1] * hidden[0].shape[1] // (BLK * BLK)
    out = jax.ShapeDtypeStruct((blocks, QUART, 2 * BLK), jnp.bfloat16)
    return pl.pallas_call(
        functools.partial(inner_body, shards=shards), out_shape=[out, out], name="inner"
    )(*mids, *d_raised, *hidden, *branch)


def outer_body(pos_a, pos_b, *refs, shards, blocks):
    xs, eas = refs[:shards], refs[shards : 2 * shards]
    cg, g, ffn_a, ffn_b = refs[2 * shards : 2 * shards + 4]
    outs = refs[2 * shards + 4 : 2 * shards + 8]
    bufs, sems = refs[2 * shards + 8 : 2 * shards + 10], refs[2 * shards + 10]
    poses = (pos_a, pos_b)
    span = xs[0].shape[0]
    total = bufs[0].shape[0]
    if total > blocks:
        for buf in bufs:
            buf[...] = jnp.zeros_like(buf)

    def put(side, block, value):
        bufs[side][poses[side][block]] = value

    first = blocks - ffn_a.shape[0]
    for side, src in enumerate((ffn_a, ffn_b)):
        for b in range(ffn_a.shape[0]):
            put(side, first + b, src[b])
    cut = [slice(s * span, (s + 1) * span) for s in range(shards)]
    grad = functools.reduce(jnp.add, [dot(x[...], g[c], 0, 0) for x, c in zip(xs, cut)])
    pack_row(grad, put, 0)
    block = grad.shape[0] * grad.shape[1] // (BLK * BLK)
    grad = functools.reduce(jnp.add, [dot(cg[c], e[...], 0, 0) for e, c in zip(eas, cut)])
    pack_row(grad, put, block)
    half = total // 2
    copies = []
    for side in range(2):
        for part in (1, 0):
            copy = pltpu.make_async_copy(
                bufs[side].at[pl.ds(part * half, half)], outs[2 * side + part], sems.at[side, part]
            )
            copy.start()
            copies.append(copy)
    for copy in copies:
        copy.wait()


def outer_call(pos_a, pos_b, xs, eas, cg, g, ffn_a, ffn_b, total):
    shards = len(xs)
    blocks = (xs[0].shape[1] * g.shape[1] + cg.shape[1] * eas[0].shape[1]) // (BLK * BLK)
    blocks += ffn_a.shape[0]
    part = jax.ShapeDtypeStruct((total // 2, QUART, 2 * BLK), jnp.bfloat16)
    buf = pltpu.VMEM((total, QUART, 2 * BLK), jnp.bfloat16)
    return pl.pallas_call(
        functools.partial(outer_body, shards=shards, blocks=blocks),
        in_specs=[pl.BlockSpec(memory_space=pltpu.SMEM)] * 2
        + [pl.BlockSpec(memory_space=pltpu.VMEM)] * (2 * shards + 4),
        out_specs=[pl.BlockSpec(memory_space=pl.ANY)] * 4,
        out_shape=[part] * 4,
        scratch_shapes=[buf, buf, pltpu.SemaphoreType.DMA((2, 2))],
        name="outer",
    )(pos_a, pos_b, *xs, *eas, cg, g, ffn_a, ffn_b)


def adam_moments(gradient, first_moment, second_moment, count_now):
    first_moment = beta_one * first_moment + (1.0 - beta_one) * gradient
    second_moment = beta_two * second_moment + (1.0 - beta_two) * gradient * gradient
    scaled = (
        first_moment
        / (1.0 - beta_one**count_now)
        / (jnp.sqrt(second_moment / (1.0 - beta_two**count_now)) + adam_eps)
    )
    return (first_moment, second_moment, scaled)


def bit_pairs(bit, size):
    return [(i, i ^ (1 << bit)) for i in range(size)]


def bit_count(size):
    return size.bit_length() - 1


def second_order(bits):
    return ([bits[1], bits[0]] + bits[2:]) if len(bits) > 1 else bits


def cast_body(w_ref, a_out, b_out, scratch):
    m = read_square(w_ref, (0,), scratch, 3, 0)
    packed = jnp.concatenate([m[:HALF], m[HALF:]], axis=1).astype(jnp.bfloat16)
    a_out[0] = packed[:QUART]
    b_out[0] = packed[QUART:]


def cast_call(flat):
    n = flat.shape[0]
    piece = jax.ShapeDtypeStruct((n, QUART, 2 * BLK), jnp.bfloat16)
    spec = pl.BlockSpec((1, QUART, 2 * BLK), lambda i: (i, 0, 0))
    return pl.pallas_call(
        cast_body,
        grid=(n,),
        in_specs=[pl.BlockSpec((1, FLAT, 128), lambda i: (i, 0, 0))],
        out_specs=[spec, spec],
        out_shape=[piece, piece],
        scratch_shapes=[pltpu.VMEM((2, BLK, 128), jnp.float32)],
        name="cast",
    )(flat)


def spread(block, order, size):
    pieces = [block[None]]
    rel = [[0]]
    for bit in order:
        moved = [lax.ppermute(p, "dp", bit_pairs(bit, size)) for p in pieces]
        rel = rel + [[r ^ (1 << bit) for r in group] for group in rel]
        pieces = pieces + moved
        if size > 8:
            pieces = [jnp.concatenate(pieces)]
            rel = [sum(rel, [])]
    return pieces, sum(rel, [])


def build_body(pos_a, pos_b, *refs, count):
    ins_a, ins_b = refs[:count], refs[count : 2 * count]
    outs = refs[2 * count : 2 * count + 4]
    buf_a, buf_b, sems = refs[2 * count + 4 :]
    copies = []
    for side, (ins, buf) in enumerate(((ins_a, buf_a), (ins_b, buf_b))):
        at = 0
        for i, src in enumerate(ins):
            m = src.shape[0]
            copy = pltpu.make_async_copy(src, buf.at[pl.ds(at, m)], sems.at[side, i])
            copy.start()
            copies.append(copy)
            at += m
    for copy in copies:
        copy.wait()
    base = 0
    for out in outs:
        rows, cols = out.shape[0] // BLK, out.shape[1] // BLK
        for i in range(rows):
            for side, (buf, pos) in enumerate(((buf_a, pos_a), (buf_b, pos_b))):
                got = [buf[pos[base + i * cols + j]] for j in range(cols)]
                at = i * BLK + side * QUART
                out[at : at + QUART, :] = jnp.concatenate([g[:, :BLK] for g in got], axis=1)
                at += HALF
                out[at : at + QUART, :] = jnp.concatenate([g[:, BLK:] for g in got], axis=1)
        base += rows * cols


def build_call(pos_a, pos_b, pieces_a, pieces_b, shapes):
    flat_a = [p.reshape(-1, QUART, 2 * BLK) for p in pieces_a]
    flat_b = [p.reshape(-1, QUART, 2 * BLK) for p in pieces_b]
    count = len(flat_a)
    total = sum(p.shape[0] for p in flat_a)
    bf16 = jnp.bfloat16
    kernel = functools.partial(build_body, count=count)
    return pl.pallas_call(
        kernel,
        in_specs=[pl.BlockSpec(memory_space=pltpu.SMEM)] * 2
        + [pl.BlockSpec(memory_space=pl.ANY)] * (2 * count),
        out_shape=[jax.ShapeDtypeStruct(s, bf16) for s in shapes],
        scratch_shapes=[
            pltpu.VMEM((total, QUART, 2 * BLK), bf16),
            pltpu.VMEM((total, QUART, 2 * BLK), bf16),
            pltpu.SemaphoreType.DMA((2, count)),
        ],
        name="build",
    )(pos_a, pos_b, *flat_a, *flat_b)


def fold(keep, send, order, size):
    for step, bit in enumerate(order):
        got = lax.ppermute(send, "dp", bit_pairs(bit, size))
        if step == len(order) - 1:
            return keep, got
        half = keep.shape[0] // 2
        cur = (keep.astype(jnp.float32) + got.astype(jnp.float32)).astype(jnp.bfloat16)
        keep, send = cur[:half], cur[half:]


def fold_position(owner, slot, order, slots, me):
    rel = owner ^ me
    index = jnp.zeros_like(rel)
    for bit in order:
        index = index * 2 + ((rel >> bit) & 1)
    return index * slots + slot


def butterfly(value, axis, size):
    for bit in range(bit_count(size)):
        value = value + lax.ppermute(value, axis, bit_pairs(bit, size))
    return value


def swap(piece, s, shards):
    return lax.ppermute(piece, "tensor", [(i, i ^ s) for i in range(shards)])


def shift(piece, pairs):
    return lax.ppermute(piece, "tensor", pairs)


def gather_rows(rows, shards, relayed=True):
    if not relayed or shards != 4:
        far = {s: swap(rows, s, shards) for s in reversed(range(1, shards))}
        return [rows] + [far[s] for s in range(1, shards)]
    two = swap(rows, 2, shards)
    one = swap(rows, 1, shards)
    relay = shift(two, [(2, 3), (1, 0)])
    inner = shift(rows, [(1, 2), (2, 1)])
    return [rows, one, two, inner + relay]


def scatter_rows(pieces, shards, relayed=False):
    if relayed and shards == 4:
        relay = shift(pieces[3], [(0, 1), (3, 2)])
        far = (pieces[2].astype(jnp.float32) + relay.astype(jnp.float32)).astype(jnp.bfloat16)
        others = [
            swap(far, 2, shards),
            swap(pieces[1], 1, shards),
            shift(pieces[3], [(1, 2), (2, 1)]),
        ]
    else:
        others = [swap(pieces[s], s, shards) for s in range(1, shards)]
    total = pieces[0].astype(jnp.float32)
    for piece in others:
        total = total + piece.astype(jnp.float32)
    return total


def body(
    tokens,
    cotangent,
    segments,
    gates_local,
    gates_shared,
    gate_logits,
    shared_logits,
    masters,
    moment_one,
    moment_two,
    block_bases,
    block_stats,
    unit_params,
    unit_first,
    unit_second,
    norm_params,
    norm_first,
    norm_second,
    slot_ids,
    step_count,
):
    shards = lax.axis_size("tensor")
    owners = lax.axis_size("dp")
    head_count = H // shards
    head_cols = head_count * HD
    unit_count = FF // shards
    slot_count = masters.shape[1]
    me = lax.axis_index("dp")
    place = lax.axis_index("tensor")
    bits = list(range(bit_count(owners)))
    head_keep = keep_prob(gate_logits[0, :head_count])
    unit_keep = keep_prob(gate_logits[0, head_count:])
    shared_keep = keep_prob(shared_logits)
    lanes = lax.broadcasted_iota(jnp.int32, (1, D), 1)
    keep_row = jnp.where(
        lanes == 0, jnp.sum(head_keep), jnp.where(lanes == 1, jnp.sum(unit_keep), 0.0)
    )
    flat_view = (slot_count, FLAT, 128)
    cast_a, cast_b = cast_call(masters.reshape(flat_view))
    order_a = bits[1:] + bits[:1]
    order_b = second_order(bits[1:]) + bits[:1]

    pieces_a, rel_a = spread(cast_a, order_a, owners)
    pieces_b, rel_b = spread(cast_b, order_b, owners)
    owner_of = slot_ids // slot_count
    slot_of = slot_ids % slot_count
    rel_of = owner_of ^ me

    def piece_spot(rel_list):
        table = [0] * owners
        for spot, rel in enumerate(rel_list):
            table[rel] = spot
        return jnp.asarray(table, jnp.int32)[rel_of] * slot_count + slot_of

    qkv_weight, out_weight, up_weight, down_weight = build_call(
        piece_spot(rel_a),
        piece_spot(rel_b),
        pieces_a,
        pieces_b,
        ((D, 3 * head_cols), (head_cols, D), (D, unit_count), (unit_count, D)),
    )
    unit_low = unit_params.astype(jnp.bfloat16)
    unit_pieces, _ = spread(unit_low[0], bits, owners)
    unit_all = jnp.concatenate(unit_pieces, axis=0)
    unit_bias = unit_all[jnp.arange(owners) ^ me].reshape(-1).astype(jnp.float32)
    head_gate = gates_local[0, :head_count]
    unit_gate = gates_local[0, head_count:]
    keeper = gates_shared[:D]
    mha_gate = gates_shared[D]
    ffn_gate = gates_shared[D + 1]
    gain_one = norm_params[0]
    shift_one = norm_params[1]
    bias_attn = norm_params[2]
    gain_two = norm_params[3]
    shift_two = norm_params[4]
    bias_ffn = norm_params[5]
    token_pieces = gather_rows(tokens, shards, False)
    span = LEN // shards
    parts = segments.reshape(shards, span)
    turned_row = parts[jnp.arange(shards) ^ place].reshape(1, LEN)
    turned_col = turned_row.reshape(LEN, 1)
    queries, key_rows, value_rows = project_call(
        token_pieces, qkv_weight, unit_bias[: 2 * head_cols].reshape(2, head_cols)
    )
    gate_row = jnp.repeat(head_gate, HD).reshape(1, head_cols)
    gated_ctx, level, *partial = attend_call(
        queries,
        key_rows,
        value_rows,
        turned_col,
        turned_row,
        gate_row.reshape(head_cols, 1),
        out_weight,
        tuple(range(shards)),
        shards,
    )
    attn_sum = scatter_rows(partial, shards, True)
    residual = tokens.astype(jnp.float32)
    hidden_one = residual + mha_gate * (attn_sum + bias_attn)
    middle, normed_one, inverse_one = norm_forward(hidden_one, gain_one, shift_one, keeper)
    middle_pieces = gather_rows(middle.astype(jnp.bfloat16), shards)
    up_bias = unit_bias[2 * head_cols :].reshape(1, unit_count)
    gate_units = unit_gate.reshape(1, unit_count)
    raised = [
        raise_call(piece, up_weight, down_weight, up_bias, gate_units) for piece in middle_pieces
    ]
    ffn_sum = scatter_rows([r[2] for r in raised], shards)
    hidden_two = middle + ffn_gate * (ffn_sum + bias_ffn)
    layer_out, normed_two, inverse_two = norm_forward(hidden_two, gain_two, shift_two, keeper)
    upstream = cotangent.astype(jnp.float32)
    grad_two, d_gain_two, d_shift_two = norm_backward(
        upstream, normed_two, inverse_two, gain_two, keeper
    )
    d_bias_ffn = ffn_gate * jnp.sum(grad_two, axis=0)
    branch_low = (ffn_gate * grad_two).astype(jnp.bfloat16)
    branch_pieces = gather_rows(branch_low, shards)
    lowered = [
        lower_call(piece, up_weight, down_weight, r[1]) for piece, r in zip(branch_pieces, raised)
    ]
    d_up_bias = functools.reduce(jnp.add, [part[2][0] for part in lowered])
    grad_middle = grad_two + scatter_rows([part[1] for part in lowered], shards)
    grad_one, d_gain_one, d_shift_one = norm_backward(
        grad_middle, normed_one, inverse_one, gain_one, keeper
    )
    d_bias_attn = mha_gate * jnp.sum(grad_one, axis=0)
    attn_low = (mha_gate * grad_one).astype(jnp.bfloat16)
    attn_pieces = gather_rows(attn_low, shards)
    norm_local = jnp.concatenate(
        [
            jnp.stack([d_gain_one, d_shift_one, d_bias_attn, d_gain_two, d_shift_two, d_bias_ffn]),
            keep_row,
        ]
    )
    summed = butterfly(norm_local, "dp", owners)
    for bit in range(bit_count(shards)):
        summed = summed + swap(summed, 1 << bit, shards)
    norm_grads = summed[:6]
    keep_sums = summed[6, :2] * (1.0 / owners)
    ffn_a, ffn_b = inner_call(
        middle_pieces, [part[0] for part in lowered], [r[0] for r in raised], branch_pieces
    )
    d_qkv, head_sums = unwind_call(
        attn_pieces,
        queries,
        key_rows,
        value_rows,
        level,
        turned_col,
        turned_row,
        gate_row,
        out_weight,
    )
    d_units = jnp.concatenate([head_sums[0], head_sums[1], d_up_bias])
    fold_a = bits
    fold_b = bits[:1] + second_order(bits[1:])
    keep_a, send_a, keep_b, send_b = outer_call(
        fold_position(owner_of, slot_of, fold_a, slot_count, me),
        fold_position(owner_of, slot_of, fold_b, slot_count, me),
        token_pieces,
        attn_pieces,
        gated_ctx,
        d_qkv,
        ffn_a,
        ffn_b,
        owners * slot_count,
    )
    keep_a, got_a = fold(keep_a, send_a, fold_a, owners)
    keep_b, got_b = fold(keep_b, send_b, fold_b, owners)
    share = unit_params.shape[1]
    units = d_units.reshape(-1, 128)
    unit_grad = lax.dynamic_slice(
        butterfly(units, "dp", owners).reshape(-1), (me * share,), (share,)
    )
    token_part = jnp.einsum(
        "rc,dc->rd", d_qkv, qkv_weight, preferred_element_type=jnp.float32
    ).astype(jnp.bfloat16)
    token_part = [token_part[s * span : (s + 1) * span] for s in range(shards)]
    token_part, got_a, got_b, unit_grad = lax.optimization_barrier(
        (token_part, got_a, got_b, unit_grad)
    )
    token_far = [swap(token_part[s], s, shards) for s in range(1, shards)]
    count_now = step_count[0].astype(jnp.float32)

    def pair_view(x):
        x = x.reshape(slot_count, 2, FLAT, 128)
        return x.transpose(0, 2, 1, 3).reshape(slot_count, 2 * FLAT, 128)

    def pair_back(x):
        x = x.reshape(slot_count, FLAT, 2, 128).transpose(0, 2, 1, 3)
        return x.reshape(1, slot_count, 2, BLK * BLK)

    correction = (1.0 / (1.0 - beta_one**count_now)).reshape(1, 1)
    owned, masters_new, moment_one_new, moment_two_new, stats_new, turned = soap_call(
        correction,
        keep_a,
        got_a,
        keep_b,
        got_b,
        masters.reshape(flat_view),
        moment_one.reshape(flat_view),
        moment_two.reshape(flat_view),
        pair_view(block_bases),
        pair_view(block_stats),
    )
    bases_new = orth_call(turned)
    bases_new, token_far = lax.optimization_barrier((bases_new, token_far))
    token_grad = grad_one + token_part[0].astype(jnp.float32)
    for far in token_far:
        token_grad = token_grad + far.astype(jnp.float32)
    flat_shape = (1, slot_count, BLK * BLK)
    unit_first_new, unit_second_new, unit_scaled = adam_moments(
        unit_grad, unit_first[0], unit_second[0], count_now
    )
    norm_first_new, norm_second_new, norm_scaled = adam_moments(
        norm_grads, norm_first, norm_second, count_now
    )
    hidden_sum = jnp.sum(shared_keep[:D])
    param_count = 1e-06 * (
        shared_keep[D] * keep_sums[0] * (4 * HD) * hidden_sum
        + shared_keep[D + 1] * keep_sums[1] * 2 * hidden_sum
    )
    return (
        layer_out.astype(jnp.bfloat16),
        token_grad,
        owned.reshape(flat_shape),
        masters_new.reshape(flat_shape),
        moment_one_new.reshape(flat_shape),
        moment_two_new.reshape(flat_shape),
        pair_back(bases_new),
        pair_back(stats_new),
        (unit_params[0] - rate_vector * unit_scaled)[None],
        unit_first_new[None],
        unit_second_new[None],
        norm_grads,
        norm_params - rate_vector * norm_scaled,
        norm_first_new,
        norm_second_new,
        param_count.reshape(1),
    )


def solution(mesh):
    placed = (
        P(("dp", "tensor"), None),
        P(("dp", "tensor"), None),
        P("dp", None),
        P("tensor", None),
        P(),
        P("tensor", None),
        P(),
        P("tensor", "dp", None),
        P("tensor", "dp", None),
        P("tensor", "dp", None),
        P("tensor", "dp", None, None),
        P("tensor", "dp", None, None),
        P("tensor", "dp"),
        P("tensor", "dp"),
        P("tensor", "dp"),
        P(),
        P(),
        P(),
        P(),
        P(),
    )
    return jax.shard_map(
        body,
        mesh=mesh,
        in_specs=placed,
        out_specs=(
            P(("dp", "tensor"), None),
            P(("dp", "tensor"), None),
            P("tensor", "dp", None),
            P("tensor", "dp", None),
            P("tensor", "dp", None),
            P("tensor", "dp", None),
            P("tensor", "dp", None, None),
            P("tensor", "dp", None, None),
            P("tensor", "dp"),
            P("tensor", "dp"),
            P("tensor", "dp"),
            P(),
            P(),
            P(),
            P(),
            P(),
        ),
        check_vma=False,
    )
```

```python
import math
import functools
import jax
import jax.numpy as jnp
from jax import lax
from jax.sharding import PartitionSpec as P
from jax.experimental import pallas as pl
from jax.experimental.pallas import tpu as pltpu

BLK = 192
HALF = 96
QUART = 48
FLAT = 288
PAN = 64
beta_one = 0.95
beta_two = 0.95
beta_stat = 0.95
adam_eps = 1e-08
rate_matrix = 0.1
HIGH = lax.Precision.HIGH
EXACT = lax.Precision.HIGHEST


def mm(a, b, da, db, precision):
    return lax.dot_general(
        a, b, (((da,), (db,)), ((), ())), precision=precision, preferred_element_type=jnp.float32
    )


def read_square(src, lead, scratch, stride, first):
    def rows(q):
        return src[lead + (pl.ds(first + q * (stride // 3), HALF, stride=stride), slice(None))]

    a, b, c = rows(0), rows(1), rows(2)
    scratch[0, pl.ds(0, HALF, stride=2), :] = a
    scratch[1, pl.ds(0, HALF, stride=2), :] = b
    scratch[0, pl.ds(1, HALF, stride=2), :] = jnp.concatenate([b[:, 64:], c[:, :64]], axis=1)
    scratch[1, pl.ds(1, HALF, stride=2), :] = jnp.concatenate([c[:, 64:], c[:, 64:]], axis=1)
    return jnp.concatenate([scratch[0], scratch[1, :, :64]], axis=1)


def write_square(value, dst, lead, scratch, stride, first):
    scratch[0] = value[:, :128]
    scratch[1, :, :64] = value[:, 128:]
    e0 = scratch[0, pl.ds(0, HALF, stride=2), :]
    e1 = scratch[1, pl.ds(0, HALF, stride=2), :]
    o0 = scratch[0, pl.ds(1, HALF, stride=2), :]
    o1 = scratch[1, pl.ds(1, HALF, stride=2), :]
    step = stride // 3
    dst[lead + (pl.ds(first, HALF, stride=stride), slice(None))] = e0
    dst[lead + (pl.ds(first + step, HALF, stride=stride), slice(None))] = jnp.concatenate(
        [e1[:, :64], o0[:, :64]], axis=1
    )
    dst[lead + (pl.ds(first + 2 * step, HALF, stride=stride), slice(None))] = jnp.concatenate(
        [o0[:, 64:], o1[:, :64]], axis=1
    )


def soap_body(
    scale_ref, ka, ra, kb, rb, w_ref, m1_ref, m2_ref, b_ref, s_ref,
    g_out, w_out, m1_out, m2_out, s_out, mt_out, *scr,
):
    scratch = list(scr)
    ga = ka[0].astype(jnp.float32) + ra[0].astype(jnp.float32)
    gb = kb[0].astype(jnp.float32) + rb[0].astype(jnp.float32)
    g = jnp.concatenate([ga[:, :BLK], gb[:, :BLK], ga[:, BLK:], gb[:, BLK:]], axis=0)
    write_square(g, g_out, (0,), scratch[0], 3, 0)
    ql = read_square(b_ref, (0,), scratch[1], 6, 0)
    qr = read_square(b_ref, (0,), scratch[2], 6, 1)
    t3 = mm(g, qr, 1, 0, HIGH)
    r = mm(ql, t3, 0, 0, HIGH)
    rs, as_ = scratch[3], scratch[4]
    write_square(r, m1_out, (0,), rs, 3, 0)
    flat = m1_out[0]
    m1 = beta_one * m1_ref[0] + (1.0 - beta_one) * flat
    m2 = beta_two * m2_ref[0] + (1.0 - beta_two) * flat * flat
    m1_out[0] = m1
    m2_out[0] = m2
    corr = scale_ref[0, 0]
    w_out[0] = (m1 * corr) / (jnp.sqrt(m2 * corr) + adam_eps)
    a = read_square(w_out, (0,), as_, 3, 0)
    restored = mm(mm(ql, a, 1, 0, HIGH), qr, 1, 1, HIGH)
    write_square(restored, w_out, (0,), rs, 3, 0)
    w_out[0] = w_ref[0] - rate_matrix * w_out[0]
    sl = read_square(s_ref, (0,), scratch[5], 6, 0)
    sl = beta_stat * sl + (1.0 - beta_stat) * mm(g, g, 1, 1, HIGH)
    write_square(sl, s_out, (0,), scratch[6], 6, 0)
    mt_out[0, 0] = mm(ql, sl, 0, 0, EXACT)
    sr = read_square(s_ref, (0,), scratch[7], 6, 1)
    sr = beta_stat * sr + (1.0 - beta_stat) * mm(g, g, 0, 0, HIGH)
    write_square(sr, s_out, (0,), scratch[6], 6, 1)
    mt_out[0, 1] = mm(qr, sr, 0, 0, EXACT)


def soap_call(scale, ka, ra, kb, rb, w, m1, m2, b, s):
    n = w.shape[0]
    f32 = jnp.float32

    def spec(shape):
        zeros = (0,) * (len(shape) - 1)
        return pl.BlockSpec((1,) + shape[1:], lambda i: (i,) + zeros)

    ins = [ka, ra, kb, rb, w, m1, m2, b, s]
    outs = [
        jax.ShapeDtypeStruct((n, FLAT, 128), f32),
        jax.ShapeDtypeStruct((n, FLAT, 128), f32),
        jax.ShapeDtypeStruct((n, FLAT, 128), f32),
        jax.ShapeDtypeStruct((n, FLAT, 128), f32),
        jax.ShapeDtypeStruct((n, 2 * FLAT, 128), f32),
        jax.ShapeDtypeStruct((n, 2, BLK, BLK), f32),
    ]
    return pl.pallas_call(
        soap_body,
        grid=(n,),
        in_specs=[pl.BlockSpec(memory_space=pltpu.SMEM)] + [spec(x.shape) for x in ins],
        out_specs=[spec(o.shape) for o in outs],
        out_shape=outs,
        scratch_shapes=[pltpu.VMEM((2, BLK, 128), f32)] * 8,
        name="soap",
    )(scale, *ins)


def orth_body(mt_ref, q_out, xa, xs, sq):
    n = mt_ref.shape[0] * 2
    for i in range(n):
        m = mt_ref[i // 2, i % 2]
        xa[i, :, 256 : 256 + BLK] = m
        xa[i, :, 0:BLK] = mm(m, m, 1, 1, EXACT)
    lane = lax.broadcasted_iota(jnp.int32, (1, 1, 2 * PAN), 2)
    eye = (
        lax.broadcasted_iota(jnp.int32, (n, PAN, PAN), 1)
        == lax.broadcasted_iota(jnp.int32, (n, PAN, PAN), 2)
    ).astype(jnp.float32)

    def pick(v, j):
        return jnp.sum(jnp.where(lane == j, v, 0.0), axis=2, keepdims=True)

    for k in range(BLK // PAN):
        lo, hi = k * PAN, (k + 1) * PAN
        xs[...] = jnp.concatenate([xa[:, lo:hi, lo:hi], eye], axis=2)
        for first in range(0, PAN, 8):
            row_id = lax.broadcasted_iota(jnp.int32, (1, PAN - first, 1), 1) + first

            def step(s, carry):
                x = xs[:, first:, :]
                j = first + 2 * s
                r0 = xs[:, pl.ds(j, 1), :]
                r1 = xs[:, pl.ds(j + 1, 1), :]
                c0, c1 = pick(x, j), pick(x, j + 1)
                p, q, d = pick(r0, j), pick(r0, j + 1), pick(r1, j + 1)
                ip = 1.0 / p
                e = q * ip
                r1 = r1 - e * r0
                ip1 = 1.0 / (d - e * q)
                f0 = c0 * ip
                f1 = (c1 - f0 * q) * ip1
                f0 = jnp.where(row_id > j, f0, 0.0)
                f1 = jnp.where(row_id > j + 1, f1, 0.0)
                xs[:, first:, :] = x - (f0 * r0 + f1 * r1)
                return carry

            lax.fori_loop(0, 4, step, 0)
        x = xs[...]
        row_id = lax.broadcasted_iota(jnp.int32, (1, PAN, 1), 1)
        diag = jnp.sum(jnp.where(lane == row_id, x, 0.0), axis=2, keepdims=True)
        t = x[:, :, PAN:] * lax.rsqrt(diag)
        for i in range(n):
            w = mm(t[i], xa[i, lo:hi, :], 1, 0, EXACT)
            xa[i, lo:hi, :] = w
            if hi < BLK:
                wt = w[:, :256].T[hi:BLK]
                xa[i, hi:, :] = xa[i, hi:, :] - mm(wt, w, 1, 0, EXACT)
    for i in range(n):
        write_square(xa[i, :, 256:].T[:BLK], q_out, (i // 2,), sq, 6, i % 2)


def orth_call(mt):
    n = mt.shape[0]
    f32 = jnp.float32
    return pl.pallas_call(
        orth_body,
        out_shape=jax.ShapeDtypeStruct((n, 2 * FLAT, 128), f32),
        scratch_shapes=[
            pltpu.VMEM((2 * n, BLK, 512), f32),
            pltpu.VMEM((2 * n, PAN, 2 * PAN), f32),
            pltpu.VMEM((2, BLK, 128), f32),
        ],
        name="orth",
    )(mt)


D = 768
H = 12
FF = 3072
HD = 64
LEN = 1024
norm_eps = 1e-12
rate_vector = 0.25
query_scale = 0.125
stretch_shift = 2.0 / 3.0 * math.log(0.1 / 1.1)
root_half = 1.0 / math.sqrt(2.0)
normal_peak = 1.0 / math.sqrt(2.0 * math.pi)


def keep_prob(logits):
    return jax.nn.sigmoid(logits - stretch_shift)


def norm_forward(hidden, gain_row, shift_row, keeper):
    row_mean = jnp.mean(hidden, axis=-1, keepdims=True)
    centred = hidden - row_mean
    variance = jnp.mean(centred * centred, axis=-1, keepdims=True)
    inverse = lax.rsqrt(variance + norm_eps)
    normed = centred * inverse
    return (keeper * (normed * gain_row + shift_row), normed, inverse)


def norm_backward(incoming, normed, inverse, gain_row, keeper):
    scaled = incoming * keeper
    d_gain = jnp.sum(scaled * normed, axis=0)
    d_shift = jnp.sum(scaled, axis=0)
    d_normed = scaled * gain_row
    d_input = inverse * (
        d_normed
        - jnp.mean(d_normed, axis=-1, keepdims=True)
        - normed * jnp.mean(d_normed * normed, axis=-1, keepdims=True)
    )
    return (d_input, d_gain, d_shift)


def project_body(*refs):
    xs, (w, bias, q_out, k_out, v_out) = refs[:-5], refs[-5:]
    weight = w[...]
    for s, x in enumerate(xs):
        rows = slice(s * x.shape[0], (s + 1) * x.shape[0])
        out = dot(x[...], weight, 1, 0)
        cols = q_out.shape[1]
        q_out[rows] = ((out[:, :cols] + bias[0:1]) * query_scale).astype(jnp.bfloat16)
        k_out[rows] = out[:, cols : 2 * cols].astype(jnp.bfloat16)
        v_out[rows] = (out[:, 2 * cols :] + bias[1:2]).astype(jnp.bfloat16)


def project_call(pieces, weight, bias):
    rows = sum(p.shape[0] for p in pieces)
    out = jax.ShapeDtypeStruct((rows, bias.shape[1]), jnp.bfloat16)
    return pl.pallas_call(project_body, out_shape=[out] * 3, name="project")(
        *pieces, weight, bias
    )


def dot(a, b, da, db):
    return lax.dot_general(
        a, b, (((da,), (db,)), ((), ())), preferred_element_type=jnp.float32
    )


def partners(piece, shards):
    return [piece ^ s for s in range(shards) if s != 2]


def item_bias(seg_col, seg_row, piece, peers, span):
    mine = seg_row[0:1, piece * span : (piece + 1) * span]
    return [
        jnp.where(seg_col[c * span : (c + 1) * span, :] == mine, 0.0, -1e30) for c in peers
    ]


def attend_body(q, k, v, seg_col, seg_row, gate_col, w, *outs, pieces, shards):
    span = q.shape[0] // shards
    cg_out, lse_out = outs[0], outs[1]
    heads = q.shape[1] // HD
    weight = w[...]
    lse_out[...] = jnp.zeros_like(lse_out)
    for at, p in enumerate(pieces):
        peers = partners(p, shards)
        bias = item_bias(seg_col, seg_row, p, peers, span)
        rows = slice(p * span, (p + 1) * span)
        mine = slice(at * span, (at + 1) * span)
        parts = []
        for h in range(heads):
            cut = slice(h * HD, (h + 1) * HD)
            qp = q[rows, cut]
            scores = [
                dot(k[c * span : (c + 1) * span, cut], qp, 1, 1) + b for c, b in zip(peers, bias)
            ]
            top = functools.reduce(jnp.maximum, [jnp.max(s, axis=0, keepdims=True) for s in scores])
            powers = [jnp.exp(s - top) for s in scores]
            total = functools.reduce(
                jnp.add, [jnp.sum(e, axis=0, keepdims=True) for e in powers]
            )
            inverse = 1.0 / total
            context = functools.reduce(
                jnp.add,
                [
                    dot(
                        v[c * span : (c + 1) * span, cut],
                        (e * inverse).astype(jnp.bfloat16),
                        0,
                        0,
                    )
                    for c, e in zip(peers, powers)
                ],
            )
            parts.append(context)
            lse_out[h : h + 1, mine] = top + jnp.log(total)
        gated = (jnp.concatenate(parts, axis=0) * gate_col[...]).T.astype(jnp.bfloat16)
        cg_out[mine] = gated
        outs[2 + at][...] = dot(gated, weight, 1, 0).astype(jnp.bfloat16)


def attend_call(q, k, v, seg_col, seg_row, gate_col, weight, pieces, shards):
    span = q.shape[0] // shards
    bf16 = jnp.bfloat16
    count = len(pieces)
    outs = [
        jax.ShapeDtypeStruct((count * span, q.shape[1]), bf16),
        jax.ShapeDtypeStruct((8, count * span), jnp.float32),
    ] + [jax.ShapeDtypeStruct((span, weight.shape[1]), bf16)] * count
    return pl.pallas_call(
        functools.partial(attend_body, pieces=pieces, shards=shards), out_shape=outs, name="attend"
    )(q, k, v, seg_col, seg_row, gate_col, weight)


def unwind_body(*refs, shards):
    eas = refs[:shards]
    q, k, v, lse, seg_col, seg_row, gate_row, w, g_out, sum_out, dk_acc, dv_acc = refs[shards:]
    span = q.shape[0] // shards
    cols = q.shape[1]
    heads = cols // HD
    weight = w[...]
    dk_acc[...] = jnp.zeros_like(dk_acc)
    dv_acc[...] = jnp.zeros_like(dv_acc)
    dq_sum = jnp.zeros((1, cols), jnp.float32)
    for p in range(shards):
        peers = partners(p, shards)
        bias = item_bias(seg_col, seg_row, p, peers, span)
        rows = slice(p * span, (p + 1) * span)
        d_ctx = (dot(eas[p][...], weight, 1, 1) * gate_row[...]).astype(jnp.bfloat16)
        parts = []
        for h in range(heads):
            cut = slice(h * HD, (h + 1) * HD)
            qp = q[rows, cut]
            do = d_ctx[:, cut]
            level = lse[h : h + 1, rows]
            probs, slopes = [], []
            for c, b in zip(peers, bias):
                ks = slice(c * span, (c + 1) * span)
                prob = jnp.exp(dot(k[ks, cut], qp, 1, 1) + (b - level))
                dv_acc[h, ks] = dv_acc[h, ks] + dot(prob.astype(jnp.bfloat16), do, 1, 0)
                probs.append(prob)
                slopes.append(dot(v[ks, cut], do, 1, 1))
            inner = functools.reduce(
                jnp.add, [jnp.sum(a * b, axis=0, keepdims=True) for a, b in zip(probs, slopes)]
            )
            dq = jnp.zeros((HD, span), jnp.float32)
            for c, a, b in zip(peers, probs, slopes):
                ks = slice(c * span, (c + 1) * span)
                ds = (a * (b - inner)).astype(jnp.bfloat16)
                dk_acc[h, ks] = dk_acc[h, ks] + dot(ds, qp, 1, 0)
                dq = dq + dot(k[ks, cut], ds, 0, 0)
            parts.append(dq)
        dq_all = jnp.concatenate(parts, axis=0).T.astype(jnp.bfloat16) * query_scale
        dq_all = dq_all.astype(jnp.bfloat16)
        g_out[rows, :cols] = dq_all
        dq_sum = dq_sum + jnp.sum(dq_all.astype(jnp.float32), axis=0, keepdims=True)
    dk = jnp.concatenate([dk_acc[h] for h in range(heads)], axis=1).astype(jnp.bfloat16)
    dv = jnp.concatenate([dv_acc[h] for h in range(heads)], axis=1).astype(jnp.bfloat16)
    g_out[:, cols:] = jnp.concatenate([dk, dv], axis=1)
    sum_out[0:1] = dq_sum
    sum_out[1:2] = jnp.sum(dv.astype(jnp.float32), axis=0, keepdims=True)


def unwind_call(eas, q, k, v, lse, seg_col, seg_row, gate_row, weight):
    rows, cols = q.shape
    return pl.pallas_call(
        functools.partial(unwind_body, shards=len(eas)),
        out_shape=[
            jax.ShapeDtypeStruct((rows, 3 * cols), jnp.bfloat16),
            jax.ShapeDtypeStruct((2, cols), jnp.float32),
        ],
        scratch_shapes=[
            pltpu.VMEM((cols // HD, rows, HD), jnp.float32),
            pltpu.VMEM((cols // HD, rows, HD), jnp.float32),
        ],
        name="unwind",
    )(*eas, q, k, v, lse, seg_col, seg_row, gate_row, weight)


def raise_body(m, w1, w2, bias, gate, h_out, slope_out, p_out):
    u = dot(m[...], w1[...], 1, 0) + bias[...]
    half = 0.5 * (1.0 + lax.erf(u * root_half))
    low = (u * half * gate[...]).astype(jnp.bfloat16)
    h_out[...] = low
    slope = half + u * jnp.exp(-0.5 * u * u) * normal_peak
    slope_out[...] = slope * gate[...]
    p_out[...] = dot(low, w2[...], 1, 0).astype(jnp.bfloat16)


def raise_call(piece, w1, w2, bias, gate):
    rows, units = piece.shape[0], w1.shape[1]
    return pl.pallas_call(
        raise_body,
        out_shape=[
            jax.ShapeDtypeStruct((rows, units), jnp.bfloat16),
            jax.ShapeDtypeStruct((rows, units), jnp.float32),
            jax.ShapeDtypeStruct(piece.shape, jnp.bfloat16),
        ],
        name="raise",
    )(piece, w1, w2, bias, gate)


def lower_body(e, w1, w2, slope, d_out, p_out, s_out):
    du = (dot(e[...], w2[...], 1, 1) * slope[...]).astype(jnp.bfloat16)
    d_out[...] = du
    p_out[...] = dot(du, w1[...], 1, 1).astype(jnp.bfloat16)
    s_out[...] = jnp.sum(du.astype(jnp.float32), axis=0, keepdims=True)


def lower_call(piece, w1, w2, slope):
    rows, units = slope.shape
    return pl.pallas_call(
        lower_body,
        out_shape=[
            jax.ShapeDtypeStruct((rows, units), jnp.bfloat16),
            jax.ShapeDtypeStruct(piece.shape, jnp.bfloat16),
            jax.ShapeDtypeStruct((1, units), jnp.float32),
        ],
        name="lower",
    )(piece, w1, w2, slope)


def pack_row(grad, put, block):
    for i in range(grad.shape[0] // BLK):
        for side in range(2):
            at = i * BLK + side * QUART
            top = grad[at : at + QUART, :].astype(jnp.bfloat16)
            low = grad[at + HALF : at + HALF + QUART, :].astype(jnp.bfloat16)
            for j in range(grad.shape[1] // BLK):
                cut = slice(j * BLK, (j + 1) * BLK)
                put(
                    side,
                    block + i * (grad.shape[1] // BLK) + j,
                    jnp.concatenate([top[:, cut], low[:, cut]], axis=1),
                )


def inner_body(*refs, shards):
    groups = [refs[i * shards : (i + 1) * shards] for i in range(4)]
    outs = refs[4 * shards :]

    def put(side, block, value):
        outs[side][block] = value

    block = 0
    for left, right in ((groups[0], groups[1]), (groups[2], groups[3])):
        grad = functools.reduce(
            jnp.add, [dot(a[...], b[...], 0, 0) for a, b in zip(left, right)]
        )
        pack_row(grad, put, block)
        block += grad.shape[0] * grad.shape[1] // (BLK * BLK)


def inner_call(mids, d_raised, hidden, branch):
    shards = len(mids)
    blocks = 2 * mids[0].shape[1] * hidden[0].shape[1] // (BLK * BLK)
    out = jax.ShapeDtypeStruct((blocks, QUART, 2 * BLK), jnp.bfloat16)
    return pl.pallas_call(
        functools.partial(inner_body, shards=shards), out_shape=[out, out], name="inner"
    )(*mids, *d_raised, *hidden, *branch)


def outer_body(pos_a, pos_b, *refs, shards, blocks):
    xs, eas = refs[:shards], refs[shards : 2 * shards]
    cg, g, ffn_a, ffn_b = refs[2 * shards : 2 * shards + 4]
    outs = refs[2 * shards + 4 : 2 * shards + 8]
    bufs, sems = refs[2 * shards + 8 : 2 * shards + 10], refs[2 * shards + 10]
    poses = (pos_a, pos_b)
    span = xs[0].shape[0]
    total = bufs[0].shape[0]
    if total > blocks:
        for buf in bufs:
            buf[...] = jnp.zeros_like(buf)

    def put(side, block, value):
        bufs[side][poses[side][block]] = value

    first = blocks - ffn_a.shape[0]
    for side, src in enumerate((ffn_a, ffn_b)):
        for b in range(ffn_a.shape[0]):
            put(side, first + b, src[b])
    cut = [slice(s * span, (s + 1) * span) for s in range(shards)]
    grad = functools.reduce(jnp.add, [dot(x[...], g[c], 0, 0) for x, c in zip(xs, cut)])
    pack_row(grad, put, 0)
    block = grad.shape[0] * grad.shape[1] // (BLK * BLK)
    grad = functools.reduce(jnp.add, [dot(cg[c], e[...], 0, 0) for e, c in zip(eas, cut)])
    pack_row(grad, put, block)
    half = total // 2
    copies = []
    for side in range(2):
        for part in (1, 0):
            copy = pltpu.make_async_copy(
                bufs[side].at[pl.ds(part * half, half)], outs[2 * side + part], sems.at[side, part]
            )
            copy.start()
            copies.append(copy)
    for copy in copies:
        copy.wait()


def outer_call(pos_a, pos_b, xs, eas, cg, g, ffn_a, ffn_b, total):
    shards = len(xs)
    blocks = (xs[0].shape[1] * g.shape[1] + cg.shape[1] * eas[0].shape[1]) // (BLK * BLK)
    blocks += ffn_a.shape[0]
    part = jax.ShapeDtypeStruct((total // 2, QUART, 2 * BLK), jnp.bfloat16)
    buf = pltpu.VMEM((total, QUART, 2 * BLK), jnp.bfloat16)
    return pl.pallas_call(
        functools.partial(outer_body, shards=shards, blocks=blocks),
        in_specs=[pl.BlockSpec(memory_space=pltpu.SMEM)] * 2
        + [pl.BlockSpec(memory_space=pltpu.VMEM)] * (2 * shards + 4),
        out_specs=[pl.BlockSpec(memory_space=pl.ANY)] * 4,
        out_shape=[part] * 4,
        scratch_shapes=[buf, buf, pltpu.SemaphoreType.DMA((2, 2))],
        name="outer",
    )(pos_a, pos_b, *xs, *eas, cg, g, ffn_a, ffn_b)


def adam_moments(gradient, first_moment, second_moment, count_now):
    first_moment = beta_one * first_moment + (1.0 - beta_one) * gradient
    second_moment = beta_two * second_moment + (1.0 - beta_two) * gradient * gradient
    scaled = (
        first_moment
        / (1.0 - beta_one**count_now)
        / (jnp.sqrt(second_moment / (1.0 - beta_two**count_now)) + adam_eps)
    )
    return (first_moment, second_moment, scaled)


def bit_pairs(bit, size):
    return [(i, i ^ (1 << bit)) for i in range(size)]


def bit_count(size):
    return size.bit_length() - 1


def second_order(bits):
    return ([bits[1], bits[0]] + bits[2:]) if len(bits) > 1 else bits


def cast_body(w_ref, a_out, b_out, scratch):
    m = read_square(w_ref, (0,), scratch, 3, 0)
    packed = jnp.concatenate([m[:HALF], m[HALF:]], axis=1).astype(jnp.bfloat16)
    a_out[0] = packed[:QUART]
    b_out[0] = packed[QUART:]


def cast_call(flat):
    n = flat.shape[0]
    piece = jax.ShapeDtypeStruct((n, QUART, 2 * BLK), jnp.bfloat16)
    spec = pl.BlockSpec((1, QUART, 2 * BLK), lambda i: (i, 0, 0))
    return pl.pallas_call(
        cast_body,
        grid=(n,),
        in_specs=[pl.BlockSpec((1, FLAT, 128), lambda i: (i, 0, 0))],
        out_specs=[spec, spec],
        out_shape=[piece, piece],
        scratch_shapes=[pltpu.VMEM((2, BLK, 128), jnp.float32)],
        name="cast",
    )(flat)


def spread(block, order, size):
    pieces = [block[None]]
    rel = [[0]]
    for bit in order:
        moved = [lax.ppermute(p, "dp", bit_pairs(bit, size)) for p in pieces]
        rel = rel + [[r ^ (1 << bit) for r in group] for group in rel]
        pieces = pieces + moved
        if size > 8:
            pieces = [jnp.concatenate(pieces)]
            rel = [sum(rel, [])]
    return pieces, sum(rel, [])


def build_body(pos_a, pos_b, *refs, count):
    ins_a, ins_b = refs[:count], refs[count : 2 * count]
    outs = refs[2 * count : 2 * count + 4]
    buf_a, buf_b, sems = refs[2 * count + 4 :]
    copies = []
    for side, (ins, buf) in enumerate(((ins_a, buf_a), (ins_b, buf_b))):
        at = 0
        for i, src in enumerate(ins):
            m = src.shape[0]
            copy = pltpu.make_async_copy(src, buf.at[pl.ds(at, m)], sems.at[side, i])
            copy.start()
            copies.append(copy)
            at += m
    for copy in copies:
        copy.wait()
    base = 0
    for out in outs:
        rows, cols = out.shape[0] // BLK, out.shape[1] // BLK
        for i in range(rows):
            for side, (buf, pos) in enumerate(((buf_a, pos_a), (buf_b, pos_b))):
                got = [buf[pos[base + i * cols + j]] for j in range(cols)]
                at = i * BLK + side * QUART
                out[at : at + QUART, :] = jnp.concatenate([g[:, :BLK] for g in got], axis=1)
                at += HALF
                out[at : at + QUART, :] = jnp.concatenate([g[:, BLK:] for g in got], axis=1)
        base += rows * cols


def build_call(pos_a, pos_b, pieces_a, pieces_b, shapes):
    flat_a = [p.reshape(-1, QUART, 2 * BLK) for p in pieces_a]
    flat_b = [p.reshape(-1, QUART, 2 * BLK) for p in pieces_b]
    count = len(flat_a)
    total = sum(p.shape[0] for p in flat_a)
    bf16 = jnp.bfloat16
    kernel = functools.partial(build_body, count=count)
    return pl.pallas_call(
        kernel,
        in_specs=[pl.BlockSpec(memory_space=pltpu.SMEM)] * 2
        + [pl.BlockSpec(memory_space=pl.ANY)] * (2 * count),
        out_shape=[jax.ShapeDtypeStruct(s, bf16) for s in shapes],
        scratch_shapes=[
            pltpu.VMEM((total, QUART, 2 * BLK), bf16),
            pltpu.VMEM((total, QUART, 2 * BLK), bf16),
            pltpu.SemaphoreType.DMA((2, count)),
        ],
        name="build",
    )(pos_a, pos_b, *flat_a, *flat_b)


def fold(keep, send, order, size):
    for step, bit in enumerate(order):
        got = lax.ppermute(send, "dp", bit_pairs(bit, size))
        if step == len(order) - 1:
            return keep, got
        half = keep.shape[0] // 2
        cur = (keep.astype(jnp.float32) + got.astype(jnp.float32)).astype(jnp.bfloat16)
        keep, send = cur[:half], cur[half:]


def fold_position(owner, slot, order, slots, me):
    rel = owner ^ me
    index = jnp.zeros_like(rel)
    for bit in order:
        index = index * 2 + ((rel >> bit) & 1)
    return index * slots + slot


def butterfly(value, axis, size):
    for bit in range(bit_count(size)):
        value = value + lax.ppermute(value, axis, bit_pairs(bit, size))
    return value


def swap(piece, s, shards):
    return lax.ppermute(piece, "tensor", [(i, i ^ s) for i in range(shards)])


def shift(piece, pairs):
    return lax.ppermute(piece, "tensor", pairs)


def gather_rows(rows, shards, relayed=True):
    if not relayed or shards != 4:
        far = {s: swap(rows, s, shards) for s in reversed(range(1, shards))}
        return [rows] + [far[s] for s in range(1, shards)]
    two = swap(rows, 2, shards)
    one = swap(rows, 1, shards)
    relay = shift(two, [(2, 3), (1, 0)])
    inner = shift(rows, [(1, 2), (2, 1)])
    return [rows, one, two, inner + relay]


def scatter_rows(pieces, shards, relayed=False):
    if relayed and shards == 4:
        relay = shift(pieces[3], [(0, 1), (3, 2)])
        far = (pieces[2].astype(jnp.float32) + relay.astype(jnp.float32)).astype(jnp.bfloat16)
        others = [
            swap(far, 2, shards),
            swap(pieces[1], 1, shards),
            shift(pieces[3], [(1, 2), (2, 1)]),
        ]
    else:
        others = [swap(pieces[s], s, shards) for s in range(1, shards)]
    total = pieces[0].astype(jnp.float32)
    for piece in others:
        total = total + piece.astype(jnp.float32)
    return total


def body(
    tokens,
    cotangent,
    segments,
    gates_local,
    gates_shared,
    gate_logits,
    shared_logits,
    masters,
    moment_one,
    moment_two,
    block_bases,
    block_stats,
    unit_params,
    unit_first,
    unit_second,
    norm_params,
    norm_first,
    norm_second,
    slot_ids,
    step_count,
):
    shards = lax.axis_size("tensor")
    owners = lax.axis_size("dp")
    head_count = H // shards
    head_cols = head_count * HD
    unit_count = FF // shards
    slot_count = masters.shape[1]
    me = lax.axis_index("dp")
    place = lax.axis_index("tensor")
    bits = list(range(bit_count(owners)))
    head_keep = keep_prob(gate_logits[0, :head_count])
    unit_keep = keep_prob(gate_logits[0, head_count:])
    shared_keep = keep_prob(shared_logits)
    lanes = lax.broadcasted_iota(jnp.int32, (1, D), 1)
    keep_row = jnp.where(
        lanes == 0, jnp.sum(head_keep), jnp.where(lanes == 1, jnp.sum(unit_keep), 0.0)
    )
    flat_view = (slot_count, FLAT, 128)
    cast_a, cast_b = cast_call(masters.reshape(flat_view))
    order_a = bits[1:] + bits[:1]
    order_b = second_order(bits[1:]) + bits[:1]

    pieces_a, rel_a = spread(cast_a, order_a, owners)
    pieces_b, rel_b = spread(cast_b, order_b, owners)
    owner_of = slot_ids // slot_count
    slot_of = slot_ids % slot_count
    rel_of = owner_of ^ me

    def piece_spot(rel_list):
        table = [0] * owners
        for spot, rel in enumerate(rel_list):
            table[rel] = spot
        return jnp.asarray(table, jnp.int32)[rel_of] * slot_count + slot_of

    qkv_weight, out_weight, up_weight, down_weight = build_call(
        piece_spot(rel_a),
        piece_spot(rel_b),
        pieces_a,
        pieces_b,
        ((D, 3 * head_cols), (head_cols, D), (D, unit_count), (unit_count, D)),
    )
    unit_low = unit_params.astype(jnp.bfloat16)
    unit_pieces, _ = spread(unit_low[0], bits, owners)
    unit_all = jnp.concatenate(unit_pieces, axis=0)
    unit_bias = unit_all[jnp.arange(owners) ^ me].reshape(-1).astype(jnp.float32)
    head_gate = gates_local[0, :head_count]
    unit_gate = gates_local[0, head_count:]
    keeper = gates_shared[:D]
    mha_gate = gates_shared[D]
    ffn_gate = gates_shared[D + 1]
    gain_one = norm_params[0]
    shift_one = norm_params[1]
    bias_attn = norm_params[2]
    gain_two = norm_params[3]
    shift_two = norm_params[4]
    bias_ffn = norm_params[5]
    token_pieces = gather_rows(tokens, shards, False)
    span = LEN // shards
    parts = segments.reshape(shards, span)
    turned_row = parts[jnp.arange(shards) ^ place].reshape(1, LEN)
    turned_col = turned_row.reshape(LEN, 1)
    queries, key_rows, value_rows = project_call(
        token_pieces, qkv_weight, unit_bias[: 2 * head_cols].reshape(2, head_cols)
    )
    gate_row = jnp.repeat(head_gate, HD).reshape(1, head_cols)
    attend = functools.partial(
        attend_call,
        queries,
        key_rows,
        value_rows,
        turned_col,
        turned_row,
        gate_row.reshape(head_cols, 1),
        out_weight,
    )
    last_ctx, last_level, last_part = attend((shards - 1,), shards)
    gated_ctx, level, *partial = attend(tuple(range(shards - 1)), shards)
    partial = partial + [last_part]
    gated_ctx = jnp.concatenate([gated_ctx, last_ctx], axis=0)
    level = jnp.concatenate([level, last_level], axis=1)
    attn_sum = scatter_rows(partial, shards, True)
    residual = tokens.astype(jnp.float32)
    hidden_one = residual + mha_gate * (attn_sum + bias_attn)
    middle, normed_one, inverse_one = norm_forward(hidden_one, gain_one, shift_one, keeper)
    middle_pieces = gather_rows(middle.astype(jnp.bfloat16), shards)
    up_bias = unit_bias[2 * head_cols :].reshape(1, unit_count)
    gate_units = unit_gate.reshape(1, unit_count)
    raised = [
        raise_call(piece, up_weight, down_weight, up_bias, gate_units) for piece in middle_pieces
    ]
    ffn_sum = scatter_rows([r[2] for r in raised], shards)
    hidden_two = middle + ffn_gate * (ffn_sum + bias_ffn)
    layer_out, normed_two, inverse_two = norm_forward(hidden_two, gain_two, shift_two, keeper)
    upstream = cotangent.astype(jnp.float32)
    grad_two, d_gain_two, d_shift_two = norm_backward(
        upstream, normed_two, inverse_two, gain_two, keeper
    )
    d_bias_ffn = ffn_gate * jnp.sum(grad_two, axis=0)
    branch_low = (ffn_gate * grad_two).astype(jnp.bfloat16)
    branch_pieces = gather_rows(branch_low, shards)
    lowered = [
        lower_call(piece, up_weight, down_weight, r[1]) for piece, r in zip(branch_pieces, raised)
    ]
    d_up_bias = functools.reduce(jnp.add, [part[2][0] for part in lowered])
    grad_middle = grad_two + scatter_rows([part[1] for part in lowered], shards)
    grad_one, d_gain_one, d_shift_one = norm_backward(
        grad_middle, normed_one, inverse_one, gain_one, keeper
    )
    d_bias_attn = mha_gate * jnp.sum(grad_one, axis=0)
    attn_low = (mha_gate * grad_one).astype(jnp.bfloat16)
    attn_pieces = gather_rows(attn_low, shards)
    norm_local = jnp.concatenate(
        [
            jnp.stack([d_gain_one, d_shift_one, d_bias_attn, d_gain_two, d_shift_two, d_bias_ffn]),
            keep_row,
        ]
    )
    summed = butterfly(norm_local, "dp", owners)
    for bit in range(bit_count(shards)):
        summed = summed + swap(summed, 1 << bit, shards)
    norm_grads = summed[:6]
    keep_sums = summed[6, :2] * (1.0 / owners)
    ffn_a, ffn_b = inner_call(
        middle_pieces, [part[0] for part in lowered], [r[0] for r in raised], branch_pieces
    )
    d_qkv, head_sums = unwind_call(
        attn_pieces,
        queries,
        key_rows,
        value_rows,
        level,
        turned_col,
        turned_row,
        gate_row,
        out_weight,
    )
    d_units = jnp.concatenate([head_sums[0], head_sums[1], d_up_bias])
    fold_a = bits
    fold_b = bits[:1] + second_order(bits[1:])
    keep_a, send_a, keep_b, send_b = outer_call(
        fold_position(owner_of, slot_of, fold_a, slot_count, me),
        fold_position(owner_of, slot_of, fold_b, slot_count, me),
        token_pieces,
        attn_pieces,
        gated_ctx,
        d_qkv,
        ffn_a,
        ffn_b,
        owners * slot_count,
    )
    keep_a, got_a = fold(keep_a, send_a, fold_a, owners)
    keep_b, got_b = fold(keep_b, send_b, fold_b, owners)
    share = unit_params.shape[1]
    units = d_units.reshape(-1, 128)
    unit_grad = lax.dynamic_slice(
        butterfly(units, "dp", owners).reshape(-1), (me * share,), (share,)
    )
    token_part = jnp.einsum(
        "rc,dc->rd", d_qkv, qkv_weight, preferred_element_type=jnp.float32
    ).astype(jnp.bfloat16)
    token_part = [token_part[s * span : (s + 1) * span] for s in range(shards)]
    token_part, got_a, got_b, unit_grad = lax.optimization_barrier(
        (token_part, got_a, got_b, unit_grad)
    )
    token_far = [swap(token_part[s], s, shards) for s in range(1, shards)]
    count_now = step_count[0].astype(jnp.float32)

    def pair_view(x):
        x = x.reshape(slot_count, 2, FLAT, 128)
        return x.transpose(0, 2, 1, 3).reshape(slot_count, 2 * FLAT, 128)

    def pair_back(x):
        x = x.reshape(slot_count, FLAT, 2, 128).transpose(0, 2, 1, 3)
        return x.reshape(1, slot_count, 2, BLK * BLK)

    correction = (1.0 / (1.0 - beta_one**count_now)).reshape(1, 1)
    owned, masters_new, moment_one_new, moment_two_new, stats_new, turned = soap_call(
        correction,
        keep_a,
        got_a,
        keep_b,
        got_b,
        masters.reshape(flat_view),
        moment_one.reshape(flat_view),
        moment_two.reshape(flat_view),
        pair_view(block_bases),
        pair_view(block_stats),
    )
    bases_new = orth_call(turned)
    bases_new, token_far = lax.optimization_barrier((bases_new, token_far))
    token_grad = grad_one + token_part[0].astype(jnp.float32)
    for far in token_far:
        token_grad = token_grad + far.astype(jnp.float32)
    flat_shape = (1, slot_count, BLK * BLK)
    unit_first_new, unit_second_new, unit_scaled = adam_moments(
        unit_grad, unit_first[0], unit_second[0], count_now
    )
    norm_first_new, norm_second_new, norm_scaled = adam_moments(
        norm_grads, norm_first, norm_second, count_now
    )
    hidden_sum = jnp.sum(shared_keep[:D])
    param_count = 1e-06 * (
        shared_keep[D] * keep_sums[0] * (4 * HD) * hidden_sum
        + shared_keep[D + 1] * keep_sums[1] * 2 * hidden_sum
    )
    return (
        layer_out.astype(jnp.bfloat16),
        token_grad,
        owned.reshape(flat_shape),
        masters_new.reshape(flat_shape),
        moment_one_new.reshape(flat_shape),
        moment_two_new.reshape(flat_shape),
        pair_back(bases_new),
        pair_back(stats_new),
        (unit_params[0] - rate_vector * unit_scaled)[None],
        unit_first_new[None],
        unit_second_new[None],
        norm_grads,
        norm_params - rate_vector * norm_scaled,
        norm_first_new,
        norm_second_new,
        param_count.reshape(1),
    )


def solution(mesh):
    placed = (
        P(("dp", "tensor"), None),
        P(("dp", "tensor"), None),
        P("dp", None),
        P("tensor", None),
        P(),
        P("tensor", None),
        P(),
        P("tensor", "dp", None),
        P("tensor", "dp", None),
        P("tensor", "dp", None),
        P("tensor", "dp", None, None),
        P("tensor", "dp", None, None),
        P("tensor", "dp"),
        P("tensor", "dp"),
        P("tensor", "dp"),
        P(),
        P(),
        P(),
        P(),
        P(),
    )
    return jax.shard_map(
        body,
        mesh=mesh,
        in_specs=placed,
        out_specs=(
            P(("dp", "tensor"), None),
            P(("dp", "tensor"), None),
            P("tensor", "dp", None),
            P("tensor", "dp", None),
            P("tensor", "dp", None),
            P("tensor", "dp", None),
            P("tensor", "dp", None, None),
            P("tensor", "dp", None, None),
            P("tensor", "dp"),
            P("tensor", "dp"),
            P("tensor", "dp"),
            P(),
            P(),
            P(),
            P(),
            P(),
        ),
        check_vma=False,
    )
```
